128 devices in a mesh: slab: 4 (over y_hi, core), orb: 8 (over x, y_lo), pois: 4 (over z).
Axes of the slice: x: 4, y: 4 (y_hi: 2, y_lo: 2; y = y_hi * 2 + y_lo), z: 4, core: 2. Of those that a mesh axis runs over, the one named last changes fastest.
Arguments:
- orbitals: bfloat16 [32, 2, 192, 128, 128], P('orb', None, 'slab', 'pois'), may hold values from -8 to 8
- occupations: float32 [32], P('orb'), may hold values from 5e-05 to 0.0005
- ext_pot: float32 [192, 128, 128], P('slab', 'pois'), may hold values from -1 to 1
- hartree_old: float32 [192, 128, 128], P('slab', 'pois'), may hold values from 0 to 2
Outputs:
- orbitals_new: float32 [32, 2, 192, 128, 128], P('orb', None, 'slab', 'pois')
- hartree_new: float32 [192, 128, 128], P('slab', 'pois', 'orb')
The draws below stay inside these ranges and needn't reach their ends.
All inputs are finite; a program needn't handle non-finite values.
Results may differ from the reference program's by a relative error of at most 0.0003.
Values may be sent and summed in bfloat16 or wider, within the bound.
No kernel may reach another device: no remote copies, remote signals or barrier semaphores. Data moves between devices by JAX's collectives and lax.ppermute only.
A program may use at most 64 MiB of HBM per device.

```python
import math
import jax
import jax.numpy as jnp
from jax import lax

NX = 192
NY = 128
NZ = 128
NORB = 32


def draw_orbitals(key, part):
    key_envelope = jax.random.fold_in(key, 11)
    key_values = jax.random.fold_in(key, 12)
    env_lowest = 0.5
    env_highest = 2.0
    raw_values = jnp.clip(jax.random.normal(key_values, (NORB, 2, NX, NY, NZ), jnp.float32), -4.0, 4.0)
    envelope = jnp.exp(jax.random.uniform(key_envelope, (NX, NY, NZ), jnp.float32, math.log(env_lowest), math.log(env_highest)))
    return jnp.clip(raw_values * envelope, -8.0, 8.0).astype(jnp.bfloat16)


def steps_of(key, dims, split, least, largest):
    def one(position, blocks):
        draws = jax.random.uniform(jax.random.fold_in(jax.random.fold_in(key, 6), position), (blocks,), jnp.float32, least / len(split), largest / len(split))
        return jnp.repeat(jnp.exp(draws), dims[position] // blocks).reshape((-1,) + (1,) * (len(dims) - position - 1))

    loudness = one(*split[0])
    for cut in split[1:]:
        loudness = loudness * one(*cut)
    return loudness


def setup_inputs(seed: int = 0) -> dict:
    key_of = jax.random.split(jax.random.key(seed), 5)
    orbitals = draw_orbitals(jax.random.fold_in(key_of[4], 71), 0)
    occupations = jnp.clip(jnp.exp(math.log(0.0005) - 2.3025852 * jax.random.uniform(key_of[1], (NORB,), jnp.float32) ** steps_of(key_of[1], (NORB,), ((0, 8),), -0.2, 0.2)), 4.999999873689376e-05, 0.0005)
    ext_pot = jnp.clip(jax.random.uniform(key_of[2], (NX, NY, NZ), jnp.float32, -1.0, 1.0) * steps_of(key_of[2], (NX, NY, NZ), ((0, 4), (1, 4)), -0.4, 0.0), -1.0, 1.0)
    hartree_old = jnp.clip(2.0 * jax.random.uniform(key_of[3], (NX, NY, NZ), jnp.float32) ** steps_of(key_of[3], (NX, NY, NZ), ((0, 4), (1, 4)), -0.2, 0.2), 0.0, 2.0)
    return dict(orbitals=orbitals, occupations=occupations, ext_pot=ext_pot, hartree_old=hartree_old)


time_step = 0.3


def sine_table(row_start, row_count, col_start, col_count, length):
    row_index = row_start + lax.iota(jnp.int32, row_count) + 1
    col_index = col_start + lax.iota(jnp.int32, col_count) + 1
    product = (row_index[:, None] * col_index[None, :]) % (2 * (length + 1))
    return jnp.sin(jnp.pi * product.astype(jnp.float32) / (length + 1))


def eigen_values(first_mode, mode_count, length):
    mode_index = first_mode + lax.iota(jnp.int32, mode_count) + 1
    return 2.0 - 2.0 * jnp.cos(jnp.pi * mode_index.astype(jnp.float32) / (length + 1))


def apply_ham(values, potential):
    padded = jnp.pad(values, ((0, 0), (1, 1), (1, 1), (1, 1)))
    beside_all = padded[:, 2:, 1:-1, 1:-1] + padded[:, :-2, 1:-1, 1:-1]
    beside_all = beside_all + padded[:, 1:-1, 2:, 1:-1] + padded[:, 1:-1, :-2, 1:-1]
    beside_all = beside_all + padded[:, 1:-1, 1:-1, 2:] + padded[:, 1:-1, 1:-1, :-2]
    return (3.0 + potential) * values - 0.5 * beside_all


def taylor(values, potential):
    image_one = apply_ham(values, potential)
    image_two = apply_ham(image_one, potential)
    rotated = jnp.stack([image_one[1], -image_one[0]])
    return values + time_step * rotated - (0.5 * time_step * time_step) * image_two


def poisson(density):
    highest = lax.Precision.HIGHEST
    sines_x = sine_table(0, NX, 0, NX, NX)
    sines_y = sine_table(0, NY, 0, NY, NY)
    sines_z = sine_table(0, NZ, 0, NZ, NZ)
    spectrum = jnp.einsum('cz,xyz->cxy', sines_z, density, precision=highest)
    spectrum = jnp.einsum('ax,cxy->ayc', sines_x, spectrum, precision=highest)
    spectrum = jnp.einsum('by,ayc->abc', sines_y, spectrum, precision=highest)
    divisor = eigen_values(0, NX, NX)[:, None, None] + eigen_values(0, NY, NY)[None, :, None] + eigen_values(0, NZ, NZ)[None, None, :]
    factor = 32.0 * jnp.pi / ((NX + 1) * (NY + 1) * (NZ + 1))
    scaled = spectrum * factor / divisor
    field_xyz = jnp.einsum('xa,abc->xbc', sines_x, scaled, precision=highest)
    field_xyz = jnp.einsum('yb,xbc->xyc', sines_y, field_xyz, precision=highest)
    return jnp.einsum('zc,xyc->xyz', sines_z, field_xyz, precision=highest)


def reference(orbitals, occupations, ext_pot, hartree_old):
    pot_start = ext_pot + hartree_old

    def add_density(density, members):
        orbital, weight = members
        predicted = taylor(orbital.astype(jnp.float32), pot_start)
        return density + weight * (predicted[0] * predicted[0] + predicted[1] * predicted[1]), None

    charge = lax.scan(add_density, jnp.zeros((NX, NY, NZ), jnp.float32), (orbitals, occupations))[0]
    density = charge - jnp.sum(charge) / (NX * NY * NZ)
    hartree_new = poisson(density)
    pot_middle = ext_pot + 0.5 * (hartree_old + hartree_new)
    orbitals_new = lax.map(lambda orbital: taylor(orbital.astype(jnp.float32), pot_middle), orbitals)
    return orbitals_new, hartree_new
```

```python
import functools
import math

import jax
import jax.numpy as jnp
import numpy as np
from jax import lax
from jax.experimental import pallas as pl
from jax.experimental.pallas import tpu as pltpu
from jax.sharding import PartitionSpec as P

NX, NY, NZ = 192, 128, 128
SLABS, ORBS, POIS = 4, 8, 4
WX, WY = NX // SLABS, NY // POIS
COMPS = 8
FWD = 13
BACK = 14
DEVICES = SLABS * ORBS * POIS
TRANSPOSE_AXES = ("orb", "pois", "slab")
DT = 0.3
HIGHEST = lax.Precision.HIGHEST
VMEM_LIMIT = 40 * 1024 * 1024
f32, bf16 = jnp.float32, jnp.bfloat16


def _sines(n):
    k = np.arange(1, n + 1)
    return np.sin(np.pi * ((k[:, None] * k[None, :]) % (2 * (n + 1))) / (n + 1))


def _lam(n):
    return 2.0 - 2.0 * np.cos(np.pi * np.arange(1, n + 1) / (n + 1))


@functools.cache
def _tables():
    sx, sy = _sines(NX), _sines(NY)
    order = np.array([s * WX + 4 * xb + xi for xi in range(4) for s in range(SLABS) for xb in range(WX // 4)])
    padded = np.zeros((SLABS * 64, NX))
    for s in range(SLABS):
        padded[s * 64 : s * 64 + WX] = sx[s * WX : (s + 1) * WX]
    ring_x = np.zeros((16, NX))
    ring_y = np.zeros((16, NY))
    for s in range(SLABS):
        if s > 0:
            ring_x[s] = sx[s * WX - 1]
        if s < SLABS - 1:
            ring_x[8 + s] = sx[(s + 1) * WX]
    for p in range(POIS):
        if p > 0:
            ring_y[p] = sy[p * WY - 1]
        if p < POIS - 1:
            ring_y[8 + p] = sy[(p + 1) * WY]
    back_x = np.concatenate([sx[order], padded, ring_x])
    modes = np.stack([_lam(NZ), sy.sum(1)])
    cast = lambda a: np.asarray(a, np.float32)
    return dict(
        sy=cast(sy),
        forward_x=cast(sx[:, order]),
        back_x=cast(back_x),
        ring_y=cast(ring_y),
        col=cast(np.stack([_lam(NX), sx.sum(1)] + [np.zeros(NX)] * 6, 1)),
        row=cast(np.stack([_lam(NY), sy.sum(1)] + [np.zeros(NY)] * 6, 0)),
        modes=cast(modes),
    )


def _iotas():
    return (
        lax.broadcasted_iota(jnp.int32, (8, 128), 0),
        lax.broadcasted_iota(jnp.int32, (8, 128), 1),
    )


def _zsum(v, lane):
    return jnp.where(lane == 0, 0.0, pltpu.roll(v, 1, 1)) + jnp.where(lane == 127, 0.0, pltpu.roll(v, 127, 1))


def _beside(below, v, above, low_row, high_row, sub, lane):
    down = [pltpu.roll(a, 1, 0) for a in v]
    up = [pltpu.roll(a, 7, 0) for a in v]
    out = []
    for i in range(4):
        d = jnp.where(sub == 0, down[i - 1] if i else low_row, down[i])
        u = jnp.where(sub == 7, up[i + 1] if i < 3 else high_row, up[i])
        out.append(((below[i] + above[i]) + (d + u)) + _zsum(v[i], lane))
    return out


def _pieces(plane):
    return [plane[8 * i : 8 * i + 8] for i in range(4)]


def _row8(ref_row):
    return jnp.broadcast_to(ref_row, (8, 128))


def _faces_kernel(psi, ext, old, x_left, x_right, y_left, y_right, c_ll, c_lr, c_rl, c_rr, rows):
    step = pl.program_id(0)

    @pl.when(step < COMPS)
    def _():
        x_left[0] = psi[0, 0:2]
        x_right[0] = psi[0, WX - 2 : WX]

        def fill(x, carry):
            top = psi[0, x, 0:16, :].astype(f32)
            bottom = psi[0, x, 16:32, :].astype(f32)
            rows[0, pl.ds(8 * x, 8), :] = top[0:8]
            rows[1, pl.ds(8 * x, 8), :] = bottom[8:16]
            return carry

        lax.fori_loop(0, WX, fill, 0, unroll=8)
        for half, ref, first in ((0, y_left, 0), (1, y_right, 6)):
            for d in range(2):
                ref[0, d] = rows[half, pl.ds(first + d, WX, 8), :].astype(bf16)
        for ref, half, y, x in (
            (c_ll, 0, 0, 0),
            (c_lr, 1, 7, 0),
            (c_rl, 0, 0, WX - 1),
            (c_rr, 1, 7, WX - 1),
        ):
            ref[0] = jnp.broadcast_to(rows[half, pl.ds(8 * x + y, 1), :], (8, 128)).astype(bf16)

    def potential(ref):
        def split(value, out, slot):
            high = value.astype(bf16)
            out[0, slot] = high
            out[0, slot + 1] = (value - high.astype(f32)).astype(bf16)

        split(ref[0], x_left, 0)
        split(ref[WX - 1], x_right, 0)

        def fill(x, carry):
            rows[0, pl.ds(8 * x, 8), :] = ref[x, 0:8, :]
            rows[1, pl.ds(8 * x, 8), :] = ref[x, 24:32, :]
            return carry

        lax.fori_loop(0, WX, fill, 0, unroll=8)
        split(rows[0, pl.ds(0, WX, 8), :], y_left, 0)
        split(rows[1, pl.ds(7, WX, 8), :], y_right, 0)
        for ref_c in (c_ll, c_lr, c_rl, c_rr):
            ref_c[0] = jnp.zeros((8, 128), bf16)

    @pl.when(step == COMPS)
    def _():
        potential(ext)

    @pl.when(step == COMPS + 1)
    def _():
        potential(old)


def _faces(psi, ext, old):
    steps = COMPS + 2
    whole = pl.BlockSpec((WX, WY, NZ), lambda i: (0, 0, 0))
    block = lambda *dims: pl.BlockSpec((1,) + dims, lambda i: (i,) + (0,) * len(dims))
    x_face, y_face, corner = (2, WY, NZ), (2, WX, NZ), (8, NZ)
    shapes = [x_face, x_face, y_face, y_face] + [corner] * 4
    return pl.pallas_call(
        _faces_kernel,
        name="faces",
        grid=(steps,),
        in_specs=[
            pl.BlockSpec((1, WX, WY, NZ), lambda i: (jnp.minimum(i, COMPS - 1), 0, 0, 0)),
            whole,
            whole,
        ],
        out_specs=[block(*s) for s in shapes],
        out_shape=[jax.ShapeDtypeStruct((steps,) + s, bf16) for s in shapes],
        scratch_shapes=[pltpu.VMEM((2, 8 * WX, 128), f32)],
        cost_estimate=pl.CostEstimate(flops=1000000, bytes_accessed=6000000, transcendentals=0),
    )(psi, ext, old)


def _images(psi, halo, mine, pot, ring, images, face_psi, face_image):
    x_low, x_high, y_low, y_high, corners = halo
    mine_low, mine_high = mine
    ring_y, ring_x = ring
    sub, lane = _iotas()
    slab, pois = lax.axis_index("slab"), lax.axis_index("pois")
    inside = lambda cond: jnp.where(cond, 1.0, 0.0).astype(f32)
    in_x = (inside(slab > 0), inside(slab < SLABS - 1))
    in_y = (inside(pois > 0), inside(pois < POIS - 1))

    def edge(c, carry):
        corner = [[corners[2 * i + j][c].astype(f32) for j in range(2)] for i in range(2)]
        for side, (far, near, own) in enumerate(((y_low, 1, mine_low), (y_high, 0, mine_high))):
            one = far[c, near].astype(f32)
            two = far[c, 1 - near].astype(f32)
            zero = own[c, side].astype(f32)
            n = WX // 8
            cells = [one[8 * i : 8 * i + 8] for i in range(n)]
            down = [pltpu.roll(a, 1, 0) for a in cells]
            up = [pltpu.roll(a, 7, 0) for a in cells]
            for i in range(n):
                d = jnp.where(sub == 0, down[i - 1] if i else corner[0][side], down[i])
                u = jnp.where(sub == 7, up[i + 1] if i < n - 1 else corner[1][side], up[i])
                total = (d + u) + (zero[8 * i : 8 * i + 8] + two[8 * i : 8 * i + 8]) + _zsum(cells[i], lane)
                face_psi[side, c, 8 * i : 8 * i + 8] = cells[i]
                face_image[side, c, 8 * i : 8 * i + 8] = in_y[side] * (
                    ring_y[side, 8 * i : 8 * i + 8] * cells[i] - 0.5 * total
                )
        plane = lambda ref, *i: _pieces(ref[(c,) + i].astype(f32))
        m2, m1 = plane(x_low, 0), plane(x_low, 1)
        q0, q1 = plane(x_high, 0), plane(x_high, 1)
        p0, p1, p46, p47 = plane(psi, 0), plane(psi, 1), plane(psi, WX - 2), plane(psi, WX - 1)
        for x, below, v, above, weight, scale, low, high in (
            (-1, m2, m1, p0, lambda i: ring_x[0, 8 * i : 8 * i + 8], in_x[0], corner[0][0], corner[0][1]),
            (0, m1, p0, p1, lambda i: pot[0, 8 * i : 8 * i + 8], None, 0, 0),
            (WX - 1, p46, p47, q0, lambda i: pot[WX - 1, 8 * i : 8 * i + 8], None, 0, 0),
            (WX, p47, q0, q1, lambda i: ring_x[1, 8 * i : 8 * i + 8], in_x[1], corner[1][0], corner[1][1]),
        ):
            if scale is None:
                low, high = (_row8(face_psi[side, c, x : x + 1, :]) for side in range(2))
            total = _beside(below, v, above, low, high, sub, lane)
            for i in range(4):
                value = weight(i) * v[i] - 0.5 * total[i]
                images[c, x + 1, 8 * i : 8 * i + 8] = value if scale is None else scale * value
        return carry

    lax.fori_loop(0, COMPS, edge, 0)

    def inner(x, carry):
        weight = [pot[x, 8 * i : 8 * i + 8] for i in range(4)]
        for c in range(COMPS):
            below, v, above = (_pieces(psi[c, x + d].astype(f32)) for d in (-1, 0, 1))
            low, high = (_row8(face_psi[side, c, pl.ds(x, 1), :]) for side in range(2))
            total = _beside(below, v, above, low, high, sub, lane)
            for i in range(4):
                images[c, x + 1, 8 * i : 8 * i + 8] = weight[i] * v[i] - 0.5 * total[i]
        return carry

    lax.fori_loop(1, WX - 1, inner, 0)


def _stepped(psi, orbital, x, weight, images, face_image, sub, lane):
    parts = []
    for c in (2 * orbital, 2 * orbital + 1):
        below, u, above = ([images[c, x + d, 8 * i : 8 * i + 8] for i in range(4)] for d in (0, 1, 2))
        low, high = (_row8(face_image[side, c, pl.ds(x, 1), :]) for side in range(2))
        total = _beside(below, u, above, low, high, sub, lane)
        second = [weight[i] * u[i] - 0.5 * total[i] for i in range(4)]
        parts.append((_pieces(psi[c, x].astype(f32)), u, second))
    (a, ua, wa), (b, ub, wb) = parts
    half = 0.5 * DT * DT
    real = [a[i] + DT * ub[i] - half * wa[i] for i in range(4)]
    imag = [b[i] - DT * ua[i] - half * wb[i] for i in range(4)]
    return real, imag


def _charge_kernel(
    occupations, psi, ext, old, x_low, x_high, y_low, y_high, c_ll, c_lr, c_rl, c_rr, mine_low, mine_high, sines,
    message, images, face_psi, face_image, pot, ring_y, ring_x, charge,
):
    sub, lane = _iotas()
    pot[...] = 3.0 + (ext[...] + old[...])
    pair = lambda ref, k: ref[k, 0].astype(f32) + ref[k, 1].astype(f32)
    for side, ref in enumerate((y_low, y_high)):
        ring_y[side] = 3.0 + (pair(ref, COMPS) + pair(ref, COMPS + 1))
    for side, ref in enumerate((x_low, x_high)):
        ring_x[side] = 3.0 + (pair(ref, COMPS) + pair(ref, COMPS + 1))
    _images(
        psi, (x_low, x_high, y_low, y_high, (c_ll, c_lr, c_rl, c_rr)), (mine_low, mine_high), pot, (ring_y, ring_x),
        images, face_psi, face_image,
    )
    occ = [occupations[k] for k in range(COMPS // 2)]

    def group(g, totals):
        def one(xi, carry):
            x = 4 * g + xi
            weight = [pot[x, 8 * i : 8 * i + 8] for i in range(4)]
            sums = [jnp.zeros((8, 128), f32) for _ in range(4)]
            for orbital in range(COMPS // 2):
                real, imag = _stepped(psi, orbital, x, weight, images, face_image, sub, lane)
                sums = [sums[i] + occ[orbital] * (real[i] * real[i] + imag[i] * imag[i]) for i in range(4)]
            for i in range(4):
                charge[pl.ds(pl.multiple_of(32 * xi + 8 * i, 8), 8), :] = sums[i]
            return carry + ((sums[0] + sums[1]) + (sums[2] + sums[3]))

        totals = lax.fori_loop(0, 4, one, totals)
        modes = lax.dot_general(
            sines[...], charge[...], (((1,), (1,)), ((), ())), precision=HIGHEST, preferred_element_type=f32
        )
        for k in range(16):
            message[pl.ds(8 * FWD * k + g, 8, FWD), :] = modes[8 * k : 8 * k + 8]
        return totals

    totals = lax.fori_loop(0, WX // 4, group, jnp.zeros((8, 128), f32))
    totals = jnp.broadcast_to(jnp.sum(totals, axis=0, keepdims=True), (8, 128))
    for k in range(16):
        message[pl.ds(8 * FWD * k + FWD - 1, 8, FWD), :] = totals


_IMAGE_SCRATCH = [
    pltpu.VMEM((COMPS, WX + 2, WY, NZ), f32),
    pltpu.VMEM((2, COMPS, WX, NZ), f32),
    pltpu.VMEM((2, COMPS, WX, NZ), f32),
    pltpu.VMEM((WX, WY, NZ), f32),
    pltpu.VMEM((2, WX, NZ), f32),
    pltpu.VMEM((2, WY, NZ), f32),
]

_VM = pl.BlockSpec(memory_space=pltpu.VMEM)
_SM = pl.BlockSpec(memory_space=pltpu.SMEM)


def _charge_messages(occupations, *arrays):
    return pl.pallas_call(
        _charge_kernel,
        name="charge",
        in_specs=[_SM] + [_VM] * len(arrays),
        out_specs=_VM,
        out_shape=jax.ShapeDtypeStruct((DEVICES * FWD, 128), f32),
        scratch_shapes=_IMAGE_SCRATCH + [pltpu.VMEM((128, 128), f32)],
        compiler_params=pltpu.CompilerParams(vmem_limit_bytes=VMEM_LIMIT),
        cost_estimate=pl.CostEstimate(flops=100000000, bytes_accessed=8000000, transcendentals=0),
    )(occupations, *arrays)


def _swap_groups(blocks, group):
    out = []
    for i in range(4):
        value = None
        for j in range(4):
            shift = (32 * (j - i)) % 128
            moved = pltpu.roll(blocks[j], shift, 1) if shift else blocks[j]
            value = moved if value is None else jnp.where(group == j, moved, value)
        out.append(value)
    return out


def _plane_kernel(modes, recv, forward_x, sy, back_x, ring_y, col, row, send, packed, block):
    dot = functools.partial(jnp.dot, precision=HIGHEST, preferred_element_type=f32)
    nt = lambda a, b: lax.dot_general(a, b, (((1,), (1,)), ((), ())), precision=HIGHEST, preferred_element_type=f32)
    kz = (lax.axis_index("orb") * POIS + lax.axis_index("pois")) * SLABS + lax.axis_index("slab")
    lam_z, sum_z = modes[0, kz], modes[1, kz]
    for p in range(POIS):
        for s in range(SLABS):
            total = None
            for o in range(ORBS):
                part = recv[pl.ds(((o * POIS + p) * SLABS + s) * FWD, 12), :]
                total = part if total is None else total + part
            packed[p, pl.ds(12 * s, 12), :] = total
    charge_total = jnp.sum(recv[pl.ds(FWD - 1, DEVICES, FWD), :])
    mean = charge_total / (NX * NY * NZ)
    group = lax.broadcasted_iota(jnp.int32, (WX, 128), 1) // 32
    plane = jnp.concatenate(_swap_groups([packed[p] for p in range(POIS)], group), axis=0)
    spectrum = dot(dot(forward_x[...], plane), sy[...])
    uniform = (mean * sum_z) * (col[:, 1:2] * row[1:2, :])
    divisor = col[:, 0:1] + row[0:1, :] + lam_z
    factor = 32.0 * math.pi / ((NX + 1) * (NY + 1) * (NZ + 1))
    scaled = (spectrum - uniform) * factor / divisor
    across = dot(back_x[...], scaled)
    field = dot(across[:NX], sy[...])
    ring = dot(across[NX + 256 :], sy[...])
    cells = _swap_groups([field[WX * i : WX * (i + 1)] for i in range(4)], group)
    lane8 = lax.broadcasted_iota(jnp.int32, (8, 128), 1)
    group8 = lane8 // 32
    faces = [nt(ring_y[...], across[NX + 128 * h : NX + 128 * (h + 1)]) for h in range(2)]
    y_rows = []
    for s in range(SLABS):
        low, high = faces[s // 2][0:8], faces[s // 2][8:16]
        if s % 2 == 0:
            high = pltpu.roll(high, 64, 1)
        else:
            low = pltpu.roll(low, 64, 1)
        y_rows.append(jnp.where(lane8 < 64, low, high))
    for p in range(POIS):
        shift = lambda v, k: pltpu.roll(v, k % 128, 1) if k % 128 else v
        x_rows = jnp.where(
            group8 == 0,
            shift(ring[0:8], -32 * p),
            jnp.where(group8 == 1, shift(ring[8:16], 32 - 32 * p), 0.0),
        )
        for s in range(SLABS):
            base = (p * SLABS + s) * BACK
            block[pl.ds(base, 12), :] = cells[p][12 * s : 12 * s + 12]
            block[pl.ds(base + 12, 1), :] = x_rows[s : s + 1]
            block[pl.ds(base + 13, 1), :] = y_rows[s][p : p + 1]
    count = POIS * SLABS * BACK
    for o in range(ORBS):
        send[pl.ds(o * count, count), :] = block[...]


def _plane(recv):
    t = _tables()
    return pl.pallas_call(
        _plane_kernel,
        name="plane",
        in_specs=[_SM] + [_VM] * 7,
        out_specs=_VM,
        out_shape=jax.ShapeDtypeStruct((DEVICES * BACK, 128), f32),
        scratch_shapes=[
            pltpu.VMEM((POIS, WX, 128), f32),
            pltpu.VMEM((POIS * SLABS * BACK, 128), f32),
        ],
        cost_estimate=pl.CostEstimate(flops=200000000, bytes_accessed=3000000, transcendentals=0),
    )(
        jnp.asarray(t["modes"]),
        recv,
        *(jnp.asarray(t[k]) for k in ("forward_x", "sy", "back_x", "ring_y", "col", "row")),
    )


def _step_kernel(
    psi, ext, old, x_low, x_high, y_low, y_high, c_ll, c_lr, c_rl, c_rr, mine_low, mine_high, sines, recv,
    new, hartree, images, face_psi, face_image, pot, ring_y, ring_x,
):
    sub, lane = _iotas()
    orb = lax.axis_index("orb")
    back = lambda r: lax.dot_general(
        recv[pl.ds(r, 128, BACK), :], sines[...], (((0,), (0,)), ((), ())), precision=HIGHEST, preferred_element_type=f32
    )
    shift = lax.rem(128 - 16 * orb, 128)

    def planes(g, carry):
        field = back(g)
        mine = pltpu.roll(field, shift, 1)
        for xi in range(4):
            x = 4 * g + xi
            cells = field[32 * xi : 32 * xi + 32]
            pot[x] = 3.0 + (ext[x] + 0.5 * (old[x] + cells))
            hartree[x] = mine[32 * xi : 32 * xi + 32, 0:16]
        return carry

    lax.fori_loop(0, WX // 4, planes, 0)
    pair = lambda ref, k: ref[k, 0].astype(f32) + ref[k, 1].astype(f32)
    field = back(12)
    for side, ref in enumerate((x_low, x_high)):
        cells = field[32 * side : 32 * side + 32]
        ring_x[side] = 3.0 + (pair(ref, COMPS) + 0.5 * (pair(ref, COMPS + 1) + cells))
    field = back(13)
    for side, ref in enumerate((y_low, y_high)):
        cells = field[64 * side : 64 * side + WX]
        ring_y[side] = 3.0 + (pair(ref, COMPS) + 0.5 * (pair(ref, COMPS + 1) + cells))
    _images(
        psi, (x_low, x_high, y_low, y_high, (c_ll, c_lr, c_rl, c_rr)), (mine_low, mine_high), pot, (ring_y, ring_x),
        images, face_psi, face_image,
    )

    def one(x, carry):
        weight = [pot[x, 8 * i : 8 * i + 8] for i in range(4)]
        for orbital in range(COMPS // 2):
            real, imag = _stepped(psi, orbital, x, weight, images, face_image, sub, lane)
            for i in range(4):
                new[2 * orbital, x, 8 * i : 8 * i + 8] = real[i]
                new[2 * orbital + 1, x, 8 * i : 8 * i + 8] = imag[i]
        return carry

    lax.fori_loop(0, WX, one, 0)


def _step(*arrays):
    return pl.pallas_call(
        _step_kernel,
        name="step",
        in_specs=[_VM] * len(arrays),
        out_specs=[_VM, _VM],
        out_shape=[
            jax.ShapeDtypeStruct((COMPS, WX, WY, NZ), f32),
            jax.ShapeDtypeStruct((WX, WY, NZ // ORBS), f32),
        ],
        scratch_shapes=_IMAGE_SCRATCH,
        compiler_params=pltpu.CompilerParams(vmem_limit_bytes=VMEM_LIMIT),
        cost_estimate=pl.CostEstimate(flops=100000000, bytes_accessed=12000000, transcendentals=0),
    )(*arrays)


def _exchange(sent):
    x_left, x_right, y_left, y_right, c_ll, c_lr, c_rl, c_rr = sent
    up = lambda n: [(i, i + 1) for i in range(n - 1)]
    down = lambda n: [(i + 1, i) for i in range(n - 1)]
    y_low = lax.ppermute(y_right, "pois", up(POIS))
    y_high = lax.ppermute(y_left, "pois", down(POIS))
    x_low = lax.ppermute(x_right, "slab", up(SLABS))
    x_high = lax.ppermute(x_left, "slab", down(SLABS))

    def diagonal(value, ds, dp):
        pairs = [
            (s * POIS + p, (s + ds) * POIS + p + dp)
            for s in range(SLABS)
            for p in range(POIS)
            if 0 <= s + ds < SLABS and 0 <= p + dp < POIS
        ]
        return lax.ppermute(value, ("slab", "pois"), pairs)

    return (
        x_low, x_high, y_low, y_high,
        diagonal(c_rr, 1, 1), diagonal(c_rl, 1, -1), diagonal(c_lr, -1, 1), diagonal(c_ll, -1, -1),
        y_left, y_right,
    )


def _swap(messages, rows):
    moved = lax.all_to_all(messages.reshape(DEVICES, 1, rows * 128), TRANSPOSE_AXES, 0, 0)
    return moved.reshape(DEVICES * rows, 128)


def body(orbitals, occupations, ext_pot, hartree_old):
    psi = orbitals.reshape(COMPS, WX, WY, NZ)
    halo = _exchange(_faces(psi, ext_pot, hartree_old))
    sines = jnp.asarray(_tables()["sy"])
    message = _charge_messages(occupations, psi, ext_pot, hartree_old, *halo, sines)
    back = _swap(_plane(_swap(message, FWD)), BACK)
    new, hartree = _step(psi, ext_pot, hartree_old, *halo, sines, back)
    return new.reshape(orbitals.shape), hartree


def solution(mesh):
    placed = (P("orb", None, "slab", "pois", None), P("orb"), P("slab", "pois", None), P("slab", "pois", None))
    return jax.shard_map(
        body,
        mesh=mesh,
        in_specs=placed,
        out_specs=(P("orb", None, "slab", "pois", None), P("slab", "pois", "orb")),
        check_vma=False,
    )
```

```python
import functools
import math

import jax
import jax.numpy as jnp
import ml_dtypes
import numpy as np
from jax import lax
from jax.experimental import pallas as pl
from jax.experimental.pallas import tpu as pltpu
from jax.sharding import PartitionSpec as P

NX, NY, NZ = 192, 128, 128
SLABS, ORBS, POIS = 4, 8, 4
WX, WY = NX // SLABS, NY // POIS
COMPS = 8
FWD = 13
BACK = 14
DEVICES = SLABS * ORBS * POIS
TRANSPOSE_AXES = ("orb", "pois", "slab")
DT = 0.3
HIGHEST = lax.Precision.HIGHEST
VMEM_LIMIT = 44 * 1024 * 1024
PITCH = 40
PLANES = WX + 2
PADDED = 8 + PLANES * PITCH
GROUP = 10
f32, bf16 = jnp.float32, jnp.bfloat16


def _sines(n):
    k = np.arange(1, n + 1)
    return np.sin(np.pi * ((k[:, None] * k[None, :]) % (2 * (n + 1))) / (n + 1))


def _lam(n):
    return 2.0 - 2.0 * np.cos(np.pi * np.arange(1, n + 1) / (n + 1))


@functools.cache
def _tables():
    sx, sy = _sines(NX), _sines(NY)
    order = np.array([s * WX + 4 * xb + xi for xi in range(4) for s in range(SLABS) for xb in range(WX // 4)])
    padded = np.zeros((SLABS * 64, NX))
    for s in range(SLABS):
        padded[s * 64 : s * 64 + WX] = sx[s * WX : (s + 1) * WX]
    ring_x = np.zeros((16, NX))
    ring_y = np.zeros((16, NY))
    for s in range(SLABS):
        if s > 0:
            ring_x[s] = sx[s * WX - 1]
        if s < SLABS - 1:
            ring_x[8 + s] = sx[(s + 1) * WX]
    for p in range(POIS):
        if p > 0:
            ring_y[p] = sy[p * WY - 1]
        if p < POIS - 1:
            ring_y[8 + p] = sy[(p + 1) * WY]
    back_x = np.concatenate([sx[order], padded, ring_x])
    modes = np.stack([_lam(NZ), sy.sum(1)])
    cast = lambda a: np.asarray(a, np.float32)
    high = cast(sy).astype(ml_dtypes.bfloat16)
    low = (cast(sy) - high.astype(np.float32)).astype(ml_dtypes.bfloat16)
    tiles = [np.arange(128) % (NZ // ORBS) + o * (NZ // ORBS) for o in range(ORBS)]
    stacked = np.concatenate([high, high, low], 0)
    shift = np.eye(NZ, k=1) + np.eye(NZ, k=-1)
    near = np.concatenate([-np.eye(NZ), -shift, -np.eye(NZ)], 0)
    return dict(
        near=near.astype(ml_dtypes.bfloat16),
        beside=np.concatenate([high, high, low], 1),
        stacked=stacked,
        tiled=np.stack([stacked[:, t] for t in tiles]),
        sy=cast(sy),
        forward_x=cast(sx[:, order]),
        back_x=cast(back_x),
        ring_y=cast(ring_y),
        col=cast(np.stack([_lam(NX), sx.sum(1)] + [np.zeros(NX)] * 6, 1)),
        row=cast(np.stack([_lam(NY), sy.sum(1)] + [np.zeros(NY)] * 6, 0)),
        modes=cast(modes),
    )


_VM = pl.BlockSpec(memory_space=pltpu.VMEM)
_SM = pl.BlockSpec(memory_space=pltpu.SMEM)
_ANY = pl.BlockSpec(memory_space=pl.ANY)
_X_FACE, _Y_FACE, _CORNER = (2, WY, NZ), (2, WX, NZ), (8, NZ)
_FACES = [_X_FACE, _X_FACE, _Y_FACE, _Y_FACE] + [_CORNER] * 4


def _iotas():
    return (
        lax.broadcasted_iota(jnp.int32, (8, 128), 0),
        lax.broadcasted_iota(jnp.int32, (8, 128), 1),
    )


def _zsum(v, lane):
    return jnp.where(lane == 0, 0.0, pltpu.roll(v, 1, 1)) + jnp.where(lane == 127, 0.0, pltpu.roll(v, 127, 1))


def _base(plane):
    return pl.multiple_of(8 + PITCH * plane, 8)


def _split(value):
    high = value.astype(bf16)
    return high, (value - high.astype(f32)).astype(bf16)


def _faces_kernel(psi, ext, old, x_left, x_right, y_left, y_right, c_ll, c_lr, c_rl, c_rr, psi_v, pots, rows, sems):
    copies = [pltpu.make_async_copy(psi.at[c], psi_v.at[c], sems.at[c]) for c in range(COMPS)]
    copies += [pltpu.make_async_copy(ref, pots.at[k], sems.at[COMPS + k]) for k, ref in enumerate((ext, old))]
    for copy in copies:
        copy.start()
    for c in range(COMPS):
        copies[c].wait()

        def fill(x, carry, c=c):
            rows[0, pl.ds(pl.multiple_of(8 * x, 8), 8), :] = psi_v[c, x, 0:16, :].astype(f32)[0:8]
            rows[1, pl.ds(pl.multiple_of(8 * x, 8), 8), :] = psi_v[c, x, 16:32, :].astype(f32)[8:16]
            return carry

        lax.fori_loop(0, WX, fill, 0, unroll=8)
        x_left[c] = psi_v[c, 0:2]
        x_right[c] = psi_v[c, WX - 2 : WX]
        for half, ref, first in ((0, y_left, 0), (1, y_right, 6)):
            for d in range(2):
                ref[c, d] = rows[half, pl.ds(first + d, WX, 8), :].astype(bf16)
        for ref, half, y, x in ((c_ll, 0, 0, 0), (c_lr, 1, 7, 0), (c_rl, 0, 0, WX - 1), (c_rr, 1, 7, WX - 1)):
            ref[c] = jnp.broadcast_to(rows[half, pl.ds(8 * x + y, 1), :], (8, 128)).astype(bf16)
    for k in range(2):
        copies[COMPS + k].wait()

        def fill_pot(x, carry, k=k):
            rows[0, pl.ds(pl.multiple_of(8 * x, 8), 8), :] = pots[k, x, 0:8, :]
            rows[1, pl.ds(pl.multiple_of(8 * x, 8), 8), :] = pots[k, x, 24:32, :]
            return carry

        lax.fori_loop(0, WX, fill_pot, 0, unroll=8)
        for ref, value in (
            (x_left, pots[k, 0]),
            (x_right, pots[k, WX - 1]),
            (y_left, rows[0, pl.ds(0, WX, 8), :]),
            (y_right, rows[1, pl.ds(7, WX, 8), :]),
        ):
            ref[COMPS + k, 0], ref[COMPS + k, 1] = _split(value)
        for ref in (c_ll, c_lr, c_rl, c_rr):
            ref[COMPS + k] = jnp.zeros((8, 128), bf16)


def _faces(psi, ext, old):
    return pl.pallas_call(
        _faces_kernel,
        name="faces",
        in_specs=[_ANY] * 3,
        out_specs=[_VM] * len(_FACES),
        out_shape=[jax.ShapeDtypeStruct((COMPS + 2,) + s, bf16) for s in _FACES],
        scratch_shapes=[
            pltpu.VMEM((COMPS, WX, WY, NZ), bf16),
            pltpu.VMEM((2, WX, WY, NZ), f32),
            pltpu.VMEM((2, 8 * WX, 128), f32),
            pltpu.SemaphoreType.DMA((COMPS + 2,)),
        ],
        cost_estimate=pl.CostEstimate(flops=1000000, bytes_accessed=6000000, transcendentals=0),
    )(psi, ext, old)


_SHARED_SCRATCH = (
    [
        pltpu.VMEM((COMPS, (WX + 4) * WY, NZ), bf16),
        pltpu.VMEM((COMPS, PADDED, NZ), f32),
        pltpu.VMEM((COMPS, PADDED, NZ), f32),
        pltpu.VMEM((PLANES * WY, NZ), f32),
        pltpu.VMEM((2, WX, NZ), f32),
        pltpu.VMEM((2, WX * WY, NZ), f32),
    ]
    + [pltpu.VMEM((COMPS + 2,) + s, bf16) for s in _FACES]
    + [pltpu.SemaphoreType.DMA((COMPS + 2 + len(_FACES),))]
)


def _fetch(hbm, scratch):
    psi, ext, old = hbm[:3]
    psi_v, pots, sems = scratch[0], scratch[5], scratch[-1]
    pairs = [(ref, buffer) for ref, buffer in zip(hbm[3:], scratch[6:-1])]
    pairs += [(ext, pots.at[0]), (old, pots.at[1])]
    pairs += [(psi.at[c], psi_v.at[c, pl.ds(2 * WY, WX * WY)]) for c in range(COMPS)]
    copies = [pltpu.make_async_copy(a, b, sems.at[k]) for k, (a, b) in enumerate(pairs)]
    for copy in copies:
        copy.start()
    return copies


def _inside():
    slab, pois = lax.axis_index("slab"), lax.axis_index("pois")
    number = lambda cond: jnp.where(cond, 1.0, 0.0).astype(f32)
    return (
        (number(slab > 0), number(slab < SLABS - 1)),
        (number(pois > 0), number(pois < POIS - 1)),
    )


def _pair(ref, k):
    return ref[k, 0].astype(f32) + ref[k, 1].astype(f32)


def _images(scratch, near, psi_copies):
    psi_v, psi_f, image, pot, ring_y, _ = scratch[:6]
    x_faces, y_faces, corners = scratch[6:8], scratch[8:10], scratch[10:14]
    in_x, in_y = _inside()
    sub, lane = _iotas()
    for c in range(COMPS):
        psi_copies[c].wait()

    def one(c, carry):
        for side in range(2):
            first = (WX + 2) * WY * side
            for d in range(2):
                value = x_faces[side][c, d].astype(f32) * in_x[side]
                psi_v[c, pl.ds(first + WY * d, WY)] = value.astype(bf16)

        def widen(p, carry):
            value = psi_v[c, pl.ds(pl.multiple_of(WY * (p + 1), WY), WY)].astype(f32)
            psi_f[c, pl.ds(_base(p), WY)] = value
            return carry

        lax.fori_loop(0, PLANES, widen, 0, unroll=10)
        for side in range(2):
            row = 8 + PITCH + (WY if side else -1)
            face = y_faces[side][c, 1 - side].astype(f32) * in_y[side]
            psi_f[c, pl.ds(row, WX, PITCH)] = face
            for i in range(2):
                corner = corners[2 * i + side][c].astype(f32) * (in_x[i] * in_y[side])
                at = 8 + PITCH * (PLANES - 1) * i + (WY if side else -1)
                psi_f[c, pl.ds(at, 1)] = corner[0:1]

        def group(j, carry):
            start = pl.multiple_of(GROUP * WY * j, WY)
            rows = GROUP * WY
            views = [psi_v[c, pl.ds(pl.multiple_of(start + WY * d, WY), rows)] for d in range(3)]
            sums = jnp.dot(jnp.concatenate(views, axis=1), near[...], preferred_element_type=f32)
            for g in range(GROUP):
                base = _base(GROUP * j + g)
                for i in range(4):
                    at = base + 8 * i
                    beside = psi_f[c, pl.ds(at - 1, 8)] + psi_f[c, pl.ds(at + 1, 8)]
                    weight = pot[pl.ds(pl.multiple_of(start + WY * g + 8 * i, 8), 8)]
                    value = weight * psi_f[c, pl.ds(pl.multiple_of(at, 8), 8)] - beside
                    first = WY * g + 8 * i
                    image[c, pl.ds(pl.multiple_of(at, 8), 8)] = sums[first : first + 8] + value
            return carry

        lax.fori_loop(0, PLANES // GROUP, group, 0)
        for i in range(2):
            edge = pl.ds(8 + PITCH * (PLANES - 1) * i, WY)
            image[c, edge] = image[c, edge] * in_x[i]
        for side in range(2):
            row = 8 + PITCH + (WY if side else -1)
            inward = -1 if side else 1
            cells = psi_f[c, pl.ds(row, WX, PITCH)]
            before = psi_f[c, pl.ds(row - PITCH, WX, PITCH)]
            after = psi_f[c, pl.ds(row + PITCH, WX, PITCH)]
            inner = psi_f[c, pl.ds(row + inward, WX, PITCH)]
            outer = y_faces[side][c, side].astype(f32)
            total = (before + after) + (inner + outer)
            value = [
                ring_y[side, 8 * i : 8 * i + 8] * cells[8 * i : 8 * i + 8]
                - (total[8 * i : 8 * i + 8] + _zsum(cells[8 * i : 8 * i + 8], lane))
                for i in range(WX // 8)
            ]
            image[c, pl.ds(row, WX, PITCH)] = jnp.concatenate(value, axis=0) * in_y[side]
        return carry

    lax.fori_loop(0, COMPS, one, 0)


def _stepped(scratch, orbital, x, i, lane):
    psi_f, image, pot = scratch[1], scratch[2], scratch[3]
    at = _base(x + 1) + 8 * i
    weight = pot[pl.ds(pl.multiple_of(WY * (x + 1) + 8 * i, 8), 8)]
    parts = []
    for c in (2 * orbital, 2 * orbital + 1):
        load = lambda row, hint=True: image[c, pl.ds(pl.multiple_of(row, 8) if hint else row, 8)]
        u = load(at)
        total = (load(at - PITCH) + load(at + PITCH)) + (load(at - 1, False) + load(at + 1, False)) + _zsum(u, lane)
        second = weight * u - total
        parts.append((psi_f[c, pl.ds(pl.multiple_of(at, 8), 8)], u, second))
    (a, ua, wa), (b, ub, wb) = parts
    scale = 0.125 * DT * DT
    return (a - scale * wa) + (0.5 * DT) * ub, (b - scale * wb) - (0.5 * DT) * ua


def _charge_kernel(occupations, near, beside, *refs):
    count = 3 + len(_FACES)
    hbm, message, scratch, charge = refs[:count], refs[count], refs[count + 1 : -1], refs[-1]
    copies = _fetch(hbm, scratch)
    pot, ring_y, pots = scratch[3:6]
    x_faces, y_faces = scratch[6:8], scratch[8:10]
    _, lane = _iotas()
    for copy in copies[:-COMPS]:
        copy.wait()
    pot[pl.ds(WY, WX * WY)] = 6.0 + 2.0 * (pots[0] + pots[1])
    for side in range(2):
        ring_y[side] = 6.0 + 2.0 * (_pair(y_faces[side], COMPS) + _pair(y_faces[side], COMPS + 1))
        edge = pl.ds((WX + 1) * WY * side, WY)
        pot[edge] = 6.0 + 2.0 * (_pair(x_faces[side], COMPS) + _pair(x_faces[side], COMPS + 1))
    _images(scratch, near, copies[-COMPS:])
    occ = [occupations[k] for k in range(COMPS // 2)]

    def group(g, totals):
        def one(xi, carry):
            for i in range(4):
                sums = None
                for orbital in range(COMPS // 2):
                    real, imag = _stepped(scratch, orbital, 4 * g + xi, i, lane)
                    term = occ[orbital] * (real * real + imag * imag)
                    sums = term if sums is None else sums + term
                charge[pl.ds(pl.multiple_of(32 * xi + 8 * i, 8), 8), :] = sums
                carry = carry + sums
            return carry

        totals = lax.fori_loop(0, 4, one, totals)
        high, low = _split(charge[...])
        modes = lax.dot_general(
            beside[...],
            jnp.concatenate([high, low, high], axis=1),
            (((1,), (1,)), ((), ())),
            preferred_element_type=f32,
        )
        for k in range(16):
            message[pl.ds(8 * FWD * k + g, 8, FWD), :] = modes[8 * k : 8 * k + 8]
        return totals

    totals = lax.fori_loop(0, WX // 4, group, jnp.zeros((8, 128), f32))
    totals = jnp.broadcast_to(jnp.sum(totals, axis=0, keepdims=True), (8, 128))
    for k in range(16):
        message[pl.ds(8 * FWD * k + FWD - 1, 8, FWD), :] = totals


def _charge_messages(occupations, *arrays):
    t = _tables()
    return pl.pallas_call(
        _charge_kernel,
        name="charge",
        in_specs=[_SM, _VM, _VM] + [_ANY] * len(arrays),
        out_specs=_VM,
        out_shape=jax.ShapeDtypeStruct((DEVICES * FWD, 128), f32),
        scratch_shapes=_SHARED_SCRATCH + [pltpu.VMEM((128, 128), f32)],
        compiler_params=pltpu.CompilerParams(vmem_limit_bytes=VMEM_LIMIT),
        cost_estimate=pl.CostEstimate(flops=100000000, bytes_accessed=8000000, transcendentals=0),
    )(occupations, jnp.asarray(t["near"]), jnp.asarray(t["beside"]), *arrays)


def _swap_groups(blocks, group):
    out = []
    for i in range(4):
        value = None
        for j in range(4):
            shift = (32 * (j - i)) % 128
            moved = pltpu.roll(blocks[j], shift, 1) if shift else blocks[j]
            value = moved if value is None else jnp.where(group == j, moved, value)
        out.append(value)
    return out


def _plane_kernel(modes, recv, forward_x, sy, back_x, ring_y, col, row, send, packed, block):
    dot = functools.partial(jnp.dot, precision=HIGHEST, preferred_element_type=f32)
    nt = lambda a, b: lax.dot_general(a, b, (((1,), (1,)), ((), ())), precision=HIGHEST, preferred_element_type=f32)
    kz = (lax.axis_index("orb") * POIS + lax.axis_index("pois")) * SLABS + lax.axis_index("slab")
    lam_z, sum_z = modes[0, kz], modes[1, kz]
    for p in range(POIS):
        for s in range(SLABS):
            total = None
            for o in range(ORBS):
                part = recv[pl.ds(((o * POIS + p) * SLABS + s) * FWD, 12), :]
                total = part if total is None else total + part
            packed[p, pl.ds(12 * s, 12), :] = total
    charge_total = jnp.sum(recv[pl.ds(FWD - 1, DEVICES, FWD), :])
    mean = charge_total / (NX * NY * NZ)
    group = lax.broadcasted_iota(jnp.int32, (WX, 128), 1) // 32
    plane = jnp.concatenate(_swap_groups([packed[p] for p in range(POIS)], group), axis=0)
    spectrum = dot(dot(forward_x[...], plane), sy[...])
    uniform = (mean * sum_z) * (col[:, 1:2] * row[1:2, :])
    divisor = col[:, 0:1] + row[0:1, :] + lam_z
    factor = 32.0 * math.pi / ((NX + 1) * (NY + 1) * (NZ + 1))
    scaled = (spectrum - uniform) * factor / divisor
    across = dot(back_x[...], scaled)
    field = dot(across[:NX], sy[...])
    ring = dot(across[NX + 256 :], sy[...])
    cells = _swap_groups([field[WX * i : WX * (i + 1)] for i in range(4)], group)
    lane8 = lax.broadcasted_iota(jnp.int32, (8, 128), 1)
    group8 = lane8 // 32
    faces = [nt(ring_y[...], across[NX + 128 * h : NX + 128 * (h + 1)]) for h in range(2)]
    y_rows = []
    for s in range(SLABS):
        low, high = faces[s // 2][0:8], faces[s // 2][8:16]
        if s % 2 == 0:
            high = pltpu.roll(high, 64, 1)
        else:
            low = pltpu.roll(low, 64, 1)
        y_rows.append(jnp.where(lane8 < 64, low, high))
    for p in range(POIS):
        shift = lambda v, k: pltpu.roll(v, k % 128, 1) if k % 128 else v
        x_rows = jnp.where(
            group8 == 0,
            shift(ring[0:8], -32 * p),
            jnp.where(group8 == 1, shift(ring[8:16], 32 - 32 * p), 0.0),
        )
        for s in range(SLABS):
            base = (p * SLABS + s) * BACK
            block[pl.ds(base, 12), :] = cells[p][12 * s : 12 * s + 12]
            block[pl.ds(base + 12, 1), :] = x_rows[s : s + 1]
            block[pl.ds(base + 13, 1), :] = y_rows[s][p : p + 1]
    count = POIS * SLABS * BACK
    for o in range(ORBS):
        send[pl.ds(o * count, count), :] = block[...]


def _plane(recv):
    t = _tables()
    return pl.pallas_call(
        _plane_kernel,
        name="plane",
        in_specs=[_SM] + [_VM] * 7,
        out_specs=_VM,
        out_shape=jax.ShapeDtypeStruct((DEVICES * BACK, 128), f32),
        scratch_shapes=[
            pltpu.VMEM((POIS, WX, 128), f32),
            pltpu.VMEM((POIS * SLABS * BACK, 128), f32),
        ],
        cost_estimate=pl.CostEstimate(flops=200000000, bytes_accessed=3000000, transcendentals=0),
    )(
        jnp.asarray(t["modes"]),
        recv,
        *(jnp.asarray(t[k]) for k in ("forward_x", "sy", "back_x", "ring_y", "col", "row")),
    )


OUT_GROUP = 8


def _step_kernel(near, stacked, recv, tiled_hbm, *refs):
    count = 3 + len(_FACES)
    hbm, new, hartree = refs[:count], refs[count], refs[count + 1]
    scratch = refs[count + 2 : count + 2 + len(_SHARED_SCRATCH)]
    tiled, slices, out, tiled_sem, out_sems = refs[count + 2 + len(_SHARED_SCRATCH) :]
    tiled_copy = pltpu.make_async_copy(tiled_hbm.at[lax.axis_index("orb")], tiled, tiled_sem)
    tiled_copy.start()
    copies = _fetch(hbm, scratch)
    pot, ring_y, pots = scratch[3:6]
    x_faces, y_faces = scratch[6:8], scratch[8:10]
    sub, lane = _iotas()
    for copy in copies[:-COMPS]:
        copy.wait()
    tiled_copy.wait()

    def back(r, table):
        high, low = _split(recv[pl.ds(r, 128, BACK), :])
        stack = jnp.concatenate([high, low, high], axis=0)
        return lax.dot_general(stack, table[...], (((0,), (0,)), ((), ())), preferred_element_type=f32)

    def planes(g, carry):
        field = back(g, stacked)
        first = pl.multiple_of(4 * WY * g, 8)
        block = pl.ds(first, 4 * WY)
        pot[pl.ds(pl.multiple_of(first + WY, 8), 4 * WY)] = 6.0 + (2.0 * pots[0, block] + (pots[1, block] + field))
        mine = back(g, tiled)
        for k in range(16):
            kept = jnp.where(lane // 16 == sub, mine[8 * k : 8 * k + 8], 0.0)
            slices[k % 4, pl.ds(4 * g + k // 4, 1), :] = jnp.sum(kept, axis=0, keepdims=True)
        return carry

    lax.fori_loop(0, WX // 4, planes, 0)
    field = back(12, stacked)
    for side in range(2):
        edge = pl.ds((WX + 1) * WY * side, WY)
        face = x_faces[side]
        cells = field[32 * side : 32 * side + 32]
        pot[edge] = 6.0 + (2.0 * _pair(face, COMPS) + (_pair(face, COMPS + 1) + cells))
    field = back(13, stacked)
    for side in range(2):
        face = y_faces[side]
        cells = field[64 * side : 64 * side + WX]
        ring_y[side] = 6.0 + (2.0 * _pair(face, COMPS) + (_pair(face, COMPS + 1) + cells))
    for q in range(4):
        turned = jnp.transpose(slices[q])
        for y in range(8):
            hartree[8 * q + y] = turned[16 * y : 16 * y + 16, 0:WX]
    _images(scratch, near, copies[-COMPS:])

    def out_copy(j, c):
        planes = pl.ds(OUT_GROUP * j, OUT_GROUP)
        return pltpu.make_async_copy(out.at[c, planes], new.at[c, planes], out_sems.at[j, c])

    def group(j, carry):
        def one(k, carry):
            x = OUT_GROUP * j + k
            for i in range(4):
                for orbital in range(COMPS // 2):
                    real, imag = _stepped(scratch, orbital, x, i, lane)
                    out[2 * orbital, x, 8 * i : 8 * i + 8] = real
                    out[2 * orbital + 1, x, 8 * i : 8 * i + 8] = imag
            return carry

        lax.fori_loop(0, OUT_GROUP, one, 0)
        for c in range(COMPS):
            out_copy(j, c).start()
        return carry

    lax.fori_loop(0, WX // OUT_GROUP, group, 0)
    for j in range(WX // OUT_GROUP):
        for c in range(COMPS):
            out_copy(j, c).wait()


def _step(recv, *arrays):
    t = _tables()
    return pl.pallas_call(
        _step_kernel,
        name="step",
        in_specs=[_VM, _VM, _VM, _ANY] + [_ANY] * len(arrays),
        out_specs=[_ANY, _VM],
        out_shape=[
            jax.ShapeDtypeStruct((COMPS, WX, WY, NZ), f32),
            jax.ShapeDtypeStruct((WY, NZ // ORBS, WX), f32),
        ],
        scratch_shapes=_SHARED_SCRATCH
        + [
            pltpu.VMEM((3 * NZ, 128), bf16),
            pltpu.VMEM((4, 128, 128), f32),
            pltpu.VMEM((COMPS, WX, WY, NZ), f32),
            pltpu.SemaphoreType.DMA,
            pltpu.SemaphoreType.DMA((WX // OUT_GROUP, COMPS)),
        ],
        compiler_params=pltpu.CompilerParams(vmem_limit_bytes=VMEM_LIMIT),
        cost_estimate=pl.CostEstimate(flops=100000000, bytes_accessed=12000000, transcendentals=0),
    )(jnp.asarray(t["near"]), jnp.asarray(t["stacked"]), recv, jnp.asarray(t["tiled"]), *arrays)


def _exchange(sent):
    x_left, x_right, y_left, y_right, c_ll, c_lr, c_rl, c_rr = sent
    ring = lambda n, d: [(i, (i + d) % n) for i in range(n)]
    y_low = lax.ppermute(y_right, "pois", ring(POIS, 1))
    y_high = lax.ppermute(y_left, "pois", ring(POIS, -1))
    x_low = lax.ppermute(x_right, "slab", ring(SLABS, 1))
    x_high = lax.ppermute(x_left, "slab", ring(SLABS, -1))

    def diagonal(value, ds, dp):
        pairs = [
            (s * POIS + p, (s + ds) % SLABS * POIS + (p + dp) % POIS) for s in range(SLABS) for p in range(POIS)
        ]
        return lax.ppermute(value, ("slab", "pois"), pairs)

    return (
        x_low, x_high, y_low, y_high,
        diagonal(c_rr, 1, 1), diagonal(c_rl, 1, -1), diagonal(c_lr, -1, 1), diagonal(c_ll, -1, -1),
    )


def _swap(messages, rows):
    moved = lax.all_to_all(messages.reshape(DEVICES, 1, rows * 128), TRANSPOSE_AXES, 0, 0)
    return moved.reshape(DEVICES * rows, 128)


def body(orbitals, occupations, ext_pot, hartree_old):
    cells = orbitals.reshape(COMPS, WX, WY, NZ)
    halo = _exchange(_faces(cells, ext_pot, hartree_old))
    flat = lambda a: a.reshape(WX * WY, NZ)
    arrays = (orbitals.reshape(COMPS, WX * WY, NZ), flat(ext_pot), flat(hartree_old), *halo)
    message = _charge_messages(occupations, *arrays)
    new, hartree = _step(_swap(_plane(_swap(message, FWD)), BACK), *arrays)
    return new.reshape(orbitals.shape), jnp.transpose(hartree, (2, 0, 1))


def solution(mesh):
    placed = (P("orb", None, "slab", "pois", None), P("orb"), P("slab", "pois", None), P("slab", "pois", None))
    return jax.shard_map(
        body,
        mesh=mesh,
        in_specs=placed,
        out_specs=(P("orb", None, "slab", "pois", None), P("slab", "pois", "orb")),
        check_vma=False,
    )
```

```python
import functools
import math

import jax
import jax.numpy as jnp
import ml_dtypes
import numpy as np
from jax import lax
from jax.experimental import pallas as pl
from jax.experimental.pallas import tpu as pltpu
from jax.sharding import PartitionSpec as P

NX, NY, NZ = 192, 128, 128
SLABS, ORBS, POIS = 4, 8, 4
WX, WY = NX // SLABS, NY // POIS
COMPS = 8
FWD = 13
BACK = 14
DEVICES = SLABS * ORBS * POIS
TRANSPOSE_AXES = ("orb", "pois", "slab")
DT = 0.3
HIGHEST = lax.Precision.HIGHEST
VMEM_LIMIT = 67043328
PITCH = 40
PLANES = WX + 2
PADDED = 8 + (PLANES + 2) * PITCH
GROUP = 25
FIRST = 8 + 2 * PITCH
f32, bf16 = jnp.float32, jnp.bfloat16


def _sines(n):
    k = np.arange(1, n + 1)
    return np.sin(np.pi * ((k[:, None] * k[None, :]) % (2 * (n + 1))) / (n + 1))


def _lam(n):
    return 2.0 - 2.0 * np.cos(np.pi * np.arange(1, n + 1) / (n + 1))


@functools.cache
def _tables():
    sx, sy = _sines(NX), _sines(NY)
    order = np.array([s * WX + 4 * xb + xi for xi in range(4) for s in range(SLABS) for xb in range(WX // 4)])
    padded = np.zeros((SLABS * 64, NX))
    for s in range(SLABS):
        padded[s * 64 : s * 64 + WX] = sx[s * WX : (s + 1) * WX]
    ring_x = np.zeros((16, NX))
    ring_y = np.zeros((16, NY))
    for s in range(SLABS):
        if s > 0:
            ring_x[s] = sx[s * WX - 1]
        if s < SLABS - 1:
            ring_x[8 + s] = sx[(s + 1) * WX]
    for p in range(POIS):
        if p > 0:
            ring_y[p] = sy[p * WY - 1]
        if p < POIS - 1:
            ring_y[8 + p] = sy[(p + 1) * WY]
    back_x = np.concatenate([sx[order], padded, ring_x])
    modes = np.stack([_lam(NZ), sy.sum(1)])
    cast = lambda a: np.asarray(a, np.float32)
    high = cast(sy).astype(ml_dtypes.bfloat16)
    low = (cast(sy) - high.astype(np.float32)).astype(ml_dtypes.bfloat16)
    tiles = [np.arange(128) % (NZ // ORBS) + o * (NZ // ORBS) for o in range(ORBS)]
    stacked = np.concatenate([high, high, low], 0)
    shift = np.eye(NZ, k=1) + np.eye(NZ, k=-1)
    return dict(
        near=shift.astype(ml_dtypes.bfloat16),
        beside=np.concatenate([high, high, low], 1),
        stacked=stacked,
        tiled=np.stack([stacked[:, t] for t in tiles]),
        sy=cast(sy),
        forward_x=cast(sx[:, order]),
        back_x=cast(back_x),
        ring_y=cast(ring_y),
        col=cast(np.stack([_lam(NX), sx.sum(1)] + [np.zeros(NX)] * 6, 1)),
        row=cast(np.stack([_lam(NY), sy.sum(1)] + [np.zeros(NY)] * 6, 0)),
        modes=cast(modes),
    )


_VM = pl.BlockSpec(memory_space=pltpu.VMEM)
_SM = pl.BlockSpec(memory_space=pltpu.SMEM)
_ANY = pl.BlockSpec(memory_space=pl.ANY)
_X_FACE, _Y_FACE, _CORNER = (2, WY, NZ), (2, WX, NZ), (8, NZ)
_FACES = [_X_FACE, _X_FACE, _Y_FACE, _Y_FACE] + [_CORNER] * 4


def _iotas():
    return (
        lax.broadcasted_iota(jnp.int32, (8, 128), 0),
        lax.broadcasted_iota(jnp.int32, (8, 128), 1),
    )


def _zsum(v, lane):
    return jnp.where(lane == 0, 0.0, pltpu.roll(v, 1, 1)) + jnp.where(lane == 127, 0.0, pltpu.roll(v, 127, 1))


def _base(plane):
    return pl.multiple_of(8 + PITCH + PITCH * plane, 8)


def _split(value):
    high = value.astype(bf16)
    return high, (value - high.astype(f32)).astype(bf16)


def _faces_kernel(psi, ext, old, x_left, x_right, y_left, y_right, c_ll, c_lr, c_rl, c_rr, psi_v, pots, rows, sems):
    copies = [pltpu.make_async_copy(psi.at[c], psi_v.at[c], sems.at[c]) for c in range(COMPS)]
    copies += [pltpu.make_async_copy(ref, pots.at[k], sems.at[COMPS + k]) for k, ref in enumerate((ext, old))]
    for copy in copies:
        copy.start()
    for c in range(COMPS):
        copies[c].wait()

        def fill(x, carry, c=c):
            rows[0, pl.ds(pl.multiple_of(8 * x, 8), 8), :] = psi_v[c, x, 0:16, :].astype(f32)[0:8]
            rows[1, pl.ds(pl.multiple_of(8 * x, 8), 8), :] = psi_v[c, x, 16:32, :].astype(f32)[8:16]
            return carry

        lax.fori_loop(0, WX, fill, 0, unroll=8)
        x_left[c] = psi_v[c, 0:2]
        x_right[c] = psi_v[c, WX - 2 : WX]
        for half, ref, first in ((0, y_left, 0), (1, y_right, 6)):
            for d in range(2):
                ref[c, d] = rows[half, pl.ds(first + d, WX, 8), :].astype(bf16)
        for ref, half, y, x in ((c_ll, 0, 0, 0), (c_lr, 1, 7, 0), (c_rl, 0, 0, WX - 1), (c_rr, 1, 7, WX - 1)):
            ref[c] = jnp.broadcast_to(rows[half, pl.ds(8 * x + y, 1), :], (8, 128)).astype(bf16)
    for k in range(2):
        copies[COMPS + k].wait()

        def fill_pot(x, carry, k=k):
            rows[0, pl.ds(pl.multiple_of(8 * x, 8), 8), :] = pots[k, x, 0:8, :]
            rows[1, pl.ds(pl.multiple_of(8 * x, 8), 8), :] = pots[k, x, 24:32, :]
            return carry

        lax.fori_loop(0, WX, fill_pot, 0, unroll=8)
        for ref, value in (
            (x_left, pots[k, 0]),
            (x_right, pots[k, WX - 1]),
            (y_left, rows[0, pl.ds(0, WX, 8), :]),
            (y_right, rows[1, pl.ds(7, WX, 8), :]),
        ):
            ref[COMPS + k, 0], ref[COMPS + k, 1] = _split(value)
        for ref in (c_ll, c_lr, c_rl, c_rr):
            ref[COMPS + k] = jnp.zeros((8, 128), bf16)


def _faces(psi, ext, old):
    return pl.pallas_call(
        _faces_kernel,
        name="faces",
        in_specs=[_ANY] * 3,
        out_specs=[_VM] * len(_FACES),
        out_shape=[jax.ShapeDtypeStruct((COMPS + 2,) + s, bf16) for s in _FACES],
        scratch_shapes=[
            pltpu.VMEM((COMPS, WX, WY, NZ), bf16),
            pltpu.VMEM((2, WX, WY, NZ), f32),
            pltpu.VMEM((2, 8 * WX, 128), f32),
            pltpu.SemaphoreType.DMA((COMPS + 2,)),
        ],
        cost_estimate=pl.CostEstimate(flops=1000000, bytes_accessed=6000000, transcendentals=0),
    )(psi, ext, old)


_SHARED_SCRATCH = (
    [
        pltpu.VMEM((COMPS, (WX + 4) * WY, NZ), bf16),
        pltpu.VMEM((COMPS, PADDED, NZ), f32),
        pltpu.VMEM((COMPS, PADDED, NZ), f32),
        pltpu.VMEM((PLANES * WY, NZ), f32),
        pltpu.VMEM((2, WX, NZ), f32),
        pltpu.VMEM((2, WX * WY, NZ), f32),
    ]
    + [pltpu.VMEM((COMPS + 2,) + s, bf16) for s in _FACES]
    + [pltpu.SemaphoreType.DMA((COMPS + 2 + len(_FACES),))]
)


def _fetch(hbm, scratch):
    psi, ext, old = hbm[:3]
    psi_v, pots, sems = scratch[0], scratch[5], scratch[-1]
    pairs = [(ref, buffer) for ref, buffer in zip(hbm[3:], scratch[6:-1])]
    pairs += [(ext, pots.at[0]), (old, pots.at[1])]
    pairs += [(psi.at[c], psi_v.at[c, pl.ds(2 * WY, WX * WY)]) for c in range(COMPS)]
    copies = [pltpu.make_async_copy(a, b, sems.at[k]) for k, (a, b) in enumerate(pairs)]
    for copy in copies:
        copy.start()
    return copies


def _inside():
    slab, pois = lax.axis_index("slab"), lax.axis_index("pois")
    number = lambda cond: jnp.where(cond, 1.0, 0.0).astype(f32)
    return (
        (number(slab > 0), number(slab < SLABS - 1)),
        (number(pois > 0), number(pois < POIS - 1)),
    )


def _pair(ref, k):
    return ref[k, 0].astype(f32) + ref[k, 1].astype(f32)


def _images(scratch, near, psi_copies):
    psi_v, psi_f, image, pot, ring_y, _ = scratch[:6]
    x_faces, y_faces, corners = scratch[6:8], scratch[8:10], scratch[10:14]
    in_x, in_y = _inside()
    sub, lane = _iotas()
    for c in range(COMPS):
        psi_copies[c].wait()

    def one(c, carry):
        for side in range(2):
            first = (WX + 2) * WY * side
            for d in range(2):
                value = x_faces[side][c, d].astype(f32) * in_x[side]
                psi_v[c, pl.ds(first + WY * d, WY)] = value.astype(bf16)

        def widen(p, carry):
            value = psi_v[c, pl.ds(pl.multiple_of(WY * p, WY), WY)].astype(f32)
            psi_f[c, pl.ds(_base(p - 1), WY)] = value
            return carry

        lax.fori_loop(0, PLANES + 2, widen, 0, unroll=13)
        for side in range(2):
            row = FIRST + (WY if side else -1)
            face = y_faces[side][c, 1 - side].astype(f32) * in_y[side]
            psi_f[c, pl.ds(row, WX, PITCH)] = face
            for i in range(2):
                corner = corners[2 * i + side][c].astype(f32) * (in_x[i] * in_y[side])
                at = FIRST - PITCH + PITCH * (PLANES - 1) * i + (WY if side else -1)
                psi_f[c, pl.ds(at, 1)] = corner[0:1]

        def group(j, carry):
            start = pl.multiple_of(GROUP * WY * j, WY)
            cells = psi_v[c, pl.ds(pl.multiple_of(start + WY, WY), GROUP * WY)]
            sums = jnp.dot(cells, near[...], preferred_element_type=f32)
            for g in range(GROUP):
                base = _base(GROUP * j + g)
                for i in range(4):
                    at = base + 8 * i
                    load = lambda row: psi_f[c, pl.ds(row, 8)]
                    beside = (load(at - 1) + load(at + 1)) + (load(at - PITCH) + load(at + PITCH))
                    first = WY * g + 8 * i
                    weight = pot[pl.ds(pl.multiple_of(start + first, 8), 8)]
                    value = weight * load(pl.multiple_of(at, 8)) - (beside + sums[first : first + 8])
                    image[c, pl.ds(pl.multiple_of(at, 8), 8)] = value
            return carry

        lax.fori_loop(0, PLANES // GROUP, group, 0)
        for i in range(2):
            edge = pl.ds(FIRST - PITCH + PITCH * (PLANES - 1) * i, WY)
            image[c, edge] = image[c, edge] * in_x[i]
        for side in range(2):
            row = FIRST + (WY if side else -1)
            inward = -1 if side else 1
            cells = psi_f[c, pl.ds(row, WX, PITCH)]
            before = psi_f[c, pl.ds(row - PITCH, WX, PITCH)]
            after = psi_f[c, pl.ds(row + PITCH, WX, PITCH)]
            inner = psi_f[c, pl.ds(row + inward, WX, PITCH)]
            outer = y_faces[side][c, side].astype(f32)
            total = (before + after) + (inner + outer)
            value = [
                ring_y[side, 8 * i : 8 * i + 8] * cells[8 * i : 8 * i + 8]
                - (total[8 * i : 8 * i + 8] + _zsum(cells[8 * i : 8 * i + 8], lane))
                for i in range(WX // 8)
            ]
            image[c, pl.ds(row, WX, PITCH)] = jnp.concatenate(value, axis=0) * in_y[side]
        return carry

    lax.fori_loop(0, COMPS, one, 0)


def _stepped(scratch, orbital, x, i, lane):
    psi_f, image, pot = scratch[1], scratch[2], scratch[3]
    at = _base(x + 1) + 8 * i
    weight = pot[pl.ds(pl.multiple_of(WY * (x + 1) + 8 * i, 8), 8)]
    parts = []
    for c in (2 * orbital, 2 * orbital + 1):
        load = lambda row, hint=True: image[c, pl.ds(pl.multiple_of(row, 8) if hint else row, 8)]
        u = load(at)
        total = (load(at - PITCH) + load(at + PITCH)) + (load(at - 1, False) + load(at + 1, False)) + _zsum(u, lane)
        second = weight * u - total
        parts.append((psi_f[c, pl.ds(pl.multiple_of(at, 8), 8)], u, second))
    (a, ua, wa), (b, ub, wb) = parts
    scale = 0.125 * DT * DT
    return (a - scale * wa) + (0.5 * DT) * ub, (b - scale * wb) - (0.5 * DT) * ua


def _charge_kernel(occupations, near, beside, *refs):
    count = 3 + len(_FACES)
    hbm, message, kept = refs[:count], refs[count], refs[count + 1]
    scratch = refs[count + 2 : count + 2 + len(_SHARED_SCRATCH)]
    charge, kept_sems, rows, row_sem = refs[count + 2 + len(_SHARED_SCRATCH) :]
    copies = _fetch(hbm, scratch)
    image, pot, ring_y, pots = scratch[2:6]
    x_faces, y_faces = scratch[6:8], scratch[8:10]
    _, lane = _iotas()
    for copy in copies[:-COMPS]:
        copy.wait()
    pot[pl.ds(WY, WX * WY)] = 6.0 + 2.0 * (pots[0] + pots[1])
    for side in range(2):
        ring_y[side] = 6.0 + 2.0 * (_pair(y_faces[side], COMPS) + _pair(y_faces[side], COMPS + 1))
        edge = pl.ds((WX + 1) * WY * side, WY)
        pot[edge] = 6.0 + 2.0 * (_pair(x_faces[side], COMPS) + _pair(x_faces[side], COMPS + 1))
    _images(scratch, near, copies[-COMPS:])
    out = [pltpu.make_async_copy(image.at[c], kept.at[c], kept_sems.at[c]) for c in range(COMPS)]
    for copy in out:
        copy.start()
    occ = [occupations[k] for k in range(COMPS // 2)]

    def pair(k, totals):
        for d in range(2):
            x = 2 * k + d
            for i in range(4):
                sums = None
                for orbital in range(COMPS // 2):
                    real, imag = _stepped(scratch, orbital, x, i, lane)
                    term = occ[orbital] * (real * real + imag * imag)
                    sums = term if sums is None else sums + term
                charge[pl.ds(pl.multiple_of(WY * x + 8 * i, 8), 8), :] = sums
                totals = totals + sums
        return totals

    totals = lax.fori_loop(0, WX // 2, pair, jnp.zeros((8, 128), f32))
    mean = jnp.broadcast_to(jnp.sum(totals, keepdims=True) / (WX * WY * NZ), (8, 128))

    def group(g, carry):
        cells = charge[pl.ds(pl.multiple_of(128 * g, 128), 128), :] - mean[0:1]
        high, low = _split(cells)
        modes = lax.dot_general(
            beside[...],
            jnp.concatenate([high, low, high], axis=1),
            (((1,), (1,)), ((), ())),
            preferred_element_type=f32,
        )
        for k in range(16):
            rows[pl.ds(8 * FWD * k + g, 8, FWD), :] = modes[8 * k : 8 * k + 8]
        return carry

    lax.fori_loop(0, WX // 4, group, 0, unroll=3)
    for k in range(16):
        rows[pl.ds(8 * FWD * k + FWD - 1, 8, FWD), :] = mean
    send = pltpu.make_async_copy(rows, message, row_sem)
    send.start()
    send.wait()
    for copy in out:
        copy.wait()


def _charge_messages(occupations, *arrays):
    t = _tables()
    return pl.pallas_call(
        _charge_kernel,
        name="charge",
        in_specs=[_SM, _VM, _VM] + [_ANY] * len(arrays),
        out_specs=[_ANY, _ANY],
        out_shape=[
            jax.ShapeDtypeStruct((DEVICES * FWD, 128), f32),
            jax.ShapeDtypeStruct((COMPS, PADDED, NZ), f32),
        ],
        scratch_shapes=_SHARED_SCRATCH
        + [
            pltpu.VMEM((WX * WY, NZ), f32),
            pltpu.SemaphoreType.DMA((COMPS,)),
            pltpu.VMEM((DEVICES * FWD, 128), f32),
            pltpu.SemaphoreType.DMA,
        ],
        compiler_params=pltpu.CompilerParams(vmem_limit_bytes=VMEM_LIMIT),
        cost_estimate=pl.CostEstimate(flops=100000000, bytes_accessed=8000000, transcendentals=0),
    )(occupations, jnp.asarray(t["near"]), jnp.asarray(t["beside"]), *arrays)


def _swap_groups(blocks, group):
    out = []
    for i in range(4):
        value = None
        for j in range(4):
            shift = (32 * (j - i)) % 128
            moved = pltpu.roll(blocks[j], shift, 1) if shift else blocks[j]
            value = moved if value is None else jnp.where(group == j, moved, value)
        out.append(value)
    return out


def _plane_kernel(modes, recv, forward_x, sy, back_x, ring_y, col, row, send, packed, block):
    dot = functools.partial(jnp.dot, precision=HIGHEST, preferred_element_type=f32)
    nt = lambda a, b: lax.dot_general(a, b, (((1,), (1,)), ((), ())), precision=HIGHEST, preferred_element_type=f32)
    kz = (lax.axis_index("orb") * POIS + lax.axis_index("pois")) * SLABS + lax.axis_index("slab")
    lam_z, sum_z = modes[0, kz], modes[1, kz]
    means = recv[pl.ds(FWD - 1, DEVICES, FWD), :]
    blocks = POIS * SLABS
    block_mean = sum(means[blocks * o : blocks * (o + 1)] for o in range(ORBS))
    mean = jnp.sum(block_mean, axis=0, keepdims=True) / blocks
    block_means = [block_mean[k : k + 1] for k in range(blocks)]
    for p in range(POIS):
        for s in range(SLABS):
            total = None
            for o in range(ORBS):
                part = recv[pl.ds(((o * POIS + p) * SLABS + s) * FWD, 12), :]
                total = part if total is None else total + part
            packed[p, pl.ds(12 * s, 12), :] = total + sum_z * (block_means[p * SLABS + s][0:1] - mean)
    group = lax.broadcasted_iota(jnp.int32, (WX, 128), 1) // 32
    plane = jnp.concatenate(_swap_groups([packed[p] for p in range(POIS)], group), axis=0)
    spectrum = dot(dot(forward_x[...], plane), sy[...])
    divisor = col[:, 0:1] + row[0:1, :] + lam_z
    factor = 32.0 * math.pi / ((NX + 1) * (NY + 1) * (NZ + 1))
    scaled = spectrum * factor / divisor
    across = dot(back_x[...], scaled)
    field = dot(across[:NX], sy[...])
    ring = dot(across[NX + 256 :], sy[...])
    cells = _swap_groups([field[WX * i : WX * (i + 1)] for i in range(4)], group)
    lane8 = lax.broadcasted_iota(jnp.int32, (8, 128), 1)
    group8 = lane8 // 32
    faces = [nt(ring_y[...], across[NX + 128 * h : NX + 128 * (h + 1)]) for h in range(2)]
    y_rows = []
    for s in range(SLABS):
        low, high = faces[s // 2][0:8], faces[s // 2][8:16]
        if s % 2 == 0:
            high = pltpu.roll(high, 64, 1)
        else:
            low = pltpu.roll(low, 64, 1)
        y_rows.append(jnp.where(lane8 < 64, low, high))
    for p in range(POIS):
        shift = lambda v, k: pltpu.roll(v, k % 128, 1) if k % 128 else v
        x_rows = jnp.where(
            group8 == 0,
            shift(ring[0:8], -32 * p),
            jnp.where(group8 == 1, shift(ring[8:16], 32 - 32 * p), 0.0),
        )
        for s in range(SLABS):
            base = (p * SLABS + s) * BACK
            block[pl.ds(base, 12), :] = cells[p][12 * s : 12 * s + 12]
            block[pl.ds(base + 12, 1), :] = x_rows[s : s + 1]
            block[pl.ds(base + 13, 1), :] = y_rows[s][p : p + 1]
    count = POIS * SLABS * BACK
    for o in range(ORBS):
        send[pl.ds(o * count, count), :] = block[...]


def _plane(recv):
    t = _tables()
    return pl.pallas_call(
        _plane_kernel,
        name="plane",
        in_specs=[_SM] + [_VM] * 7,
        out_specs=_VM,
        out_shape=jax.ShapeDtypeStruct((DEVICES * BACK, 128), f32),
        scratch_shapes=[
            pltpu.VMEM((POIS, WX, 128), f32),
            pltpu.VMEM((POIS * SLABS * BACK, 128), f32),
        ],
        cost_estimate=pl.CostEstimate(flops=200000000, bytes_accessed=3000000, transcendentals=0),
    )(
        jnp.asarray(t["modes"]),
        recv,
        *(jnp.asarray(t[k]) for k in ("forward_x", "sy", "back_x", "ring_y", "col", "row")),
    )


OUT_GROUP = 8


def _step_kernel(stacked, recv_hbm, tiled_hbm, kept, psi, ext, old, x_low, x_high, y_low, y_high, new, hartree, *scratch):
    psi_v, psi_f, image, pot, change, ring_y, pots, recv, tiled, slices, out = scratch[:11]
    faces, sems, out_sems = scratch[11:15], scratch[15], scratch[16]
    orb = lax.axis_index("orb")
    in_x, in_y = _inside()
    sub, lane = _iotas()
    pairs = [(recv_hbm, recv), (tiled_hbm.at[orb], tiled), (ext, pots.at[0]), (old, pots.at[1])]
    pairs += list(zip((x_low, x_high, y_low, y_high), faces))
    early = len(pairs)
    for c in range(COMPS):
        pairs += [(psi.at[c], psi_v.at[c, pl.ds(WY, WX * WY)]), (kept.at[c], image.at[c])]
    copies = [pltpu.make_async_copy(a, b, sems.at[k]) for k, (a, b) in enumerate(pairs)]
    for copy in copies:
        copy.start()
    for copy in copies[:early]:
        copy.wait()

    def back(r, table):
        high, low = _split(recv[pl.ds(r, 128, BACK), :])
        stack = jnp.concatenate([high, low, high], axis=0)
        return lax.dot_general(stack, table[...], (((0,), (0,)), ((), ())), preferred_element_type=f32)

    def planes(g, carry):
        field = back(g, stacked)
        first = pl.multiple_of(4 * WY * g, 8)
        block = pl.ds(first, 4 * WY)
        moved = pl.ds(pl.multiple_of(first + WY, 8), 4 * WY)
        pot[moved] = 6.0 + (2.0 * pots[0, block] + (pots[1, block] + field))
        change[moved] = field - pots[1, block]
        mine = back(g, tiled)
        for k in range(16):
            kept_lanes = jnp.where(lane // 16 == sub, mine[8 * k : 8 * k + 8], 0.0)
            slices[k % 4, pl.ds(4 * g + k // 4, 1), :] = jnp.sum(kept_lanes, axis=0, keepdims=True)
        return carry

    lax.fori_loop(0, WX // 4, planes, 0, unroll=2)
    x_field, y_field = back(12, stacked), back(13, stacked)
    for side in range(2):
        edge = pl.ds((WX + 1) * WY * side, WY)
        change[edge] = (x_field[32 * side : 32 * side + 32] - _pair(faces[side], COMPS + 1)) * in_x[side]
        ring_y[side] = (y_field[64 * side : 64 * side + WX] - _pair(faces[2 + side], COMPS + 1)) * in_y[side]
    for q in range(4):
        turned = jnp.transpose(slices[q])
        for y in range(8):
            hartree[8 * q + y] = turned[16 * y : 16 * y + 16, 0:WX]

    for c in range(COMPS):
        copies[early + 2 * c].wait()
        copies[early + 2 * c + 1].wait()

    def one(c, carry):
        for side in range(2):
            psi_v[c, pl.ds((WX + 1) * WY * side, WY)] = faces[side][c, 1 - side]

        def planes_of(j, carry):
            for k in range(5):
                p = 5 * j + k
                rows = pl.ds(pl.multiple_of(WY * p, WY), WY)
                value = psi_v[c, rows].astype(f32)
                at = pl.ds(_base(p), WY)
                image[c, at] = image[c, at] + change[rows] * value
                psi_f[c, at] = value
            return carry

        lax.fori_loop(0, PLANES // 5, planes_of, 0)
        for side in range(2):
            at = pl.ds(FIRST + (WY if side else -1), WX, PITCH)
            image[c, at] = image[c, at] + ring_y[side] * faces[2 + side][c, 1 - side].astype(f32)
        return carry

    lax.fori_loop(0, COMPS, one, 0)

    def out_copy(j, c):
        planes = pl.ds(OUT_GROUP * j, OUT_GROUP)
        return pltpu.make_async_copy(out.at[c, planes], new.at[c, planes], out_sems.at[j, c])

    def group(j, carry):
        def pair(k, carry):
            for d in range(2):
                x = OUT_GROUP * j + 2 * k + d
                for i in range(4):
                    for orbital in range(COMPS // 2):
                        real, imag = _stepped((None, psi_f, image, pot), orbital, x, i, lane)
                        out[2 * orbital, x, 8 * i : 8 * i + 8] = real
                        out[2 * orbital + 1, x, 8 * i : 8 * i + 8] = imag
            return carry

        lax.fori_loop(0, OUT_GROUP // 2, pair, 0)
        for c in range(COMPS):
            out_copy(j, c).start()
        return carry

    lax.fori_loop(0, WX // OUT_GROUP, group, 0)
    for j in range(WX // OUT_GROUP):
        for c in range(COMPS):
            out_copy(j, c).wait()


def _step(recv, kept, *arrays):
    t = _tables()
    arrays = arrays[:7]
    return pl.pallas_call(
        _step_kernel,
        name="step",
        in_specs=[_VM, _ANY, _ANY, _ANY] + [_ANY] * len(arrays),
        out_specs=[_ANY, _VM],
        out_shape=[
            jax.ShapeDtypeStruct((COMPS, WX, WY, NZ), f32),
            jax.ShapeDtypeStruct((WY, NZ // ORBS, WX), f32),
        ],
        scratch_shapes=[
            pltpu.VMEM((COMPS, PLANES * WY, NZ), bf16),
            pltpu.VMEM((COMPS, PADDED, NZ), f32),
            pltpu.VMEM((COMPS, PADDED, NZ), f32),
            pltpu.VMEM((PLANES * WY, NZ), f32),
            pltpu.VMEM((PLANES * WY, NZ), f32),
            pltpu.VMEM((2, WX, NZ), f32),
            pltpu.VMEM((2, WX * WY, NZ), f32),
            pltpu.VMEM((DEVICES * BACK, 128), f32),
            pltpu.VMEM((3 * NZ, 128), bf16),
            pltpu.VMEM((4, 128, 128), f32),
            pltpu.VMEM((COMPS, WX, WY, NZ), f32),
        ]
        + [pltpu.VMEM((COMPS + 2,) + s, bf16) for s in _FACES[:4]]
        + [
            pltpu.SemaphoreType.DMA((8 + 2 * COMPS,)),
            pltpu.SemaphoreType.DMA((WX // OUT_GROUP, COMPS)),
        ],
        compiler_params=pltpu.CompilerParams(vmem_limit_bytes=VMEM_LIMIT),
        cost_estimate=pl.CostEstimate(flops=100000000, bytes_accessed=20000000, transcendentals=0),
    )(jnp.asarray(t["stacked"]), recv, jnp.asarray(t["tiled"]), kept, *arrays)


def _exchange(sent):
    x_left, x_right, y_left, y_right, c_ll, c_lr, c_rl, c_rr = sent
    ring = lambda n, d: [(i, (i + d) % n) for i in range(n)]
    y_low = lax.ppermute(y_right, "pois", ring(POIS, 1))
    y_high = lax.ppermute(y_left, "pois", ring(POIS, -1))
    x_low = lax.ppermute(x_right, "slab", ring(SLABS, 1))
    x_high = lax.ppermute(x_left, "slab", ring(SLABS, -1))

    def diagonal(value, ds, dp):
        pairs = [
            (s * POIS + p, (s + ds) % SLABS * POIS + (p + dp) % POIS) for s in range(SLABS) for p in range(POIS)
        ]
        return lax.ppermute(value, ("slab", "pois"), pairs)

    return (
        x_low, x_high, y_low, y_high,
        diagonal(c_rr, 1, 1), diagonal(c_rl, 1, -1), diagonal(c_lr, -1, 1), diagonal(c_ll, -1, -1),
    )


def _swap(messages, rows):
    moved = lax.all_to_all(messages.reshape(DEVICES, 1, rows * 128), TRANSPOSE_AXES, 0, 0)
    return moved.reshape(DEVICES * rows, 128)


def body(orbitals, occupations, ext_pot, hartree_old):
    cells = orbitals.reshape(COMPS, WX, WY, NZ)
    halo = _exchange(_faces(cells, ext_pot, hartree_old))
    flat = lambda a: a.reshape(WX * WY, NZ)
    arrays = (orbitals.reshape(COMPS, WX * WY, NZ), flat(ext_pot), flat(hartree_old), *halo)
    message, kept = _charge_messages(occupations, *arrays)
    new, hartree = _step(_swap(_plane(_swap(message, FWD)), BACK), kept, *arrays)
    return new.reshape(orbitals.shape), jnp.transpose(hartree, (2, 0, 1))


def solution(mesh):
    placed = (P("orb", None, "slab", "pois", None), P("orb"), P("slab", "pois", None), P("slab", "pois", None))
    return jax.shard_map(
        body,
        mesh=mesh,
        in_specs=placed,
        out_specs=(P("orb", None, "slab", "pois", None), P("slab", "pois", "orb")),
        check_vma=False,
    )
```

```python
import functools
import math

import jax
import jax.numpy as jnp
import ml_dtypes
import numpy as np
from jax import lax
from jax.experimental import pallas as pl
from jax.experimental.pallas import tpu as pltpu
from jax.sharding import PartitionSpec as P

NX, NY, NZ = 192, 128, 128
SLABS, ORBS, POIS = 4, 8, 4
WX, WY = NX // SLABS, NY // POIS
COMPS = 8
FWD = 13
BACK = 14
DEVICES = SLABS * ORBS * POIS
TRANSPOSE_AXES = ("orb", "pois", "slab")
DT = 0.3
HIGHEST = lax.Precision.HIGHEST
VMEM_LIMIT = 67043328
PITCH = 40
PLANES = WX + 2
PADDED = 8 + (PLANES + 2) * PITCH
GROUP = 24
HALF = COMPS // 2
FIRST = 8 + 2 * PITCH
f32, bf16 = jnp.float32, jnp.bfloat16


def _sines(n):
    k = np.arange(1, n + 1)
    return np.sin(np.pi * ((k[:, None] * k[None, :]) % (2 * (n + 1))) / (n + 1))


def _lam(n):
    return 2.0 - 2.0 * np.cos(np.pi * np.arange(1, n + 1) / (n + 1))


@functools.cache
def _tables():
    sx, sy = _sines(NX), _sines(NY)
    order = np.array([s * WX + 4 * xb + xi for xi in range(4) for s in range(SLABS) for xb in range(WX // 4)])
    padded = np.zeros((SLABS * 64, NX))
    for s in range(SLABS):
        padded[s * 64 : s * 64 + WX] = sx[s * WX : (s + 1) * WX]
    ring_x = np.zeros((16, NX))
    ring_y = np.zeros((16, NY))
    for s in range(SLABS):
        if s > 0:
            ring_x[s] = sx[s * WX - 1]
        if s < SLABS - 1:
            ring_x[8 + s] = sx[(s + 1) * WX]
    for p in range(POIS):
        if p > 0:
            ring_y[p] = sy[p * WY - 1]
        if p < POIS - 1:
            ring_y[8 + p] = sy[(p + 1) * WY]
    back_x = np.concatenate([sx[order], padded, ring_x])
    modes = np.stack([_lam(NZ), sy.sum(1)])
    cast = lambda a: np.asarray(a, np.float32)
    high = cast(sy).astype(ml_dtypes.bfloat16)
    low = (cast(sy) - high.astype(np.float32)).astype(ml_dtypes.bfloat16)
    tiles = [np.arange(128) % (NZ // ORBS) + o * (NZ // ORBS) for o in range(ORBS)]
    stacked = np.concatenate([high, high, low], 0)
    shift = np.eye(NZ, k=1) + np.eye(NZ, k=-1)
    return dict(
        near=shift.astype(ml_dtypes.bfloat16),
        beside=np.concatenate([high, high, low], 1),
        stacked=stacked,
        tiled=np.stack([stacked[:, t] for t in tiles]),
        sy=cast(sy),
        forward_x=cast(sx[:, order]),
        back_x=cast(back_x),
        ring_y=cast(ring_y),
        col=cast(np.stack([_lam(NX), sx.sum(1)] + [np.zeros(NX)] * 6, 1)),
        row=cast(np.stack([_lam(NY), sy.sum(1)] + [np.zeros(NY)] * 6, 0)),
        modes=cast(modes),
    )


_VM = pl.BlockSpec(memory_space=pltpu.VMEM)
_SM = pl.BlockSpec(memory_space=pltpu.SMEM)
_ANY = pl.BlockSpec(memory_space=pl.ANY)
_HBM = pl.BlockSpec(memory_space=pltpu.HBM)
CORNERS = COMPS + 2
_X_FACE, _Y_FACE = (COMPS + 3, 2, WY, NZ), (COMPS + 2, 2, WX, NZ)
_FACES = [_X_FACE, _X_FACE, _Y_FACE, _Y_FACE]


def _iotas():
    return (
        lax.broadcasted_iota(jnp.int32, (8, 128), 0),
        lax.broadcasted_iota(jnp.int32, (8, 128), 1),
    )


def _zsum(v, lane):
    return jnp.where(lane == 0, 0.0, pltpu.roll(v, 1, 1)) + jnp.where(lane == 127, 0.0, pltpu.roll(v, 127, 1))


def _base(plane):
    return pl.multiple_of(8 + PITCH + PITCH * plane, 8)


def _split(value):
    high = value.astype(bf16)
    return high, (value - high.astype(f32)).astype(bf16)


def _faces_kernel(psi, ext, old, x_left, x_right, y_left, y_right, pots, rows, sems):
    copies = [pltpu.make_async_copy(ref, pots.at[k], sems.at[k]) for k, ref in enumerate((ext, old))]
    for copy in copies:
        copy.start()
    for c in range(COMPS):

        def fill(x, carry, c=c):
            start = pl.multiple_of(WY * x, WY)
            rows[0, pl.ds(pl.multiple_of(8 * x, 8), 8), :] = psi[c, pl.ds(start, 16), :].astype(f32)[0:8]
            rows[1, pl.ds(pl.multiple_of(8 * x, 8), 8), :] = psi[c, pl.ds(start + 16, 16), :].astype(f32)[8:16]
            return carry

        lax.fori_loop(0, WX, fill, 0, unroll=16)
        for d in range(2):
            x_left[c, d] = psi[c, WY * d : WY * (d + 1)]
            x_right[c, d] = psi[c, WY * (WX - 2 + d) : WY * (WX - 1 + d)]
        for half, ref, first in ((0, y_left, 0), (1, y_right, 6)):
            for d in range(2):
                ref[c, d] = rows[half, pl.ds(first + d, WX, 8), :].astype(bf16)
    for k in range(2):
        copies[k].wait()
        for ref, value in (
            (x_left, pots[k, 0:WY]),
            (x_right, pots[k, WY * (WX - 1) : WY * WX]),
            (y_left, pots[k, pl.ds(0, WX, WY), :]),
            (y_right, pots[k, pl.ds(WY - 1, WX, WY), :]),
        ):
            ref[COMPS + k, 0], ref[COMPS + k, 1] = _split(value)


def _faces(psi, ext, old):
    return pl.pallas_call(
        _faces_kernel,
        name="faces",
        in_specs=[_VM, _HBM, _HBM],
        out_specs=[_VM] * 4,
        out_shape=[jax.ShapeDtypeStruct(s, bf16) for s in _FACES],
        scratch_shapes=[
            pltpu.VMEM((2, WX * WY, NZ), f32),
            pltpu.VMEM((2, 8 * WX, 128), f32),
            pltpu.SemaphoreType.DMA((2,)),
        ],
        compiler_params=pltpu.CompilerParams(vmem_limit_bytes=16 * 1024 * 1024),
        cost_estimate=pl.CostEstimate(flops=1000000, bytes_accessed=6000000, transcendentals=0),
    )(psi, ext, old)


def _corners_kernel(x_left, x_right, low_first, low_last, high_first, high_last, left, right, block):
    del x_left, x_right
    for out, refs, row in ((left, (low_first, high_first), 0), (right, (low_last, high_last), 15)):
        for side in range(2):
            for c in range(COMPS):
                block[c : c + 1] = refs[side][c, 0].astype(f32)[row : row + 1]
            out[0, side] = block[...].astype(bf16)


def _corners(x_left, x_right, y_low, y_high):
    entry = pl.BlockSpec((1, 2, WY, NZ), lambda i: (CORNERS, 0, 0, 0))
    rows = lambda near, at: pl.BlockSpec((COMPS, 1, 16, NZ), lambda i: (0, near, at, 0))
    shape = jax.ShapeDtypeStruct(_X_FACE, bf16)
    return pl.pallas_call(
        _corners_kernel,
        name="corners",
        grid=(1,),
        in_specs=[entry, entry, rows(1, 0), rows(1, 2), rows(0, 0), rows(0, 2)],
        out_specs=[entry, entry],
        out_shape=[shape, shape],
        scratch_shapes=[pltpu.VMEM((WY, NZ), f32)],
        input_output_aliases={0: 0, 1: 1},
        cost_estimate=pl.CostEstimate(flops=10000, bytes_accessed=200000, transcendentals=0),
    )(x_left, x_right, y_low, y_low, y_high, y_high)


def _inner_kernel(first_part, near, psi, *refs):
    if first_part == 0:
        ext, old, image, pot, psi_f, pots, sems = refs
        copies = [pltpu.make_async_copy(ref, pots.at[k], sems.at[k]) for k, ref in enumerate((ext, old))]
        for copy in copies:
            copy.start()
    else:
        pot, image, psi_f = refs
    for c in range(HALF):

        def widen(x, carry, c=c):
            rows = pl.ds(pl.multiple_of(WY * x, WY), WY)
            psi_f[c, pl.ds(_base(x + 1), WY)] = psi[first_part + c, rows].astype(f32)
            return carry

        lax.fori_loop(0, WX, widen, 0, unroll=16)
        for side in range(2):
            psi_f[c, pl.ds(FIRST + (WY if side else -1), WX, PITCH)] = jnp.zeros((WX, NZ), f32)
            psi_f[c, pl.ds(FIRST - PITCH + (WX + 1) * PITCH * side, WY)] = jnp.zeros((WY, NZ), f32)
    if first_part == 0:
        for copy in copies:
            copy.wait()
        pot[...] = 6.0 + 2.0 * (pots[0] + pots[1])

    def group(k, carry):
        c, j = k // (WX // GROUP), k % (WX // GROUP)
        start = pl.multiple_of(GROUP * WY * j, WY)
        sums = jnp.dot(
            psi[first_part + c, pl.ds(start, GROUP * WY)], near[...], preferred_element_type=f32
        )
        for g in range(GROUP):
            base = _base(GROUP * j + g + 1)
            for i in range(4):
                at = base + 8 * i
                load = lambda row: psi_f[c, pl.ds(row, 8)]
                beside = (load(at - 1) + load(at + 1)) + (load(at - PITCH) + load(at + PITCH))
                first = WY * g + 8 * i
                weight = pot[pl.ds(pl.multiple_of(start + first, 8), 8)]
                value = weight * load(pl.multiple_of(at, 8)) - (beside + sums[first : first + 8])
                image[c, pl.ds(pl.multiple_of(at, 8), 8)] = value
        return carry

    lax.fori_loop(0, HALF * (WX // GROUP), group, 0)


def _inner(first_part, psi, *arrays):
    image = jax.ShapeDtypeStruct((HALF, PADDED, NZ), f32)
    pot = jax.ShapeDtypeStruct((WX * WY, NZ), f32)
    scratch = [pltpu.VMEM((HALF, PADDED, NZ), f32)]
    if first_part == 0:
        scratch += [pltpu.VMEM((2, WX * WY, NZ), f32), pltpu.SemaphoreType.DMA((2,))]
    return pl.pallas_call(
        functools.partial(_inner_kernel, first_part),
        name="inner",
        in_specs=[_VM, _VM] + ([_HBM, _HBM] if first_part == 0 else [_VM]),
        out_specs=[_VM, _VM] if first_part == 0 else _VM,
        out_shape=[image, pot] if first_part == 0 else image,
        scratch_shapes=scratch,
        compiler_params=pltpu.CompilerParams(vmem_limit_bytes=24 * 1024 * 1024),
        cost_estimate=pl.CostEstimate(flops=400000000, bytes_accessed=12000000, transcendentals=0),
    )(jnp.asarray(_tables()["near"]), psi, *arrays)


def _inside():
    slab, pois = lax.axis_index("slab"), lax.axis_index("pois")
    number = lambda cond: jnp.where(cond, 1.0, 0.0).astype(f32)
    return (
        (number(slab > 0), number(slab < SLABS - 1)),
        (number(pois > 0), number(pois < POIS - 1)),
    )


def _pair(ref, k):
    return ref[k, 0].astype(f32) + ref[k, 1].astype(f32)


def _stepped(cells, images, pot, orbital, at, lane):
    parts = []
    for k in range(2):
        load = lambda row, hint=True: images[k](pl.multiple_of(row, 8) if hint else row)
        u = load(at)
        total = (load(at - PITCH) + load(at + PITCH)) + (load(at - 1, False) + load(at + 1, False)) + _zsum(u, lane)
        parts.append((cells[k], u, pot * u - total))
    (a, ua, wa), (b, ub, wb) = parts
    scale = 0.125 * DT * DT
    return (a - scale * wa) + (0.5 * DT) * ub, (b - scale * wb) - (0.5 * DT) * ua


def _charge_kernel(
    occupations, beside, psi, pot, image_a, image_b, x_low_h, x_high_h, y_low_h, y_high_h, own_low_h, own_high_h,
    message, kept, a, b, x_low, x_high, y_low, y_high, own_low, own_high, column, charge, rows, sems, kept_sems, row_sem,
):
    del image_a, image_b
    pairs = list(zip((x_low_h, x_high_h, y_low_h, y_high_h, own_low_h, own_high_h), (x_low, x_high, y_low, y_high, own_low, own_high)))
    copies = [pltpu.make_async_copy(p, q, sems.at[k]) for k, (p, q) in enumerate(pairs)]
    for copy in copies:
        copy.start()
    for copy in copies:
        copy.wait()
    sub, lane = _iotas()
    in_x, in_y = _inside()
    x_faces, y_faces, own = (x_low, x_high), (y_low, y_high), (own_low, own_high)
    ring_x = [6.0 + 2.0 * (_pair(f, COMPS) + _pair(f, COMPS + 1)) for f in x_faces]
    ring_y = [6.0 + 2.0 * (_pair(f, COMPS) + _pair(f, COMPS + 1)) for f in y_faces]
    corner = [[x_faces[i][CORNERS, j].astype(f32) * (in_x[i] * in_y[j]) for j in range(2)] for i in range(2)]
    for i in range(2):
        for j in range(2):
            column[3 + 2 * i + j, 0:8] = corner[i][j][0:8]
    for half, image in enumerate((a, b)):

        def edges(c, carry, half=half, image=image):
            part = HALF * half + c
            for side in range(2):
                near = x_faces[side][part, 1 - side].astype(f32) * in_x[side]
                far = x_faces[side][part, side].astype(f32)
                inner = psi[part, pl.ds(WY * (WX - 1) * side, WY)].astype(f32)
                at = pl.ds(FIRST + PITCH * (WX - 1) * side, WY)
                image[c, at] = image[c, at] - near
                column[side, 8:40] = near
                column[side, 7:8] = column[3 + 2 * side, pl.ds(part, 1)]
                column[side, 40:41] = column[4 + 2 * side, pl.ds(part, 1)]
                across = column[side, 7:39] + column[side, 9:41]
                total = (far + inner) + across
                for i in range(4):
                    r = slice(8 * i, 8 * i + 8)
                    ring = ring_x[side][r] * near[r] - (total[r] + _zsum(near[r], lane))
                    image[c, pl.ds(FIRST - PITCH + PITCH * (WX + 1) * side + 8 * i, 8)] = ring * in_x[side]
            for side in range(2):
                near = y_faces[side][part, 1 - side].astype(f32) * in_y[side]
                far = y_faces[side][part, side].astype(f32)
                inner = own[side][part, side].astype(f32)
                at = pl.ds(FIRST + (WY - 1) * side, WX, PITCH)
                image[c, at] = image[c, at] - near
                column[2, 8:56] = near
                column[2, 7:8] = column[3 + side, pl.ds(part, 1)]
                column[2, 56:57] = column[5 + side, pl.ds(part, 1)]
                total = (far + inner) + (column[2, 7:55] + column[2, 9:57])
                value = [
                    ring_y[side][r] * near[r] - (total[r] + _zsum(near[r], lane))
                    for r in (slice(8 * i, 8 * i + 8) for i in range(WX // 8))
                ]
                image[c, pl.ds(FIRST + (WY if side else -1), WX, PITCH)] = jnp.concatenate(value, axis=0) * in_y[side]
            return carry

        lax.fori_loop(0, HALF, edges, 0)
    out = [
        pltpu.make_async_copy((a, b)[c // HALF].at[c % HALF], kept.at[c], kept_sems.at[c]) for c in range(COMPS)
    ]
    for copy in out:
        copy.start()
    occ = [occupations[k] for k in range(COMPS // 2)]

    def pair(k, totals):
        for d in range(2):
            x = 2 * k + d
            for h in range(2):
                cells = [psi[c, pl.ds(pl.multiple_of(WY * x + 16 * h, 16), 16)].astype(f32) for c in range(COMPS)]
                for i in (2 * h, 2 * h + 1):
                    r = slice(8 * (i % 2), 8 * (i % 2) + 8)
                    row = pl.ds(pl.multiple_of(WY * x + 8 * i, 8), 8)
                    weight = pot[row]
                    sums = None
                    for orbital in range(COMPS // 2):
                        picked = [
                            lambda at, c=c: (a, b)[c // HALF][c % HALF, pl.ds(at, 8)]
                            for c in (2 * orbital, 2 * orbital + 1)
                        ]
                        own_cells = (cells[2 * orbital][r], cells[2 * orbital + 1][r])
                        real, imag = _stepped(own_cells, picked, weight, orbital, _base(x + 1) + 8 * i, lane)
                        term = occ[orbital] * (real * real + imag * imag)
                        sums = term if sums is None else sums + term
                    charge[row, :] = sums
                    totals = totals + sums
        return totals

    totals = lax.fori_loop(0, WX // 2, pair, jnp.zeros((8, 128), f32))
    mean = jnp.broadcast_to(jnp.sum(totals, keepdims=True) / (WX * WY * NZ), (8, 128))

    def group(g, carry):
        cells = charge[pl.ds(pl.multiple_of(128 * g, 128), 128), :] - mean[0:1]
        high, low = _split(cells)
        modes = lax.dot_general(
            beside[...],
            jnp.concatenate([high, low, high], axis=1),
            (((1,), (1,)), ((), ())),
            preferred_element_type=f32,
        )
        for k in range(16):
            rows[pl.ds(8 * FWD * k + g, 8, FWD), :] = modes[8 * k : 8 * k + 8]
        return carry

    lax.fori_loop(0, WX // 4, group, 0, unroll=3)
    for k in range(16):
        rows[pl.ds(8 * FWD * k + FWD - 1, 8, FWD), :] = mean
    send = pltpu.make_async_copy(rows, message, row_sem)
    send.start()
    send.wait()
    for copy in out:
        copy.wait()


def _charge_messages(occupations, psi, pot, image_a, image_b, *faces):
    t = _tables()
    half = jax.ShapeDtypeStruct((HALF, PADDED, NZ), f32)
    shapes = _FACES + [_Y_FACE] * 2
    return pl.pallas_call(
        _charge_kernel,
        name="charge",
        in_specs=[_SM] + [_VM] * 5 + [_HBM] * len(faces),
        out_specs=[_HBM, _HBM, _VM, _VM],
        out_shape=[
            jax.ShapeDtypeStruct((DEVICES * FWD, 128), f32),
            jax.ShapeDtypeStruct((COMPS, PADDED, NZ), f32),
            half,
            half,
        ],
        scratch_shapes=[pltpu.VMEM(s, bf16) for s in shapes]
        + [
            pltpu.VMEM((7, 64, NZ), f32),
            pltpu.VMEM((WX * WY, NZ), f32),
            pltpu.VMEM((DEVICES * FWD, 128), f32),
            pltpu.SemaphoreType.DMA((len(shapes),)),
            pltpu.SemaphoreType.DMA((COMPS,)),
            pltpu.SemaphoreType.DMA,
        ],
        input_output_aliases={4: 2, 5: 3},
        compiler_params=pltpu.CompilerParams(vmem_limit_bytes=32 * 1024 * 1024),
        cost_estimate=pl.CostEstimate(flops=100000000, bytes_accessed=8000000, transcendentals=0),
    )(occupations, jnp.asarray(t["beside"]), psi, pot, image_a, image_b, *faces)[:2]


def _swap_groups(blocks, group):
    out = []
    for i in range(4):
        value = None
        for j in range(4):
            shift = (32 * (j - i)) % 128
            moved = pltpu.roll(blocks[j], shift, 1) if shift else blocks[j]
            value = moved if value is None else jnp.where(group == j, moved, value)
        out.append(value)
    return out


def _plane_kernel(modes, recv, forward_x, sy, back_x, ring_y, col, row, send, packed, block):
    dot = functools.partial(jnp.dot, precision=HIGHEST, preferred_element_type=f32)
    nt = lambda a, b: lax.dot_general(a, b, (((1,), (1,)), ((), ())), precision=HIGHEST, preferred_element_type=f32)
    kz = (lax.axis_index("orb") * POIS + lax.axis_index("pois")) * SLABS + lax.axis_index("slab")
    lam_z, sum_z = modes[0, kz], modes[1, kz]
    means = recv[pl.ds(FWD - 1, DEVICES, FWD), :]
    blocks = POIS * SLABS
    block_mean = sum(means[blocks * o : blocks * (o + 1)] for o in range(ORBS))
    mean = jnp.sum(block_mean, axis=0, keepdims=True) / blocks
    block_means = [block_mean[k : k + 1] for k in range(blocks)]
    for p in range(POIS):
        for s in range(SLABS):
            total = None
            for o in range(ORBS):
                part = recv[pl.ds(((o * POIS + p) * SLABS + s) * FWD, 12), :]
                total = part if total is None else total + part
            packed[p, pl.ds(12 * s, 12), :] = total + sum_z * (block_means[p * SLABS + s][0:1] - mean)
    group = lax.broadcasted_iota(jnp.int32, (WX, 128), 1) // 32
    plane = jnp.concatenate(_swap_groups([packed[p] for p in range(POIS)], group), axis=0)
    spectrum = dot(dot(forward_x[...], plane), sy[...])
    divisor = col[:, 0:1] + row[0:1, :] + lam_z
    factor = 32.0 * math.pi / ((NX + 1) * (NY + 1) * (NZ + 1))
    scaled = spectrum * factor / divisor
    across = dot(back_x[...], scaled)
    field = dot(across[:NX], sy[...])
    ring = dot(across[NX + 256 :], sy[...])
    cells = _swap_groups([field[WX * i : WX * (i + 1)] for i in range(4)], group)
    lane8 = lax.broadcasted_iota(jnp.int32, (8, 128), 1)
    group8 = lane8 // 32
    faces = [nt(ring_y[...], across[NX + 128 * h : NX + 128 * (h + 1)]) for h in range(2)]
    y_rows = []
    for s in range(SLABS):
        low, high = faces[s // 2][0:8], faces[s // 2][8:16]
        if s % 2 == 0:
            high = pltpu.roll(high, 64, 1)
        else:
            low = pltpu.roll(low, 64, 1)
        y_rows.append(jnp.where(lane8 < 64, low, high))
    for p in range(POIS):
        shift = lambda v, k: pltpu.roll(v, k % 128, 1) if k % 128 else v
        x_rows = jnp.where(
            group8 == 0,
            shift(ring[0:8], -32 * p),
            jnp.where(group8 == 1, shift(ring[8:16], 32 - 32 * p), 0.0),
        )
        for s in range(SLABS):
            base = (p * SLABS + s) * BACK
            block[pl.ds(base, 12), :] = cells[p][12 * s : 12 * s + 12]
            block[pl.ds(base + 12, 1), :] = x_rows[s : s + 1]
            block[pl.ds(base + 13, 1), :] = y_rows[s][p : p + 1]
    count = POIS * SLABS * BACK
    for o in range(ORBS):
        send[pl.ds(o * count, count), :] = block[...]


def _plane(recv):
    t = _tables()
    return pl.pallas_call(
        _plane_kernel,
        name="plane",
        in_specs=[_SM] + [_VM] * 7,
        out_specs=_VM,
        out_shape=jax.ShapeDtypeStruct((DEVICES * BACK, 128), f32),
        scratch_shapes=[
            pltpu.VMEM((POIS, WX, 128), f32),
            pltpu.VMEM((POIS * SLABS * BACK, 128), f32),
        ],
        cost_estimate=pl.CostEstimate(flops=200000000, bytes_accessed=3000000, transcendentals=0),
    )(
        jnp.asarray(t["modes"]),
        recv,
        *(jnp.asarray(t[k]) for k in ("forward_x", "sy", "back_x", "ring_y", "col", "row")),
    )


OUT_GROUP = 8


def _step_kernel(stacked, recv_hbm, tiled_hbm, kept, psi, ext, old, x_low, x_high, y_low, y_high, new, hartree, *scratch):
    psi_v, psi_f, image, pot, change, ring_y, pots, recv, tiled, slices, out = scratch[:11]
    faces, sems, out_sems = scratch[11:15], scratch[15], scratch[16]
    orb = lax.axis_index("orb")
    in_x, in_y = _inside()
    sub, lane = _iotas()
    pairs = [(recv_hbm, recv), (tiled_hbm.at[orb], tiled), (ext, pots.at[0]), (old, pots.at[1])]
    pairs += list(zip((x_low, x_high, y_low, y_high), faces))
    early = len(pairs)
    for c in range(COMPS):
        pairs += [(psi.at[c], psi_v.at[c, pl.ds(WY, WX * WY)]), (kept.at[c], image.at[c])]
    copies = [pltpu.make_async_copy(a, b, sems.at[k]) for k, (a, b) in enumerate(pairs)]
    for copy in copies:
        copy.start()
    for copy in copies[:early]:
        copy.wait()

    def back(r, table):
        high, low = _split(recv[pl.ds(r, 128, BACK), :])
        stack = jnp.concatenate([high, low, high], axis=0)
        return lax.dot_general(stack, table[...], (((0,), (0,)), ((), ())), preferred_element_type=f32)

    def planes(g, carry):
        field = back(g, stacked)
        first = pl.multiple_of(4 * WY * g, 8)
        block = pl.ds(first, 4 * WY)
        moved = pl.ds(pl.multiple_of(first + WY, 8), 4 * WY)
        pot[moved] = 6.0 + (2.0 * pots[0, block] + (pots[1, block] + field))
        change[moved] = field - pots[1, block]
        mine = back(g, tiled)
        for k in range(16):
            kept_lanes = jnp.where(lane // 16 == sub, mine[8 * k : 8 * k + 8], 0.0)
            slices[k % 4, pl.ds(4 * g + k // 4, 1), :] = jnp.sum(kept_lanes, axis=0, keepdims=True)
        return carry

    lax.fori_loop(0, WX // 4, planes, 0, unroll=2)
    x_field, y_field = back(12, stacked), back(13, stacked)
    for side in range(2):
        edge = pl.ds((WX + 1) * WY * side, WY)
        change[edge] = (x_field[32 * side : 32 * side + 32] - _pair(faces[side], COMPS + 1)) * in_x[side]
        ring_y[side] = (y_field[64 * side : 64 * side + WX] - _pair(faces[2 + side], COMPS + 1)) * in_y[side]
    for q in range(4):
        turned = jnp.transpose(slices[q])
        for y in range(8):
            hartree[8 * q + y] = turned[16 * y : 16 * y + 16, 0:WX]

    for c in range(COMPS):
        copies[early + 2 * c].wait()
        copies[early + 2 * c + 1].wait()

    def one(c, carry):
        for side in range(2):
            psi_v[c, pl.ds((WX + 1) * WY * side, WY)] = faces[side][c, 1 - side]

        def planes_of(j, carry):
            for k in range(5):
                p = 5 * j + k
                rows = pl.ds(pl.multiple_of(WY * p, WY), WY)
                value = psi_v[c, rows].astype(f32)
                at = pl.ds(_base(p), WY)
                image[c, at] = image[c, at] + change[rows] * value
                psi_f[c, at] = value
            return carry

        lax.fori_loop(0, PLANES // 5, planes_of, 0)
        for side in range(2):
            at = pl.ds(FIRST + (WY if side else -1), WX, PITCH)
            image[c, at] = image[c, at] + ring_y[side] * faces[2 + side][c, 1 - side].astype(f32)
        return carry

    lax.fori_loop(0, COMPS, one, 0)

    def out_copy(j, c):
        planes = pl.ds(OUT_GROUP * j, OUT_GROUP)
        return pltpu.make_async_copy(out.at[c, planes], new.at[c, planes], out_sems.at[j, c])

    def group(j, carry):
        def pair(k, carry):
            for d in range(2):
                x = OUT_GROUP * j + 2 * k + d
                for i in range(4):
                    at = _base(x + 1) + 8 * i
                    weight = pot[pl.ds(pl.multiple_of(WY * (x + 1) + 8 * i, 8), 8)]
                    for orbital in range(COMPS // 2):
                        parts = (2 * orbital, 2 * orbital + 1)
                        cells = [psi_f[c, pl.ds(pl.multiple_of(at, 8), 8)] for c in parts]
                        picked = [lambda row, c=c: image[c, pl.ds(row, 8)] for c in parts]
                        real, imag = _stepped(cells, picked, weight, orbital, at, lane)
                        out[2 * orbital, x, 8 * i : 8 * i + 8] = real
                        out[2 * orbital + 1, x, 8 * i : 8 * i + 8] = imag
            return carry

        lax.fori_loop(0, OUT_GROUP // 2, pair, 0)
        for c in range(COMPS):
            out_copy(j, c).start()
        return carry

    lax.fori_loop(0, WX // OUT_GROUP, group, 0)
    for j in range(WX // OUT_GROUP):
        for c in range(COMPS):
            out_copy(j, c).wait()


def _step(recv, kept, *arrays):
    t = _tables()
    return pl.pallas_call(
        _step_kernel,
        name="step",
        in_specs=[_VM, _HBM, _HBM, _HBM] + [_HBM] * len(arrays),
        out_specs=[_HBM, _VM],
        out_shape=[
            jax.ShapeDtypeStruct((COMPS, WX, WY, NZ), f32),
            jax.ShapeDtypeStruct((WY, NZ // ORBS, WX), f32),
        ],
        scratch_shapes=[
            pltpu.VMEM((COMPS, PLANES * WY, NZ), bf16),
            pltpu.VMEM((COMPS, PADDED, NZ), f32),
            pltpu.VMEM((COMPS, PADDED, NZ), f32),
            pltpu.VMEM((PLANES * WY, NZ), f32),
            pltpu.VMEM((PLANES * WY, NZ), f32),
            pltpu.VMEM((2, WX, NZ), f32),
            pltpu.VMEM((2, WX * WY, NZ), f32),
            pltpu.VMEM((DEVICES * BACK, 128), f32),
            pltpu.VMEM((3 * NZ, 128), bf16),
            pltpu.VMEM((4, 128, 128), f32),
            pltpu.VMEM((COMPS, WX, WY, NZ), f32),
        ]
        + [pltpu.VMEM(s, bf16) for s in _FACES]
        + [
            pltpu.SemaphoreType.DMA((8 + 2 * COMPS,)),
            pltpu.SemaphoreType.DMA((WX // OUT_GROUP, COMPS)),
        ],
        compiler_params=pltpu.CompilerParams(vmem_limit_bytes=VMEM_LIMIT),
        cost_estimate=pl.CostEstimate(flops=100000000, bytes_accessed=20000000, transcendentals=0),
    )(jnp.asarray(t["stacked"]), recv, jnp.asarray(t["tiled"]), kept, *arrays)


def _shifted(value, axis, count, step):
    return lax.ppermute(value, axis, [(i, (i + step) % count) for i in range(count)])


def _swap(messages, rows):
    moved = lax.all_to_all(messages.reshape(DEVICES, 1, rows * 128), TRANSPOSE_AXES, 0, 0)
    return moved.reshape(DEVICES * rows, 128)


def body(orbitals, occupations, ext_pot, hartree_old):
    psi = orbitals.reshape(COMPS, WX * WY, NZ)
    ext, old = ext_pot.reshape(WX * WY, NZ), hartree_old.reshape(WX * WY, NZ)
    x_left, x_right, y_left, y_right = _faces(psi, ext, old)
    y_low = _shifted(y_right, "pois", POIS, 1)
    y_high = _shifted(y_left, "pois", POIS, -1)
    image_a, pot = _inner(0, psi, ext, old)
    x_left, x_right = _corners(x_left, x_right, y_low, y_high)
    x_low = _shifted(x_right, "slab", SLABS, 1)
    x_high = _shifted(x_left, "slab", SLABS, -1)
    image_b = _inner(HALF, psi, pot)
    faces = (x_low, x_high, y_low, y_high)
    message, kept = _charge_messages(occupations, psi, pot, image_a, image_b, *faces, y_left, y_right)
    back = _swap(_plane(_swap(message, FWD)), BACK)
    new, hartree = _step(back, kept, psi, ext, old, *faces)
    return new.reshape(orbitals.shape), jnp.transpose(hartree, (2, 0, 1))


def solution(mesh):
    placed = (P("orb", None, "slab", "pois", None), P("orb"), P("slab", "pois", None), P("slab", "pois", None))
    return jax.shard_map(
        body,
        mesh=mesh,
        in_specs=placed,
        out_specs=(P("orb", None, "slab", "pois", None), P("slab", "pois", "orb")),
        check_vma=False,
    )
```

```python
import functools
import math

import jax
import jax.numpy as jnp
import ml_dtypes
import numpy as np
from jax import lax
from jax.experimental import pallas as pl
from jax.experimental.pallas import tpu as pltpu
from jax.sharding import PartitionSpec as P

NX, NY, NZ = 192, 128, 128
SLABS, ORBS, POIS = 4, 8, 4
WX, WY = NX // SLABS, NY // POIS
COMPS = 8
FWD = 13
BACK = 14
DEVICES = SLABS * ORBS * POIS
TRANSPOSE_AXES = ("orb", "pois", "slab")
DT = 0.3
HIGHEST = lax.Precision.HIGHEST
VMEM_LIMIT = 67043328

PITCH = 40
PLANES = WX + 2
PADDED = 8 + (PLANES + 2) * PITCH
GROUP = 24
HALF = COMPS // 2
FIRST = 8 + 2 * PITCH
f32, bf16 = jnp.float32, jnp.bfloat16


def _sines(n):
    k = np.arange(1, n + 1)
    return np.sin(np.pi * ((k[:, None] * k[None, :]) % (2 * (n + 1))) / (n + 1))


def _lam(n):
    return 2.0 - 2.0 * np.cos(np.pi * np.arange(1, n + 1) / (n + 1))


@functools.cache
def _tables():
    sx, sy = _sines(NX), _sines(NY)
    order = np.array([s * WX + 4 * xb + xi for xi in range(4) for s in range(SLABS) for xb in range(WX // 4)])
    padded = np.zeros((SLABS * 64, NX))
    for s in range(SLABS):
        padded[s * 64 : s * 64 + WX] = sx[s * WX : (s + 1) * WX]
    ring_x = np.zeros((16, NX))
    ring_y = np.zeros((16, NY))
    for s in range(SLABS):
        if s > 0:
            ring_x[s] = sx[s * WX - 1]
        if s < SLABS - 1:
            ring_x[8 + s] = sx[(s + 1) * WX]
    for p in range(POIS):
        if p > 0:
            ring_y[p] = sy[p * WY - 1]
        if p < POIS - 1:
            ring_y[8 + p] = sy[(p + 1) * WY]
    back_x = np.concatenate([sx[order], padded, ring_x])
    modes = np.stack([_lam(NZ), sy.sum(1)])
    cast = lambda a: np.asarray(a, np.float32)
    high = cast(sy).astype(ml_dtypes.bfloat16)
    low = (cast(sy) - high.astype(np.float32)).astype(ml_dtypes.bfloat16)
    tiles = [np.arange(128) % (NZ // ORBS) + o * (NZ // ORBS) for o in range(ORBS)]
    stacked = np.concatenate([high, high, low], 0)
    shift = np.eye(NZ, k=1) + np.eye(NZ, k=-1)
    return dict(
        near=shift.astype(ml_dtypes.bfloat16),
        beside=np.concatenate([high, high, low], 1),
        stacked=stacked,
        tiled=np.stack([stacked[:, t] for t in tiles]),
        sy=cast(sy),
        forward_x=cast(sx[:, order]),
        back_x=cast(back_x),
        ring_y=cast(ring_y),
        col=cast(np.stack([_lam(NX), sx.sum(1)] + [np.zeros(NX)] * 6, 1)),
        row=cast(np.stack([_lam(NY), sy.sum(1)] + [np.zeros(NY)] * 6, 0)),
        modes=cast(modes),
    )


_VM = pl.BlockSpec(memory_space=pltpu.VMEM)
_SM = pl.BlockSpec(memory_space=pltpu.SMEM)
_ANY = pl.BlockSpec(memory_space=pl.ANY)
_HBM = pl.BlockSpec(memory_space=pltpu.HBM)
CORNERS = COMPS + 2
_X_FACE, _Y_FACE = (COMPS + 3, 2, WY, NZ), (COMPS + 2, 2, WX, NZ)
_FACES = [_X_FACE, _X_FACE, _Y_FACE, _Y_FACE]


def _iotas():
    return (
        lax.broadcasted_iota(jnp.int32, (8, 128), 0),
        lax.broadcasted_iota(jnp.int32, (8, 128), 1),
    )


def _zsum(v, lane):
    return jnp.where(lane == 0, 0.0, pltpu.roll(v, 1, 1)) + jnp.where(lane == 127, 0.0, pltpu.roll(v, 127, 1))


def _base(plane):
    return pl.multiple_of(8 + PITCH + PITCH * plane, 8)


def _split(value):
    high = value.astype(bf16)
    return high, (value - high.astype(f32)).astype(bf16)


def _faces_kernel(psi_hbm, ext, old, x_left, x_right, y_left, y_right, pot, psi, pots, rows, sems):
    copies = [pltpu.make_async_copy(psi_hbm.at[c], psi.at[c], sems.at[2 + c]) for c in range(COMPS)]
    copies = [pltpu.make_async_copy(ref, pots.at[k], sems.at[k]) for k, ref in enumerate((ext, old))] + copies
    for copy in copies:
        copy.start()
    for c in range(COMPS):
        copies[2 + c].wait()

        def fill(x, carry, c=c):
            start = pl.multiple_of(WY * x, WY)
            rows[0, pl.ds(pl.multiple_of(8 * x, 8), 8), :] = psi[c, pl.ds(start, 16), :].astype(f32)[0:8]
            rows[1, pl.ds(pl.multiple_of(8 * x, 8), 8), :] = psi[c, pl.ds(start + 16, 16), :].astype(f32)[8:16]
            return carry

        lax.fori_loop(0, WX, fill, 0, unroll=16)
        for d in range(2):
            x_left[c, d] = psi[c, WY * d : WY * (d + 1)]
            x_right[c, d] = psi[c, WY * (WX - 2 + d) : WY * (WX - 1 + d)]
        for half, ref, first in ((0, y_left, 0), (1, y_right, 6)):
            for d in range(2):
                ref[c, d] = rows[half, pl.ds(first + d, WX, 8), :].astype(bf16)
    for k in range(2):
        copies[k].wait()
        for ref, value in (
            (x_left, pots[k, 0:WY]),
            (x_right, pots[k, WY * (WX - 1) : WY * WX]),
            (y_left, pots[k, pl.ds(0, WX, WY), :]),
            (y_right, pots[k, pl.ds(WY - 1, WX, WY), :]),
        ):
            ref[COMPS + k, 0], ref[COMPS + k, 1] = _split(value)
    pot[...] = 6.0 + 2.0 * (pots[0] + pots[1])


def _faces(psi, ext, old):
    return pl.pallas_call(
        _faces_kernel,
        name="faces",
        in_specs=[_HBM] * 3,
        out_specs=[_VM] * 5,
        out_shape=[jax.ShapeDtypeStruct(s, bf16) for s in _FACES] + [jax.ShapeDtypeStruct((WX * WY, NZ), f32)],
        scratch_shapes=[
            pltpu.VMEM((COMPS, WX * WY, NZ), bf16),
            pltpu.VMEM((2, WX * WY, NZ), f32),
            pltpu.VMEM((2, 8 * WX, 128), f32),
            pltpu.SemaphoreType.DMA((2 + COMPS,)),
        ],
        compiler_params=pltpu.CompilerParams(vmem_limit_bytes=VMEM_LIMIT),
        cost_estimate=pl.CostEstimate(flops=1000000, bytes_accessed=6000000, transcendentals=0),
    )(psi, ext, old)


def _corners_kernel(x_left, x_right, low_first, low_last, high_first, high_last, after, left, right, block):
    del x_left, x_right, after
    for out, refs, row in ((left, (low_first, high_first), 0), (right, (low_last, high_last), 15)):
        for side in range(2):
            for c in range(COMPS):
                block[c : c + 1] = refs[side][c, 0].astype(f32)[row : row + 1]
            out[0, side] = block[...].astype(bf16)


def _corners(x_left, x_right, y_low, y_high, after):
    entry = pl.BlockSpec((1, 2, WY, NZ), lambda i: (CORNERS, 0, 0, 0))
    rows = lambda near, at: pl.BlockSpec((COMPS, 1, 16, NZ), lambda i: (0, near, at, 0))
    shape = jax.ShapeDtypeStruct(_X_FACE, bf16)
    return pl.pallas_call(
        _corners_kernel,
        name="corners",
        grid=(1,),
        in_specs=[entry, entry, rows(1, 0), rows(1, 2), rows(0, 0), rows(0, 2), _ANY],
        out_specs=[entry, entry],
        out_shape=[shape, shape],
        scratch_shapes=[pltpu.VMEM((WY, NZ), f32)],
        input_output_aliases={0: 0, 1: 1},
        cost_estimate=pl.CostEstimate(flops=10000, bytes_accessed=200000, transcendentals=0),
    )(x_left, x_right, y_low, y_low, y_high, y_high, after)


def _inner_kernel(first_part, near, psi, pot, image, token, psi_f):
    token[...] = jnp.zeros((8, NZ), f32)
    for c in range(HALF):

        def widen(x, carry, c=c):
            rows = pl.ds(pl.multiple_of(WY * x, WY), WY)
            psi_f[c, pl.ds(_base(x + 1), WY)] = psi[first_part + c, rows].astype(f32)
            return carry

        lax.fori_loop(0, WX, widen, 0, unroll=16)
        for side in range(2):
            psi_f[c, pl.ds(FIRST + (WY if side else -1), WX, PITCH)] = jnp.zeros((WX, NZ), f32)
            psi_f[c, pl.ds(FIRST - PITCH + (WX + 1) * PITCH * side, WY)] = jnp.zeros((WY, NZ), f32)

    def group(k, carry):
        c, j = k // (WX // GROUP), k % (WX // GROUP)
        start = pl.multiple_of(GROUP * WY * j, WY)
        sums = jnp.dot(
            psi[first_part + c, pl.ds(start, GROUP * WY)], near[...], preferred_element_type=f32
        )
        for g in range(GROUP):
            base = _base(GROUP * j + g + 1)
            for i in range(4):
                at = base + 8 * i
                load = lambda row: psi_f[c, pl.ds(row, 8)]
                beside = (load(at - 1) + load(at + 1)) + (load(at - PITCH) + load(at + PITCH))
                first = WY * g + 8 * i
                weight = pot[pl.ds(pl.multiple_of(start + first, 8), 8)]
                value = weight * load(pl.multiple_of(at, 8)) - (beside + sums[first : first + 8])
                image[c, pl.ds(pl.multiple_of(at, 8), 8)] = value
        return carry

    lax.fori_loop(0, HALF * (WX // GROUP), group, 0)


def _inner(first_part, psi, pot):
    return pl.pallas_call(
        functools.partial(_inner_kernel, first_part),
        name="inner",
        in_specs=[_VM] * 3,
        out_specs=[_VM, _VM],
        out_shape=[jax.ShapeDtypeStruct((HALF, PADDED, NZ), f32), jax.ShapeDtypeStruct((8, NZ), f32)],
        scratch_shapes=[pltpu.VMEM((HALF, PADDED, NZ), f32)],
        compiler_params=pltpu.CompilerParams(vmem_limit_bytes=24 * 1024 * 1024),
        cost_estimate=pl.CostEstimate(flops=400000000, bytes_accessed=12000000, transcendentals=0),
    )(jnp.asarray(_tables()["near"]), psi, pot)


def _inside():
    slab, pois = lax.axis_index("slab"), lax.axis_index("pois")
    number = lambda cond: jnp.where(cond, 1.0, 0.0).astype(f32)
    return (
        (number(slab > 0), number(slab < SLABS - 1)),
        (number(pois > 0), number(pois < POIS - 1)),
    )


def _pair(ref, k):
    return ref[k, 0].astype(f32) + ref[k, 1].astype(f32)


def _stepped(cells, images, pot, orbital, at, lane):
    parts = []
    for k in range(2):
        load = lambda row, hint=True: images[k](pl.multiple_of(row, 8) if hint else row)
        u = load(at)
        total = (load(at - PITCH) + load(at + PITCH)) + (load(at - 1, False) + load(at + 1, False)) + _zsum(u, lane)
        parts.append((cells[k], u, pot * u - total))
    (a, ua, wa), (b, ub, wb) = parts
    scale = 0.125 * DT * DT
    return (a - scale * wa) + (0.5 * DT) * ub, (b - scale * wb) - (0.5 * DT) * ua


def _charge_kernel(
    occupations, beside, psi, pot, image_a, image_b, x_low_h, x_high_h, y_low_h, y_high_h, own_low_h, own_high_h,
    message, kept, a, b, x_low, x_high, y_low, y_high, own_low, own_high, column, charge, rows, sems, kept_sems, row_sem,
):
    del image_a, image_b
    pairs = list(zip((x_low_h, x_high_h, y_low_h, y_high_h, own_low_h, own_high_h), (x_low, x_high, y_low, y_high, own_low, own_high)))
    copies = [pltpu.make_async_copy(p, q, sems.at[k]) for k, (p, q) in enumerate(pairs)]
    for copy in copies:
        copy.start()
    for copy in copies:
        copy.wait()
    sub, lane = _iotas()
    in_x, in_y = _inside()
    x_faces, y_faces, own = (x_low, x_high), (y_low, y_high), (own_low, own_high)
    ring_x = [6.0 + 2.0 * (_pair(f, COMPS) + _pair(f, COMPS + 1)) for f in x_faces]
    ring_y = [6.0 + 2.0 * (_pair(f, COMPS) + _pair(f, COMPS + 1)) for f in y_faces]
    corner = [[x_faces[i][CORNERS, j].astype(f32) * (in_x[i] * in_y[j]) for j in range(2)] for i in range(2)]
    for i in range(2):
        for j in range(2):
            column[3 + 2 * i + j, 0:8] = corner[i][j][0:8]
    for half, image in enumerate((a, b)):

        def edges(c, carry, half=half, image=image):
            part = HALF * half + c
            for side in range(2):
                near = x_faces[side][part, 1 - side].astype(f32) * in_x[side]
                far = x_faces[side][part, side].astype(f32)
                inner = psi[part, pl.ds(WY * (WX - 1) * side, WY)].astype(f32)
                at = pl.ds(FIRST + PITCH * (WX - 1) * side, WY)
                image[c, at] = image[c, at] - near
                column[side, 8:40] = near
                column[side, 7:8] = column[3 + 2 * side, pl.ds(part, 1)]
                column[side, 40:41] = column[4 + 2 * side, pl.ds(part, 1)]
                across = column[side, 7:39] + column[side, 9:41]
                total = (far + inner) + across
                for i in range(4):
                    r = slice(8 * i, 8 * i + 8)
                    ring = ring_x[side][r] * near[r] - (total[r] + _zsum(near[r], lane))
                    image[c, pl.ds(FIRST - PITCH + PITCH * (WX + 1) * side + 8 * i, 8)] = ring * in_x[side]
            for side in range(2):
                near = y_faces[side][part, 1 - side].astype(f32) * in_y[side]
                far = y_faces[side][part, side].astype(f32)
                inner = own[side][part, side].astype(f32)
                at = pl.ds(FIRST + (WY - 1) * side, WX, PITCH)
                image[c, at] = image[c, at] - near
                column[2, 8:56] = near
                column[2, 7:8] = column[3 + side, pl.ds(part, 1)]
                column[2, 56:57] = column[5 + side, pl.ds(part, 1)]
                total = (far + inner) + (column[2, 7:55] + column[2, 9:57])
                value = [
                    ring_y[side][r] * near[r] - (total[r] + _zsum(near[r], lane))
                    for r in (slice(8 * i, 8 * i + 8) for i in range(WX // 8))
                ]
                image[c, pl.ds(FIRST + (WY if side else -1), WX, PITCH)] = jnp.concatenate(value, axis=0) * in_y[side]
            return carry

        lax.fori_loop(0, HALF, edges, 0)
    out = [
        pltpu.make_async_copy((a, b)[c // HALF].at[c % HALF], kept.at[c], kept_sems.at[c]) for c in range(COMPS)
    ]
    for copy in out:
        copy.start()
    occ = [occupations[k] for k in range(COMPS // 2)]

    def pair(k, totals):
        for d in range(2):
            x = 2 * k + d
            for h in range(2):
                cells = [psi[c, pl.ds(pl.multiple_of(WY * x + 16 * h, 16), 16)].astype(f32) for c in range(COMPS)]
                for i in (2 * h, 2 * h + 1):
                    r = slice(8 * (i % 2), 8 * (i % 2) + 8)
                    row = pl.ds(pl.multiple_of(WY * x + 8 * i, 8), 8)
                    weight = pot[row]
                    sums = None
                    for orbital in range(COMPS // 2):
                        picked = [
                            lambda at, c=c: (a, b)[c // HALF][c % HALF, pl.ds(at, 8)]
                            for c in (2 * orbital, 2 * orbital + 1)
                        ]
                        own_cells = (cells[2 * orbital][r], cells[2 * orbital + 1][r])
                        real, imag = _stepped(own_cells, picked, weight, orbital, _base(x + 1) + 8 * i, lane)
                        term = occ[orbital] * (real * real + imag * imag)
                        sums = term if sums is None else sums + term
                    charge[row, :] = sums
                    totals = totals + sums
        return totals

    totals = lax.fori_loop(0, WX // 2, pair, jnp.zeros((8, 128), f32))
    mean = jnp.broadcast_to(jnp.sum(totals, keepdims=True) / (WX * WY * NZ), (8, 128))

    def group(g, carry):
        cells = charge[pl.ds(pl.multiple_of(128 * g, 128), 128), :] - mean[0:1]
        high, low = _split(cells)
        modes = lax.dot_general(
            beside[...],
            jnp.concatenate([high, low, high], axis=1),
            (((1,), (1,)), ((), ())),
            preferred_element_type=f32,
        )
        for k in range(16):
            rows[pl.ds(8 * FWD * k + g, 8, FWD), :] = modes[8 * k : 8 * k + 8]
        return carry

    lax.fori_loop(0, WX // 4, group, 0, unroll=3)
    for k in range(16):
        rows[pl.ds(8 * FWD * k + FWD - 1, 8, FWD), :] = mean
    send = pltpu.make_async_copy(rows, message, row_sem)
    send.start()
    send.wait()
    for copy in out:
        copy.wait()


def _charge_messages(occupations, psi, pot, image_a, image_b, *faces):
    t = _tables()
    half = jax.ShapeDtypeStruct((HALF, PADDED, NZ), f32)
    shapes = _FACES + [_Y_FACE] * 2
    return pl.pallas_call(
        _charge_kernel,
        name="charge",
        in_specs=[_SM] + [_VM] * 5 + [_HBM] * len(faces),
        out_specs=[_HBM, _HBM, _VM, _VM],
        out_shape=[
            jax.ShapeDtypeStruct((DEVICES * FWD, 128), f32),
            jax.ShapeDtypeStruct((COMPS, PADDED, NZ), f32),
            half,
            half,
        ],
        scratch_shapes=[pltpu.VMEM(s, bf16) for s in shapes]
        + [
            pltpu.VMEM((7, 64, NZ), f32),
            pltpu.VMEM((WX * WY, NZ), f32),
            pltpu.VMEM((DEVICES * FWD, 128), f32),
            pltpu.SemaphoreType.DMA((len(shapes),)),
            pltpu.SemaphoreType.DMA((COMPS,)),
            pltpu.SemaphoreType.DMA,
        ],
        input_output_aliases={4: 2, 5: 3},
        compiler_params=pltpu.CompilerParams(vmem_limit_bytes=32 * 1024 * 1024),
        cost_estimate=pl.CostEstimate(flops=100000000, bytes_accessed=8000000, transcendentals=0),
    )(occupations, jnp.asarray(t["beside"]), psi, pot, image_a, image_b, *faces)[:2]


def _swap_groups(blocks, group):
    out = []
    for i in range(4):
        value = None
        for j in range(4):
            shift = (32 * (j - i)) % 128
            moved = pltpu.roll(blocks[j], shift, 1) if shift else blocks[j]
            value = moved if value is None else jnp.where(group == j, moved, value)
        out.append(value)
    return out


def _plane_kernel(modes, recv, forward_x, sy, back_x, ring_y, col, row, send, packed, block):
    dot = functools.partial(jnp.dot, precision=HIGHEST, preferred_element_type=f32)
    nt = lambda a, b: lax.dot_general(a, b, (((1,), (1,)), ((), ())), precision=HIGHEST, preferred_element_type=f32)
    kz = (lax.axis_index("orb") * POIS + lax.axis_index("pois")) * SLABS + lax.axis_index("slab")
    lam_z, sum_z = modes[0, kz], modes[1, kz]
    means = recv[pl.ds(FWD - 1, DEVICES, FWD), :]
    blocks = POIS * SLABS
    block_mean = sum(means[blocks * o : blocks * (o + 1)] for o in range(ORBS))
    mean = jnp.sum(block_mean, axis=0, keepdims=True) / blocks
    block_means = [block_mean[k : k + 1] for k in range(blocks)]
    for p in range(POIS):
        for s in range(SLABS):
            total = None
            for o in range(ORBS):
                part = recv[pl.ds(((o * POIS + p) * SLABS + s) * FWD, 12), :]
                total = part if total is None else total + part
            packed[p, pl.ds(12 * s, 12), :] = total + sum_z * (block_means[p * SLABS + s][0:1] - mean)
    group = lax.broadcasted_iota(jnp.int32, (WX, 128), 1) // 32
    plane = jnp.concatenate(_swap_groups([packed[p] for p in range(POIS)], group), axis=0)
    spectrum = dot(dot(forward_x[...], plane), sy[...])
    divisor = col[:, 0:1] + row[0:1, :] + lam_z
    factor = 32.0 * math.pi / ((NX + 1) * (NY + 1) * (NZ + 1))
    scaled = spectrum * factor / divisor
    across = dot(back_x[...], scaled)
    field = dot(across[:NX], sy[...])
    ring = dot(across[NX + 256 :], sy[...])
    cells = _swap_groups([field[WX * i : WX * (i + 1)] for i in range(4)], group)
    lane8 = lax.broadcasted_iota(jnp.int32, (8, 128), 1)
    group8 = lane8 // 32
    faces = [nt(ring_y[...], across[NX + 128 * h : NX + 128 * (h + 1)]) for h in range(2)]
    y_rows = []
    for s in range(SLABS):
        low, high = faces[s // 2][0:8], faces[s // 2][8:16]
        if s % 2 == 0:
            high = pltpu.roll(high, 64, 1)
        else:
            low = pltpu.roll(low, 64, 1)
        y_rows.append(jnp.where(lane8 < 64, low, high))
    for p in range(POIS):
        shift = lambda v, k: pltpu.roll(v, k % 128, 1) if k % 128 else v
        x_rows = jnp.where(
            group8 == 0,
            shift(ring[0:8], -32 * p),
            jnp.where(group8 == 1, shift(ring[8:16], 32 - 32 * p), 0.0),
        )
        for s in range(SLABS):
            base = (p * SLABS + s) * BACK
            block[pl.ds(base, 12), :] = cells[p][12 * s : 12 * s + 12]
            block[pl.ds(base + 12, 1), :] = x_rows[s : s + 1]
            block[pl.ds(base + 13, 1), :] = y_rows[s][p : p + 1]
    count = POIS * SLABS * BACK
    for o in range(ORBS):
        send[pl.ds(o * count, count), :] = block[...]


def _plane(recv):
    t = _tables()
    return pl.pallas_call(
        _plane_kernel,
        name="plane",
        in_specs=[_SM] + [_VM] * 7,
        out_specs=_VM,
        out_shape=jax.ShapeDtypeStruct((DEVICES * BACK, 128), f32),
        scratch_shapes=[
            pltpu.VMEM((POIS, WX, 128), f32),
            pltpu.VMEM((POIS * SLABS * BACK, 128), f32),
        ],
        cost_estimate=pl.CostEstimate(flops=200000000, bytes_accessed=3000000, transcendentals=0),
    )(
        jnp.asarray(t["modes"]),
        recv,
        *(jnp.asarray(t[k]) for k in ("forward_x", "sy", "back_x", "ring_y", "col", "row")),
    )


OUT_GROUP = 8


def _step_kernel(stacked, recv_hbm, tiled_hbm, kept, psi, ext, old, x_low, x_high, y_low, y_high, new, hartree, *scratch):
    psi_v, psi_f, image, pot, change, ring_y, pots, recv, tiled, slices, out = scratch[:11]
    faces, sems, out_sems = scratch[11:15], scratch[15], scratch[16]
    orb = lax.axis_index("orb")
    in_x, in_y = _inside()
    sub, lane = _iotas()
    pairs = [(recv_hbm, recv), (tiled_hbm.at[orb], tiled), (ext, pots.at[0]), (old, pots.at[1])]
    pairs += list(zip((x_low, x_high, y_low, y_high), faces))
    early = len(pairs)
    for c in range(COMPS):
        pairs += [(psi.at[c], psi_v.at[c, pl.ds(WY, WX * WY)]), (kept.at[c], image.at[c])]
    copies = [pltpu.make_async_copy(a, b, sems.at[k]) for k, (a, b) in enumerate(pairs)]
    for copy in copies:
        copy.start()
    for copy in copies[:early]:
        copy.wait()

    def back(r, table):
        high, low = _split(recv[pl.ds(r, 128, BACK), :])
        stack = jnp.concatenate([high, low, high], axis=0)
        return lax.dot_general(stack, table[...], (((0,), (0,)), ((), ())), preferred_element_type=f32)

    def planes(g, carry):
        field = back(g, stacked)
        first = pl.multiple_of(4 * WY * g, 8)
        block = pl.ds(first, 4 * WY)
        moved = pl.ds(pl.multiple_of(first + WY, 8), 4 * WY)
        pot[moved] = 6.0 + (2.0 * pots[0, block] + (pots[1, block] + field))
        change[moved] = field - pots[1, block]
        mine = back(g, tiled)
        for k in range(16):
            kept_lanes = jnp.where(lane // 16 == sub, mine[8 * k : 8 * k + 8], 0.0)
            slices[k % 4, pl.ds(4 * g + k // 4, 1), :] = jnp.sum(kept_lanes, axis=0, keepdims=True)
        return carry

    lax.fori_loop(0, WX // 4, planes, 0, unroll=2)
    x_field, y_field = back(12, stacked), back(13, stacked)
    for side in range(2):
        edge = pl.ds((WX + 1) * WY * side, WY)
        change[edge] = (x_field[32 * side : 32 * side + 32] - _pair(faces[side], COMPS + 1)) * in_x[side]
        ring_y[side] = (y_field[64 * side : 64 * side + WX] - _pair(faces[2 + side], COMPS + 1)) * in_y[side]
    for q in range(4):
        turned = jnp.transpose(slices[q])
        for y in range(8):
            hartree[8 * q + y] = turned[16 * y : 16 * y + 16, 0:WX]

    for c in range(COMPS):
        copies[early + 2 * c].wait()
        copies[early + 2 * c + 1].wait()

    def one(c, carry):
        for side in range(2):
            psi_v[c, pl.ds((WX + 1) * WY * side, WY)] = faces[side][c, 1 - side]

        def planes_of(j, carry):
            for k in range(5):
                p = 5 * j + k
                rows = pl.ds(pl.multiple_of(WY * p, WY), WY)
                value = psi_v[c, rows].astype(f32)
                at = pl.ds(_base(p), WY)
                image[c, at] = image[c, at] + change[rows] * value
                psi_f[c, at] = value
            return carry

        lax.fori_loop(0, PLANES // 5, planes_of, 0)
        for side in range(2):
            at = pl.ds(FIRST + (WY if side else -1), WX, PITCH)
            image[c, at] = image[c, at] + ring_y[side] * faces[2 + side][c, 1 - side].astype(f32)
        return carry

    lax.fori_loop(0, COMPS, one, 0)

    def out_copy(j, c):
        planes = pl.ds(OUT_GROUP * j, OUT_GROUP)
        return pltpu.make_async_copy(out.at[c, planes], new.at[c, planes], out_sems.at[j, c])

    def group(j, carry):
        def pair(k, carry):
            for d in range(2):
                x = OUT_GROUP * j + 2 * k + d
                for i in range(4):
                    at = _base(x + 1) + 8 * i
                    weight = pot[pl.ds(pl.multiple_of(WY * (x + 1) + 8 * i, 8), 8)]
                    for orbital in range(COMPS // 2):
                        parts = (2 * orbital, 2 * orbital + 1)
                        cells = [psi_f[c, pl.ds(pl.multiple_of(at, 8), 8)] for c in parts]
                        picked = [lambda row, c=c: image[c, pl.ds(row, 8)] for c in parts]
                        real, imag = _stepped(cells, picked, weight, orbital, at, lane)
                        out[2 * orbital, x, 8 * i : 8 * i + 8] = real
                        out[2 * orbital + 1, x, 8 * i : 8 * i + 8] = imag
            return carry

        lax.fori_loop(0, OUT_GROUP // 2, pair, 0)
        for c in range(COMPS):
            out_copy(j, c).start()
        return carry

    lax.fori_loop(0, WX // OUT_GROUP, group, 0)
    for j in range(WX // OUT_GROUP):
        for c in range(COMPS):
            out_copy(j, c).wait()


def _step(recv, kept, *arrays):
    t = _tables()
    return pl.pallas_call(
        _step_kernel,
        name="step",
        in_specs=[_VM, _HBM, _HBM, _HBM] + [_HBM] * len(arrays),
        out_specs=[_HBM, _VM],
        out_shape=[
            jax.ShapeDtypeStruct((COMPS, WX, WY, NZ), f32),
            jax.ShapeDtypeStruct((WY, NZ // ORBS, WX), f32),
        ],
        scratch_shapes=[
            pltpu.VMEM((COMPS, PLANES * WY, NZ), bf16),
            pltpu.VMEM((COMPS, PADDED, NZ), f32),
            pltpu.VMEM((COMPS, PADDED, NZ), f32),
            pltpu.VMEM((PLANES * WY, NZ), f32),
            pltpu.VMEM((PLANES * WY, NZ), f32),
            pltpu.VMEM((2, WX, NZ), f32),
            pltpu.VMEM((2, WX * WY, NZ), f32),
            pltpu.VMEM((DEVICES * BACK, 128), f32),
            pltpu.VMEM((3 * NZ, 128), bf16),
            pltpu.VMEM((4, 128, 128), f32),
            pltpu.VMEM((COMPS, WX, WY, NZ), f32),
        ]
        + [pltpu.VMEM(s, bf16) for s in _FACES]
        + [
            pltpu.SemaphoreType.DMA((8 + 2 * COMPS,)),
            pltpu.SemaphoreType.DMA((WX // OUT_GROUP, COMPS)),
        ],
        compiler_params=pltpu.CompilerParams(vmem_limit_bytes=VMEM_LIMIT),
        cost_estimate=pl.CostEstimate(flops=100000000, bytes_accessed=20000000, transcendentals=0),
    )(jnp.asarray(t["stacked"]), recv, jnp.asarray(t["tiled"]), kept, *arrays)


def _shifted(value, axis, count, step):
    return lax.ppermute(value, axis, [(i, (i + step) % count) for i in range(count)])


def _swap(messages, rows):
    moved = lax.all_to_all(messages.reshape(DEVICES, 1, rows * 128), TRANSPOSE_AXES, 0, 0)
    return moved.reshape(DEVICES * rows, 128)


def body(orbitals, occupations, ext_pot, hartree_old):
    psi = orbitals.reshape(COMPS, WX * WY, NZ)
    ext, old = ext_pot.reshape(WX * WY, NZ), hartree_old.reshape(WX * WY, NZ)
    x_left, x_right, y_left, y_right, pot = _faces(psi, ext, old)
    y_low = _shifted(y_right, "pois", POIS, 1)
    y_high = _shifted(y_left, "pois", POIS, -1)
    image_a, done = _inner(0, psi, pot)
    x_left, x_right = _corners(x_left, x_right, y_low, y_high, done)
    x_low = _shifted(x_right, "slab", SLABS, 1)
    x_high = _shifted(x_left, "slab", SLABS, -1)
    image_b, _ = _inner(HALF, psi, pot)
    faces = (x_low, x_high, y_low, y_high)
    message, kept = _charge_messages(occupations, psi, pot, image_a, image_b, *faces, y_left, y_right)
    back = _swap(_plane(_swap(message, FWD)), BACK)
    new, hartree = _step(back, kept, psi, ext, old, *faces)
    return new.reshape(orbitals.shape), jnp.transpose(hartree, (2, 0, 1))


def solution(mesh):
    placed = (P("orb", None, "slab", "pois", None), P("orb"), P("slab", "pois", None), P("slab", "pois", None))
    return jax.shard_map(
        body,
        mesh=mesh,
        in_specs=placed,
        out_specs=(P("orb", None, "slab", "pois", None), P("slab", "pois", "orb")),
        check_vma=False,
    )
```

```python
import functools
import math

import jax
import jax.numpy as jnp
import ml_dtypes
import numpy as np
from jax import lax
from jax.experimental import pallas as pl
from jax.experimental.pallas import tpu as pltpu
from jax.sharding import PartitionSpec as P

NX, NY, NZ = 192, 128, 128
SLABS, ORBS, POIS = 4, 8, 4
WX, WY = NX // SLABS, NY // POIS
COMPS = 8
FWD = 13
BACK = 14
DEVICES = SLABS * ORBS * POIS
TRANSPOSE_AXES = ("orb", "pois", "slab")
DT = 0.3
VMEM_LIMIT = 67043328

PITCH = 40
PLANES = WX + 2
PADDED = 8 + (PLANES + 2) * PITCH
GROUP = 24
HALF = COMPS // 2
FIRST = 8 + 2 * PITCH
f32, bf16 = jnp.float32, jnp.bfloat16


def _sines(n):
    k = np.arange(1, n + 1)
    return np.sin(np.pi * ((k[:, None] * k[None, :]) % (2 * (n + 1))) / (n + 1))


def _lam(n):
    return 2.0 - 2.0 * np.cos(np.pi * np.arange(1, n + 1) / (n + 1))


@functools.cache
def _tables():
    sx, sy = _sines(NX), _sines(NY)
    order = np.array([s * WX + 4 * xb + xi for xi in range(4) for s in range(SLABS) for xb in range(WX // 4)])
    padded = np.zeros((SLABS * 64, NX))
    for s in range(SLABS):
        padded[s * 64 : s * 64 + WX] = sx[s * WX : (s + 1) * WX]
    ring_x = np.zeros((16, NX))
    ring_y = np.zeros((16, NY))
    for s in range(SLABS):
        if s > 0:
            ring_x[s] = sx[s * WX - 1]
        if s < SLABS - 1:
            ring_x[8 + s] = sx[(s + 1) * WX]
    for p in range(POIS):
        if p > 0:
            ring_y[p] = sy[p * WY - 1]
        if p < POIS - 1:
            ring_y[8 + p] = sy[(p + 1) * WY]
    back_x = np.concatenate([sx[order], padded, ring_x])
    modes = np.stack([_lam(NZ), sy.sum(1)])
    cast = lambda a: np.asarray(a, np.float32)

    def split(a):
        high = cast(a).astype(ml_dtypes.bfloat16)
        return high, (cast(a) - high.astype(np.float32)).astype(ml_dtypes.bfloat16)

    def wide(a):
        high, low = split(a)
        return np.concatenate([high, high, low], 1)

    high, low = split(sy)
    tiles = [np.arange(128) % (NZ // ORBS) + o * (NZ // ORBS) for o in range(ORBS)]
    stacked = np.concatenate([high, high, low], 0)
    shift = np.eye(NZ, k=1) + np.eye(NZ, k=-1)
    return dict(
        near=shift.astype(ml_dtypes.bfloat16),
        beside=wide(sy),
        stacked=stacked,
        tiled=np.stack([stacked[:, t] for t in tiles]),
        forward_x=wide(sx[:, order]),
        back_x=wide(back_x),
        ring_y=wide(ring_y),
        col=cast(np.stack([_lam(NX), sx.sum(1)] + [np.zeros(NX)] * 6, 1)),
        row=cast(np.stack([_lam(NY), sy.sum(1)] + [np.zeros(NY)] * 6, 0)),
        modes=cast(modes),
    )


_VM = pl.BlockSpec(memory_space=pltpu.VMEM)
_SM = pl.BlockSpec(memory_space=pltpu.SMEM)
_ANY = pl.BlockSpec(memory_space=pl.ANY)
_HBM = pl.BlockSpec(memory_space=pltpu.HBM)
CORNERS = COMPS + 2
_X_FACE, _Y_FACE = (COMPS + 3, 2, WY, NZ), (COMPS + 2, 2, WX, NZ)
_FACES = [_X_FACE, _X_FACE, _Y_FACE, _Y_FACE]


def _iotas():
    return (
        lax.broadcasted_iota(jnp.int32, (8, 128), 0),
        lax.broadcasted_iota(jnp.int32, (8, 128), 1),
    )


def _zsum(v, lane):
    return jnp.where(lane == 0, 0.0, pltpu.roll(v, 1, 1)) + jnp.where(lane == 127, 0.0, pltpu.roll(v, 127, 1))


def _base(plane):
    return pl.multiple_of(8 + PITCH + PITCH * plane, 8)


def _split(value):
    high = value.astype(bf16)
    return high, (value - high.astype(f32)).astype(bf16)


def _faces_kernel(psi_hbm, ext, old, x_left, x_right, y_left, y_right, pot, psi, pots, rows, sems):
    copies = [pltpu.make_async_copy(psi_hbm.at[c], psi.at[c], sems.at[2 + c]) for c in range(COMPS)]
    copies = [pltpu.make_async_copy(ref, pots.at[k], sems.at[k]) for k, ref in enumerate((ext, old))] + copies
    for copy in copies:
        copy.start()
    for c in range(COMPS):
        copies[2 + c].wait()

        def fill(x, carry, c=c):
            start = pl.multiple_of(WY * x, WY)
            rows[0, pl.ds(pl.multiple_of(8 * x, 8), 8), :] = psi[c, pl.ds(start, 16), :].astype(f32)[0:8]
            rows[1, pl.ds(pl.multiple_of(8 * x, 8), 8), :] = psi[c, pl.ds(start + 16, 16), :].astype(f32)[8:16]
            return carry

        lax.fori_loop(0, WX, fill, 0, unroll=16)
        for d in range(2):
            x_left[c, d] = psi[c, WY * d : WY * (d + 1)]
            x_right[c, d] = psi[c, WY * (WX - 2 + d) : WY * (WX - 1 + d)]
        for half, ref, first in ((0, y_left, 0), (1, y_right, 6)):
            for d in range(2):
                ref[c, d] = rows[half, pl.ds(first + d, WX, 8), :].astype(bf16)
    for k in range(2):
        copies[k].wait()
        for ref, value in (
            (x_left, pots[k, 0:WY]),
            (x_right, pots[k, WY * (WX - 1) : WY * WX]),
            (y_left, pots[k, pl.ds(0, WX, WY), :]),
            (y_right, pots[k, pl.ds(WY - 1, WX, WY), :]),
        ):
            ref[COMPS + k, 0], ref[COMPS + k, 1] = _split(value)
    pot[...] = 6.0 + 2.0 * (pots[0] + pots[1])


def _faces(psi, ext, old):
    return pl.pallas_call(
        _faces_kernel,
        name="faces",
        in_specs=[_HBM] * 3,
        out_specs=[_VM] * 5,
        out_shape=[jax.ShapeDtypeStruct(s, bf16) for s in _FACES] + [jax.ShapeDtypeStruct((WX * WY, NZ), f32)],
        scratch_shapes=[
            pltpu.VMEM((COMPS, WX * WY, NZ), bf16),
            pltpu.VMEM((2, WX * WY, NZ), f32),
            pltpu.VMEM((2, 8 * WX, 128), f32),
            pltpu.SemaphoreType.DMA((2 + COMPS,)),
        ],
        compiler_params=pltpu.CompilerParams(vmem_limit_bytes=VMEM_LIMIT),
        cost_estimate=pl.CostEstimate(flops=1000000, bytes_accessed=6000000, transcendentals=0),
    )(psi, ext, old)


def _corners_kernel(x_left, x_right, low_first, low_last, high_first, high_last, after, left, right, block):
    del x_left, x_right, after
    for out, refs, row in ((left, (low_first, high_first), 0), (right, (low_last, high_last), 15)):
        for side in range(2):
            for c in range(COMPS):
                block[c : c + 1] = refs[side][c, 0].astype(f32)[row : row + 1]
            out[0, side] = block[...].astype(bf16)


def _corners(x_left, x_right, y_low, y_high, after):
    entry = pl.BlockSpec((1, 2, WY, NZ), lambda i: (CORNERS, 0, 0, 0))
    rows = lambda near, at: pl.BlockSpec((COMPS, 1, 16, NZ), lambda i: (0, near, at, 0))
    shape = jax.ShapeDtypeStruct(_X_FACE, bf16)
    return pl.pallas_call(
        _corners_kernel,
        name="corners",
        grid=(1,),
        in_specs=[entry, entry, rows(1, 0), rows(1, 2), rows(0, 0), rows(0, 2), _ANY],
        out_specs=[entry, entry],
        out_shape=[shape, shape],
        scratch_shapes=[pltpu.VMEM((WY, NZ), f32)],
        input_output_aliases={0: 0, 1: 1},
        compiler_params=pltpu.CompilerParams(vmem_limit_bytes=2 * 1024 * 1024),
        cost_estimate=pl.CostEstimate(flops=10000, bytes_accessed=200000, transcendentals=0),
    )(x_left, x_right, y_low, y_low, y_high, y_high, after)


def _inner_kernel(first_part, near, psi, pot, image, token, psi_f):
    token[...] = jnp.zeros((8, NZ), f32)
    for c in range(HALF):

        def widen(x, carry, c=c):
            rows = pl.ds(pl.multiple_of(WY * x, WY), WY)
            psi_f[c, pl.ds(_base(x + 1), WY)] = psi[first_part + c, rows].astype(f32)
            return carry

        lax.fori_loop(0, WX, widen, 0, unroll=16)
        for side in range(2):
            psi_f[c, pl.ds(FIRST + (WY if side else -1), WX, PITCH)] = jnp.zeros((WX, NZ), f32)
            psi_f[c, pl.ds(FIRST - PITCH + (WX + 1) * PITCH * side, WY)] = jnp.zeros((WY, NZ), f32)

    def group(k, carry):
        c, j = k // (WX // GROUP), k % (WX // GROUP)
        start = pl.multiple_of(GROUP * WY * j, WY)
        sums = jnp.dot(
            psi[first_part + c, pl.ds(start, GROUP * WY)], near[...], preferred_element_type=f32
        )
        for g in range(GROUP):
            base = _base(GROUP * j + g + 1)
            for i in range(4):
                at = base + 8 * i
                load = lambda row: psi_f[c, pl.ds(row, 8)]
                beside = (load(at - 1) + load(at + 1)) + (load(at - PITCH) + load(at + PITCH))
                first = WY * g + 8 * i
                weight = pot[pl.ds(pl.multiple_of(start + first, 8), 8)]
                value = weight * load(pl.multiple_of(at, 8)) - (beside + sums[first : first + 8])
                image[c, pl.ds(pl.multiple_of(at, 8), 8)] = value
        return carry

    lax.fori_loop(0, HALF * (WX // GROUP), group, 0)


def _inner(first_part, psi, pot):
    return pl.pallas_call(
        functools.partial(_inner_kernel, first_part),
        name="inner",
        in_specs=[_VM] * 3,
        out_specs=[_VM, _VM],
        out_shape=[jax.ShapeDtypeStruct((HALF, PADDED, NZ), f32), jax.ShapeDtypeStruct((8, NZ), f32)],
        scratch_shapes=[pltpu.VMEM((HALF, PADDED, NZ), f32)],
        compiler_params=pltpu.CompilerParams(vmem_limit_bytes=24 * 1024 * 1024),
        cost_estimate=pl.CostEstimate(flops=400000000, bytes_accessed=12000000, transcendentals=0),
    )(jnp.asarray(_tables()["near"]), psi, pot)


def _inside():
    slab, pois = lax.axis_index("slab"), lax.axis_index("pois")
    number = lambda cond: jnp.where(cond, 1.0, 0.0).astype(f32)
    return (
        (number(slab > 0), number(slab < SLABS - 1)),
        (number(pois > 0), number(pois < POIS - 1)),
    )


def _pair(ref, k):
    return ref[k, 0].astype(f32) + ref[k, 1].astype(f32)


def _stepped(cells, images, pot, orbital, at, lane):
    parts = []
    for k in range(2):
        load = lambda row, hint=True: images[k](pl.multiple_of(row, 8) if hint else row)
        u = load(at)
        total = (load(at - PITCH) + load(at + PITCH)) + (load(at - 1, False) + load(at + 1, False)) + _zsum(u, lane)
        parts.append((cells[k], u, pot * u - total))
    (a, ua, wa), (b, ub, wb) = parts
    scale = 0.125 * DT * DT
    return (a - scale * wa) + (0.5 * DT) * ub, (b - scale * wb) - (0.5 * DT) * ua


def _charge_kernel(
    occupations, beside, psi, pot, image_a, image_b, x_low_h, x_high_h, y_low_h, y_high_h, own_low_h, own_high_h,
    message, a, b, x_low, x_high, y_low, y_high, own_low, own_high, column, charge, rows, sems, row_sem,
):
    del image_a, image_b
    pairs = list(zip((x_low_h, x_high_h, y_low_h, y_high_h, own_low_h, own_high_h), (x_low, x_high, y_low, y_high, own_low, own_high)))
    copies = [pltpu.make_async_copy(p, q, sems.at[k]) for k, (p, q) in enumerate(pairs)]
    for copy in copies:
        copy.start()
    for copy in copies:
        copy.wait()
    sub, lane = _iotas()
    in_x, in_y = _inside()
    x_faces, y_faces, own = (x_low, x_high), (y_low, y_high), (own_low, own_high)
    ring_x = [6.0 + 2.0 * (_pair(f, COMPS) + _pair(f, COMPS + 1)) for f in x_faces]
    ring_y = [6.0 + 2.0 * (_pair(f, COMPS) + _pair(f, COMPS + 1)) for f in y_faces]
    corner = [[x_faces[i][CORNERS, j].astype(f32) * (in_x[i] * in_y[j]) for j in range(2)] for i in range(2)]
    for i in range(2):
        for j in range(2):
            column[3 + 2 * i + j, 0:8] = corner[i][j][0:8]
    for half, image in enumerate((a, b)):

        def edges(c, carry, half=half, image=image):
            part = HALF * half + c
            for side in range(2):
                near = x_faces[side][part, 1 - side].astype(f32) * in_x[side]
                far = x_faces[side][part, side].astype(f32)
                inner = psi[part, pl.ds(WY * (WX - 1) * side, WY)].astype(f32)
                at = pl.ds(FIRST + PITCH * (WX - 1) * side, WY)
                image[c, at] = image[c, at] - near
                column[side, 8:40] = near
                column[side, 7:8] = column[3 + 2 * side, pl.ds(part, 1)]
                column[side, 40:41] = column[4 + 2 * side, pl.ds(part, 1)]
                across = column[side, 7:39] + column[side, 9:41]
                total = (far + inner) + across
                for i in range(4):
                    r = slice(8 * i, 8 * i + 8)
                    ring = ring_x[side][r] * near[r] - (total[r] + _zsum(near[r], lane))
                    image[c, pl.ds(FIRST - PITCH + PITCH * (WX + 1) * side + 8 * i, 8)] = ring * in_x[side]
            for side in range(2):
                near = y_faces[side][part, 1 - side].astype(f32) * in_y[side]
                far = y_faces[side][part, side].astype(f32)
                inner = own[side][part, side].astype(f32)
                at = pl.ds(FIRST + (WY - 1) * side, WX, PITCH)
                image[c, at] = image[c, at] - near
                column[2, 8:56] = near
                column[2, 7:8] = column[3 + side, pl.ds(part, 1)]
                column[2, 56:57] = column[5 + side, pl.ds(part, 1)]
                total = (far + inner) + (column[2, 7:55] + column[2, 9:57])
                value = [
                    ring_y[side][r] * near[r] - (total[r] + _zsum(near[r], lane))
                    for r in (slice(8 * i, 8 * i + 8) for i in range(WX // 8))
                ]
                image[c, pl.ds(FIRST + (WY if side else -1), WX, PITCH)] = jnp.concatenate(value, axis=0) * in_y[side]
            return carry

        lax.fori_loop(0, HALF, edges, 0)
    occ = [occupations[k] for k in range(COMPS // 2)]

    def pair(k, totals):
        for d in range(2):
            x = 2 * k + d
            for h in range(2):
                cells = [psi[c, pl.ds(pl.multiple_of(WY * x + 16 * h, 16), 16)].astype(f32) for c in range(COMPS)]
                for i in (2 * h, 2 * h + 1):
                    r = slice(8 * (i % 2), 8 * (i % 2) + 8)
                    row = pl.ds(pl.multiple_of(WY * x + 8 * i, 8), 8)
                    weight = pot[row]
                    sums = None
                    for orbital in range(COMPS // 2):
                        picked = [
                            lambda at, c=c: (a, b)[c // HALF][c % HALF, pl.ds(at, 8)]
                            for c in (2 * orbital, 2 * orbital + 1)
                        ]
                        own_cells = (cells[2 * orbital][r], cells[2 * orbital + 1][r])
                        real, imag = _stepped(own_cells, picked, weight, orbital, _base(x + 1) + 8 * i, lane)
                        term = occ[orbital] * (real * real + imag * imag)
                        sums = term if sums is None else sums + term
                    charge[row, :] = sums
                    totals = totals + sums
        return totals

    totals = lax.fori_loop(0, WX // 2, pair, jnp.zeros((8, 128), f32))
    mean = jnp.broadcast_to(jnp.sum(totals, keepdims=True) / (WX * WY * NZ), (8, 128))

    def group(g, carry):
        cells = charge[pl.ds(pl.multiple_of(128 * g, 128), 128), :] - mean[0:1]
        high, low = _split(cells)
        modes = lax.dot_general(
            beside[...],
            jnp.concatenate([high, low, high], axis=1),
            (((1,), (1,)), ((), ())),
            preferred_element_type=f32,
        )
        for k in range(16):
            rows[pl.ds(8 * FWD * k + g, 8, FWD), :] = modes[8 * k : 8 * k + 8]
        return carry

    lax.fori_loop(0, WX // 4, group, 0, unroll=3)
    for k in range(16):
        rows[pl.ds(8 * FWD * k + FWD - 1, 8, FWD), :] = mean
    send = pltpu.make_async_copy(rows, message, row_sem)
    send.start()
    send.wait()


def _charge_messages(occupations, psi, pot, image_a, image_b, *faces):
    t = _tables()
    half = jax.ShapeDtypeStruct((HALF, PADDED, NZ), f32)
    shapes = _FACES + [_Y_FACE] * 2
    return pl.pallas_call(
        _charge_kernel,
        name="charge",
        in_specs=[_SM] + [_VM] * 5 + [_HBM] * len(faces),
        out_specs=[_HBM, _VM, _VM],
        out_shape=[
            jax.ShapeDtypeStruct((DEVICES * FWD, 128), f32),
            half,
            half,
        ],
        scratch_shapes=[pltpu.VMEM(s, bf16) for s in shapes]
        + [
            pltpu.VMEM((7, 64, NZ), f32),
            pltpu.VMEM((WX * WY, NZ), f32),
            pltpu.VMEM((DEVICES * FWD, 128), f32),
            pltpu.SemaphoreType.DMA((len(shapes),)),
            pltpu.SemaphoreType.DMA,
        ],
        input_output_aliases={4: 1, 5: 2},
        compiler_params=pltpu.CompilerParams(vmem_limit_bytes=32 * 1024 * 1024),
        cost_estimate=pl.CostEstimate(flops=100000000, bytes_accessed=8000000, transcendentals=0),
    )(occupations, jnp.asarray(t["beside"]), psi, pot, image_a, image_b, *faces)


def _swap_groups(blocks, group):
    out = []
    for i in range(4):
        value = None
        for j in range(4):
            shift = (32 * (j - i)) % 128
            moved = pltpu.roll(blocks[j], shift, 1) if shift else blocks[j]
            value = moved if value is None else jnp.where(group == j, moved, value)
        out.append(value)
    return out


def _plane_kernel(modes, recv, forward_x, stacked, back_x, ring_y, col, row, send, packed, block):
    dot = functools.partial(jnp.dot, preferred_element_type=f32)

    def parts(value, axis):
        high, low = _split(value)
        return jnp.concatenate([high, low, high], axis=axis)

    left = lambda table, value: dot(table[...], parts(value, 0))
    right = lambda value: dot(parts(value, 1), stacked[...])
    nt = lambda table, value: lax.dot_general(
        table[...], parts(value, 1), (((1,), (1,)), ((), ())), preferred_element_type=f32
    )
    kz = (lax.axis_index("orb") * POIS + lax.axis_index("pois")) * SLABS + lax.axis_index("slab")
    lam_z, sum_z = modes[0, kz], modes[1, kz]
    means = recv[pl.ds(FWD - 1, DEVICES, FWD), :]
    blocks = POIS * SLABS
    block_mean = sum(means[blocks * o : blocks * (o + 1)] for o in range(ORBS))
    mean = jnp.sum(block_mean, axis=0, keepdims=True) / blocks
    block_means = [block_mean[k : k + 1] for k in range(blocks)]
    for p in range(POIS):
        for s in range(SLABS):
            total = None
            for o in range(ORBS):
                part = recv[pl.ds(((o * POIS + p) * SLABS + s) * FWD, 12), :]
                total = part if total is None else total + part
            packed[p, pl.ds(12 * s, 12), :] = total + sum_z * (block_means[p * SLABS + s][0:1] - mean)
    group = lax.broadcasted_iota(jnp.int32, (WX, 128), 1) // 32
    plane = jnp.concatenate(_swap_groups([packed[p] for p in range(POIS)], group), axis=0)
    spectrum = right(left(forward_x, plane))
    divisor = col[:, 0:1] + row[0:1, :] + lam_z
    factor = 32.0 * math.pi / ((NX + 1) * (NY + 1) * (NZ + 1))
    scaled = spectrum * factor / divisor
    across = left(back_x, scaled)
    field = right(across[:NX])
    ring = right(across[NX + 256 :])
    cells = _swap_groups([field[WX * i : WX * (i + 1)] for i in range(4)], group)
    lane8 = lax.broadcasted_iota(jnp.int32, (8, 128), 1)
    group8 = lane8 // 32
    faces = [nt(ring_y, across[NX + 128 * h : NX + 128 * (h + 1)]) for h in range(2)]
    y_rows = []
    for s in range(SLABS):
        low, high = faces[s // 2][0:8], faces[s // 2][8:16]
        if s % 2 == 0:
            high = pltpu.roll(high, 64, 1)
        else:
            low = pltpu.roll(low, 64, 1)
        y_rows.append(jnp.where(lane8 < 64, low, high))
    for p in range(POIS):
        shift = lambda v, k: pltpu.roll(v, k % 128, 1) if k % 128 else v
        x_rows = jnp.where(
            group8 == 0,
            shift(ring[0:8], -32 * p),
            jnp.where(group8 == 1, shift(ring[8:16], 32 - 32 * p), 0.0),
        )
        for s in range(SLABS):
            base = (p * SLABS + s) * BACK
            block[pl.ds(base, 12), :] = cells[p][12 * s : 12 * s + 12]
            block[pl.ds(base + 12, 1), :] = x_rows[s : s + 1]
            block[pl.ds(base + 13, 1), :] = y_rows[s][p : p + 1]
    count = POIS * SLABS * BACK
    for o in range(ORBS):
        send[pl.ds(o * count, count), :] = block[...]


def _plane(recv):
    t = _tables()
    return pl.pallas_call(
        _plane_kernel,
        name="plane",
        in_specs=[_SM] + [_VM] * 7,
        out_specs=_VM,
        out_shape=jax.ShapeDtypeStruct((DEVICES * BACK, 128), f32),
        scratch_shapes=[
            pltpu.VMEM((POIS, WX, 128), f32),
            pltpu.VMEM((POIS * SLABS * BACK, 128), f32),
        ],
        compiler_params=pltpu.CompilerParams(vmem_limit_bytes=8 * 1024 * 1024),
        cost_estimate=pl.CostEstimate(flops=200000000, bytes_accessed=3000000, transcendentals=0),
    )(
        jnp.asarray(t["modes"]),
        recv,
        *(jnp.asarray(t[k]) for k in ("forward_x", "stacked", "back_x", "ring_y", "col", "row")),
    )


OUT_GROUP = 8


def _step_kernel(
    stacked, recv, tiled_hbm, image_a, image_b, psi, ext, old, x_low, x_high, y_low, y_high,
    new, hartree, image, pot, change, ring_y, tiled, slices, out, sem, out_sems,
):
    faces = (x_low, x_high, y_low, y_high)
    in_x, in_y = _inside()
    sub, lane = _iotas()
    tiled_copy = pltpu.make_async_copy(tiled_hbm.at[lax.axis_index("orb")], tiled, sem)
    tiled_copy.start()
    tiled_copy.wait()

    def back(r, table):
        high, low = _split(recv[pl.ds(r, 128, BACK), :])
        stack = jnp.concatenate([high, low, high], axis=0)
        return lax.dot_general(stack, table[...], (((0,), (0,)), ((), ())), preferred_element_type=f32)

    def planes(g, carry):
        field = back(g, stacked)
        first = pl.multiple_of(4 * WY * g, 8)
        block = pl.ds(first, 4 * WY)
        moved = pl.ds(pl.multiple_of(first + WY, 8), 4 * WY)
        pot[moved] = 6.0 + (2.0 * ext[block] + (old[block] + field))
        change[moved] = field - old[block]
        mine = back(g, tiled)
        for k in range(16):
            kept_lanes = jnp.where(lane // 16 == sub, mine[8 * k : 8 * k + 8], 0.0)
            slices[k % 4, pl.ds(4 * g + k // 4, 1), :] = jnp.sum(kept_lanes, axis=0, keepdims=True)
        return carry

    lax.fori_loop(0, WX // 4, planes, 0, unroll=2)
    x_field, y_field = back(12, stacked), back(13, stacked)
    for side in range(2):
        edge = pl.ds((WX + 1) * WY * side, WY)
        change[edge] = (x_field[32 * side : 32 * side + 32] - _pair(faces[side], COMPS + 1)) * in_x[side]
        ring_y[side] = (y_field[64 * side : 64 * side + WX] - _pair(faces[2 + side], COMPS + 1)) * in_y[side]
    for q in range(4):
        turned = jnp.transpose(slices[q])
        for y in range(8):
            hartree[8 * q + y] = turned[16 * y : 16 * y + 16, 0:WX]

    for half, start in enumerate((image_a, image_b)):

        def one(c, carry, half=half, start=start):
            part = HALF * half + c

            def planes_of(j, carry):
                for k in range(6):
                    x = 6 * j + k
                    value = psi[part, pl.ds(pl.multiple_of(WY * x, WY), WY)].astype(f32)
                    at = pl.ds(_base(x + 1), WY)
                    image[part, at] = start[c, at] + change[pl.ds(pl.multiple_of(WY * (x + 1), WY), WY)] * value
                return carry

            lax.fori_loop(0, WX // 6, planes_of, 0)
            for side in range(2):
                at = pl.ds(FIRST - PITCH + PITCH * (WX + 1) * side, WY)
                value = faces[side][part, 1 - side].astype(f32)
                image[part, at] = start[c, at] + change[pl.ds((WX + 1) * WY * side, WY)] * value
                at = pl.ds(FIRST + (WY if side else -1), WX, PITCH)
                image[part, at] = start[c, at] + ring_y[side] * faces[2 + side][part, 1 - side].astype(f32)
            return carry

        lax.fori_loop(0, HALF, one, 0)

    def out_copy(j, c):
        planes = pl.ds(OUT_GROUP * j, OUT_GROUP)
        return pltpu.make_async_copy(out.at[c, planes], new.at[c, planes], out_sems.at[j, c])

    def group(j, carry):
        def pair(k, carry):
            for d in range(2):
                x = OUT_GROUP * j + 2 * k + d
                for h in range(2):
                    rows = pl.ds(pl.multiple_of(WY * x + 16 * h, 16), 16)
                    cells = [psi[c, rows].astype(f32) for c in range(COMPS)]
                    for i in (2 * h, 2 * h + 1):
                        r = slice(8 * (i % 2), 8 * (i % 2) + 8)
                        weight = pot[pl.ds(pl.multiple_of(WY * (x + 1) + 8 * i, 8), 8)]
                        for orbital in range(COMPS // 2):
                            parts = (2 * orbital, 2 * orbital + 1)
                            picked = [lambda row, c=c: image[c, pl.ds(row, 8)] for c in parts]
                            own = [cells[c][r] for c in parts]
                            real, imag = _stepped(own, picked, weight, orbital, _base(x + 1) + 8 * i, lane)
                            out[2 * orbital, x, 8 * i : 8 * i + 8] = real
                            out[2 * orbital + 1, x, 8 * i : 8 * i + 8] = imag
            return carry

        lax.fori_loop(0, OUT_GROUP // 2, pair, 0)
        for c in range(COMPS):
            out_copy(j, c).start()
        return carry

    lax.fori_loop(0, WX // OUT_GROUP, group, 0)
    for j in range(WX // OUT_GROUP):
        for c in range(COMPS):
            out_copy(j, c).wait()


def _step(recv, *arrays):
    t = _tables()
    return pl.pallas_call(
        _step_kernel,
        name="step",
        in_specs=[_VM, _VM, _HBM] + [_VM] * len(arrays),
        out_specs=[_HBM, _VM],
        out_shape=[
            jax.ShapeDtypeStruct((COMPS, WX, WY, NZ), f32),
            jax.ShapeDtypeStruct((WY, NZ // ORBS, WX), f32),
        ],
        scratch_shapes=[
            pltpu.VMEM((COMPS, PADDED, NZ), f32),
            pltpu.VMEM((PLANES * WY, NZ), f32),
            pltpu.VMEM((PLANES * WY, NZ), f32),
            pltpu.VMEM((2, WX, NZ), f32),
            pltpu.VMEM((3 * NZ, 128), bf16),
            pltpu.VMEM((4, 128, 128), f32),
            pltpu.VMEM((COMPS, WX, WY, NZ), f32),
            pltpu.SemaphoreType.DMA,
            pltpu.SemaphoreType.DMA((WX // OUT_GROUP, COMPS)),
        ],
        compiler_params=pltpu.CompilerParams(vmem_limit_bytes=24 * 1024 * 1024),
        cost_estimate=pl.CostEstimate(flops=100000000, bytes_accessed=20000000, transcendentals=0),
    )(jnp.asarray(t["stacked"]), recv, jnp.asarray(t["tiled"]), *arrays)


def _shifted(value, axis, count, step):
    return lax.ppermute(value, axis, [(i, (i + step) % count) for i in range(count)])


def _swap(messages, rows):
    moved = lax.all_to_all(messages.reshape(DEVICES, 1, rows * 128), TRANSPOSE_AXES, 0, 0)
    return moved.reshape(DEVICES * rows, 128)


def body(orbitals, occupations, ext_pot, hartree_old):
    psi = orbitals.reshape(COMPS, WX * WY, NZ)
    ext, old = ext_pot.reshape(WX * WY, NZ), hartree_old.reshape(WX * WY, NZ)
    x_left, x_right, y_left, y_right, pot = _faces(psi, ext, old)
    y_low = _shifted(y_right, "pois", POIS, 1)
    y_high = _shifted(y_left, "pois", POIS, -1)
    image_a, done = _inner(0, psi, pot)
    x_left, x_right = _corners(x_left, x_right, y_low, y_high, done)
    x_low = _shifted(x_right, "slab", SLABS, 1)
    x_high = _shifted(x_left, "slab", SLABS, -1)
    image_b, _ = _inner(HALF, psi, pot)
    faces = (x_low, x_high, y_low, y_high)
    message, image_a, image_b = _charge_messages(occupations, psi, pot, image_a, image_b, *faces, y_left, y_right)
    back = _swap(_plane(_swap(message, FWD)), BACK)
    new, hartree = _step(back, image_a, image_b, psi, ext, old, *faces)
    return new.reshape(orbitals.shape), jnp.transpose(hartree, (2, 0, 1))


def solution(mesh):
    placed = (P("orb", None, "slab", "pois", None), P("orb"), P("slab", "pois", None), P("slab", "pois", None))
    return jax.shard_map(
        body,
        mesh=mesh,
        in_specs=placed,
        out_specs=(P("orb", None, "slab", "pois", None), P("slab", "pois", "orb")),
        check_vma=False,
    )
```

```python
import functools
import math

import jax
import jax.numpy as jnp
import ml_dtypes
import numpy as np
from jax import lax
from jax.experimental import pallas as pl
from jax.experimental.pallas import tpu as pltpu
from jax.sharding import PartitionSpec as P

NX, NY, NZ = 192, 128, 128
SLABS, ORBS, POIS = 4, 8, 4
WX, WY = NX // SLABS, NY // POIS
COMPS = 8
FWD = 13
BACK = 14
DEVICES = SLABS * ORBS * POIS
TRANSPOSE_AXES = ("orb", "pois", "slab")
DT = 0.3
VMEM_LIMIT = 67043328

PITCH = 40
PLANES = WX + 2
PADDED = 8 + (PLANES + 2) * PITCH
GROUP = 24
HALF = COMPS // 2
FIRST = 8 + 2 * PITCH
f32, bf16 = jnp.float32, jnp.bfloat16


def _sines(n):
    k = np.arange(1, n + 1)
    return np.sin(np.pi * ((k[:, None] * k[None, :]) % (2 * (n + 1))) / (n + 1))


def _lam(n):
    return 2.0 - 2.0 * np.cos(np.pi * np.arange(1, n + 1) / (n + 1))


@functools.cache
def _tables():
    sx, sy = _sines(NX), _sines(NY)
    order = np.array([s * WX + 4 * xb + xi for xi in range(4) for s in range(SLABS) for xb in range(WX // 4)])
    padded = np.zeros((SLABS * 64, NX))
    for s in range(SLABS):
        padded[s * 64 : s * 64 + WX] = sx[s * WX : (s + 1) * WX]
    ring_x = np.zeros((16, NX))
    ring_y = np.zeros((16, NY))
    for s in range(SLABS):
        if s > 0:
            ring_x[s] = sx[s * WX - 1]
        if s < SLABS - 1:
            ring_x[8 + s] = sx[(s + 1) * WX]
    for p in range(POIS):
        if p > 0:
            ring_y[p] = sy[p * WY - 1]
        if p < POIS - 1:
            ring_y[8 + p] = sy[(p + 1) * WY]
    back_x = np.concatenate([sx[order], padded, ring_x])
    modes = np.stack([_lam(NZ), sy.sum(1)])
    cast = lambda a: np.asarray(a, np.float32)

    def split(a):
        high = cast(a).astype(ml_dtypes.bfloat16)
        return high, (cast(a) - high.astype(np.float32)).astype(ml_dtypes.bfloat16)

    def wide(a):
        high, low = split(a)
        return np.concatenate([high, high, low], 1)

    high, low = split(sy)
    tiles = [np.arange(128) % (NZ // ORBS) + o * (NZ // ORBS) for o in range(ORBS)]
    stacked = np.concatenate([high, high, low], 0)
    shift = np.eye(NZ, k=1) + np.eye(NZ, k=-1)
    return dict(
        near=shift.astype(ml_dtypes.bfloat16),
        beside=wide(sy),
        stacked=stacked,
        tiled=np.stack([stacked[:, t] for t in tiles]),
        forward_x=wide(sx[:, order]),
        back_x=wide(back_x),
        ring_y=wide(ring_y),
        col=cast(np.stack([_lam(NX), sx.sum(1)] + [np.zeros(NX)] * 6, 1)),
        row=cast(np.stack([_lam(NY), sy.sum(1)] + [np.zeros(NY)] * 6, 0)),
        modes=cast(modes),
    )


_VM = pl.BlockSpec(memory_space=pltpu.VMEM)
_SM = pl.BlockSpec(memory_space=pltpu.SMEM)
_ANY = pl.BlockSpec(memory_space=pl.ANY)
_HBM = pl.BlockSpec(memory_space=pltpu.HBM)
CORNERS = COMPS + 2
_X_FACE, _Y_FACE = (COMPS + 3, 2, WY, NZ), (COMPS + 2, 2, WX, NZ)
_FACES = [_X_FACE, _X_FACE, _Y_FACE, _Y_FACE]


def _iotas():
    return (
        lax.broadcasted_iota(jnp.int32, (8, 128), 0),
        lax.broadcasted_iota(jnp.int32, (8, 128), 1),
    )


def _zsum(v, lane):
    return jnp.where(lane == 0, 0.0, pltpu.roll(v, 1, 1)) + jnp.where(lane == 127, 0.0, pltpu.roll(v, 127, 1))


def _base(plane):
    return pl.multiple_of(8 + PITCH + PITCH * plane, 8)


def _split(value):
    high = value.astype(bf16)
    return high, (value - high.astype(f32)).astype(bf16)


def _faces_kernel(psi_hbm, ext, old, x_left, x_right, y_left, y_right, pot, psi, pots, rows, sems):
    copies = [pltpu.make_async_copy(psi_hbm.at[c], psi.at[c], sems.at[2 + c]) for c in range(COMPS)]
    copies = [pltpu.make_async_copy(ref, pots.at[k], sems.at[k]) for k, ref in enumerate((ext, old))] + copies
    for copy in copies:
        copy.start()
    for c in range(COMPS):
        copies[2 + c].wait()

        def fill(x, carry, c=c):
            start = pl.multiple_of(WY * x, WY)
            rows[0, pl.ds(pl.multiple_of(8 * x, 8), 8), :] = psi[c, pl.ds(start, 16), :].astype(f32)[0:8]
            rows[1, pl.ds(pl.multiple_of(8 * x, 8), 8), :] = psi[c, pl.ds(start + 16, 16), :].astype(f32)[8:16]
            return carry

        lax.fori_loop(0, WX, fill, 0, unroll=16)
        for d in range(2):
            x_left[c, d] = psi[c, WY * d : WY * (d + 1)]
            x_right[c, d] = psi[c, WY * (WX - 2 + d) : WY * (WX - 1 + d)]
        for half, ref, first in ((0, y_left, 0), (1, y_right, 6)):
            for d in range(2):
                ref[c, d] = rows[half, pl.ds(first + d, WX, 8), :].astype(bf16)
    for k in range(2):
        copies[k].wait()
        for ref, value in (
            (x_left, pots[k, 0:WY]),
            (x_right, pots[k, WY * (WX - 1) : WY * WX]),
            (y_left, pots[k, pl.ds(0, WX, WY), :]),
            (y_right, pots[k, pl.ds(WY - 1, WX, WY), :]),
        ):
            ref[COMPS + k, 0], ref[COMPS + k, 1] = _split(value)
    pot[...] = 6.0 + 2.0 * (pots[0] + pots[1])


def _faces(psi, ext, old):
    return pl.pallas_call(
        _faces_kernel,
        name="faces",
        in_specs=[_HBM] * 3,
        out_specs=[_VM] * 5,
        out_shape=[jax.ShapeDtypeStruct(s, bf16) for s in _FACES] + [jax.ShapeDtypeStruct((WX * WY, NZ), f32)],
        scratch_shapes=[
            pltpu.VMEM((COMPS, WX * WY, NZ), bf16),
            pltpu.VMEM((2, WX * WY, NZ), f32),
            pltpu.VMEM((2, 8 * WX, 128), f32),
            pltpu.SemaphoreType.DMA((2 + COMPS,)),
        ],
        compiler_params=pltpu.CompilerParams(vmem_limit_bytes=VMEM_LIMIT),
        cost_estimate=pl.CostEstimate(flops=1000000, bytes_accessed=6000000, transcendentals=0),
    )(psi, ext, old)


def _corners_kernel(x_left, x_right, low_first, low_last, high_first, high_last, after, left, right, block):
    del x_left, x_right, after
    for out, refs, row in ((left, (low_first, high_first), 0), (right, (low_last, high_last), 15)):
        for side in range(2):
            for c in range(COMPS):
                block[c : c + 1] = refs[side][c, 0].astype(f32)[row : row + 1]
            out[0, side] = block[...].astype(bf16)


def _corners(x_left, x_right, y_low, y_high, after):
    entry = pl.BlockSpec((1, 2, WY, NZ), lambda i: (CORNERS, 0, 0, 0))
    rows = lambda near, at: pl.BlockSpec((COMPS, 1, 16, NZ), lambda i: (0, near, at, 0))
    shape = jax.ShapeDtypeStruct(_X_FACE, bf16)
    return pl.pallas_call(
        _corners_kernel,
        name="corners",
        grid=(1,),
        in_specs=[entry, entry, rows(1, 0), rows(1, 2), rows(0, 0), rows(0, 2), _ANY],
        out_specs=[entry, entry],
        out_shape=[shape, shape],
        scratch_shapes=[pltpu.VMEM((WY, NZ), f32)],
        input_output_aliases={0: 0, 1: 1},
        compiler_params=pltpu.CompilerParams(vmem_limit_bytes=2 * 1024 * 1024),
        cost_estimate=pl.CostEstimate(flops=10000, bytes_accessed=200000, transcendentals=0),
    )(x_left, x_right, y_low, y_low, y_high, y_high, after)


def _inner_kernel(first_part, near, psi, pot, image, token, psi_f):
    token[...] = jnp.zeros((8, NZ), f32)
    for c in range(HALF):

        def widen(x, carry, c=c):
            rows = pl.ds(pl.multiple_of(WY * x, WY), WY)
            psi_f[c, pl.ds(_base(x + 1), WY)] = psi[first_part + c, rows].astype(f32)
            return carry

        lax.fori_loop(0, WX, widen, 0, unroll=16)
        for side in range(2):
            psi_f[c, pl.ds(FIRST + (WY if side else -1), WX, PITCH)] = jnp.zeros((WX, NZ), f32)
            psi_f[c, pl.ds(FIRST - PITCH + (WX + 1) * PITCH * side, WY)] = jnp.zeros((WY, NZ), f32)

    def group(k, carry):
        c, j = k // (WX // GROUP), k % (WX // GROUP)
        start = pl.multiple_of(GROUP * WY * j, WY)
        sums = jnp.dot(
            psi[first_part + c, pl.ds(start, GROUP * WY)], near[...], preferred_element_type=f32
        )
        for g in range(GROUP):
            base = _base(GROUP * j + g + 1)
            for i in range(4):
                at = base + 8 * i
                load = lambda row: psi_f[c, pl.ds(row, 8)]
                beside = (load(at - 1) + load(at + 1)) + (load(at - PITCH) + load(at + PITCH))
                first = WY * g + 8 * i
                weight = pot[pl.ds(pl.multiple_of(start + first, 8), 8)]
                value = weight * load(pl.multiple_of(at, 8)) - (beside + sums[first : first + 8])
                image[c, pl.ds(pl.multiple_of(at, 8), 8)] = value
        return carry

    lax.fori_loop(0, HALF * (WX // GROUP), group, 0)


def _inner(first_part, psi, pot):
    return pl.pallas_call(
        functools.partial(_inner_kernel, first_part),
        name="inner",
        in_specs=[_VM] * 3,
        out_specs=[_VM, _VM],
        out_shape=[jax.ShapeDtypeStruct((HALF, PADDED, NZ), f32), jax.ShapeDtypeStruct((8, NZ), f32)],
        scratch_shapes=[pltpu.VMEM((HALF, PADDED, NZ), f32)],
        compiler_params=pltpu.CompilerParams(vmem_limit_bytes=24 * 1024 * 1024),
        cost_estimate=pl.CostEstimate(flops=400000000, bytes_accessed=12000000, transcendentals=0),
    )(jnp.asarray(_tables()["near"]), psi, pot)


def _inside():
    slab, pois = lax.axis_index("slab"), lax.axis_index("pois")
    number = lambda cond: jnp.where(cond, 1.0, 0.0).astype(f32)
    return (
        (number(slab > 0), number(slab < SLABS - 1)),
        (number(pois > 0), number(pois < POIS - 1)),
    )


def _pair(ref, k):
    return ref[k, 0].astype(f32) + ref[k, 1].astype(f32)


def _stepped(cells, images, pot, orbital, at, lane):
    parts = []
    for k in range(2):
        load = lambda row, hint=True: images[k](pl.multiple_of(row, 8) if hint else row)
        u = load(at)
        total = (load(at - PITCH) + load(at + PITCH)) + (load(at - 1, False) + load(at + 1, False)) + _zsum(u, lane)
        parts.append((cells[k], u, pot * u - total))
    (a, ua, wa), (b, ub, wb) = parts
    scale = 0.125 * DT * DT
    return (a - scale * wa) + (0.5 * DT) * ub, (b - scale * wb) - (0.5 * DT) * ua


def _plane_charge(x, occ, psi, pot, halves, charge, totals, lane):
    for h in range(2):
        cells = [psi[c, pl.ds(pl.multiple_of(WY * x + 16 * h, 16), 16)].astype(f32) for c in range(COMPS)]
        for i in (2 * h, 2 * h + 1):
            r = slice(8 * (i % 2), 8 * (i % 2) + 8)
            row = pl.ds(pl.multiple_of(WY * x + 8 * i, 8), 8)
            weight = pot[row]
            sums = None
            for orbital in range(COMPS // 2):
                parts = (2 * orbital, 2 * orbital + 1)
                picked = [lambda at, c=c: halves[c // HALF][c % HALF, pl.ds(at, 8)] for c in parts]
                own = [cells[c][r] for c in parts]
                real, imag = _stepped(own, picked, weight, orbital, _base(x + 1) + 8 * i, lane)
                term = occ[orbital] * (real * real + imag * imag)
                sums = term if sums is None else sums + term
            charge[row, :] = sums
            totals = totals + sums
    return totals


def _middle_kernel(occupations, psi, pot, image_a, image_b, y_low, y_high, own_low, own_high, a, b, charge, totals, column):
    del image_a, image_b
    _, lane = _iotas()
    _, in_y = _inside()
    y_faces, own = (y_low, y_high), (own_low, own_high)
    ring_y = [6.0 + 2.0 * (_pair(f, COMPS) + _pair(f, COMPS + 1)) for f in y_faces]
    column[...] = jnp.zeros_like(column)
    for half, image in enumerate((a, b)):

        def edges(c, carry, half=half, image=image):
            part = HALF * half + c
            for side in range(2):
                near = y_faces[side][part, 1 - side].astype(f32) * in_y[side]
                far = y_faces[side][part, side].astype(f32)
                inner = own[side][part, side].astype(f32)
                at = pl.ds(FIRST + (WY - 1) * side, WX, PITCH)
                image[c, at] = image[c, at] - near
                column[side, 8:56] = near
                total = (far + inner) + (column[side, 7:55] + column[side, 9:57])
                value = [
                    ring_y[side][r] * near[r] - (total[r] + _zsum(near[r], lane))
                    for r in (slice(8 * i, 8 * i + 8) for i in range(WX // 8))
                ]
                image[c, pl.ds(FIRST + (WY if side else -1), WX, PITCH)] = jnp.concatenate(value, axis=0) * in_y[side]
            return carry

        lax.fori_loop(0, HALF, edges, 0)
    occ = [occupations[k] for k in range(COMPS // 2)]

    def pair(k, sums):
        for d in range(2):
            sums = _plane_charge(2 * k + d, occ, psi, pot, (a, b), charge, sums, lane)
        return sums

    totals[...] = lax.fori_loop(1, WX // 2 - 1, pair, jnp.zeros((8, 128), f32))


def _edge_kernel(
    occupations, beside, psi, pot, image_a, image_b, charge_in, totals, x_low, x_high, a, b, charge, message, column
):
    del image_a, image_b, charge_in
    _, lane = _iotas()
    in_x, in_y = _inside()
    x_faces = (x_low, x_high)
    ring_x = [6.0 + 2.0 * (_pair(f, COMPS) + _pair(f, COMPS + 1)) for f in x_faces]
    for i in range(2):
        for j in range(2):
            column[2 + 2 * i + j, 0:8] = x_faces[i][CORNERS, j].astype(f32)[0:8] * (in_x[i] * in_y[j])
    for half, image in enumerate((a, b)):

        def edges(c, carry, half=half, image=image):
            part = HALF * half + c
            for side in range(2):
                near = x_faces[side][part, 1 - side].astype(f32) * in_x[side]
                far = x_faces[side][part, side].astype(f32)
                inner = psi[part, pl.ds(WY * (WX - 1) * side, WY)].astype(f32)
                first = FIRST + PITCH * (WX - 1) * side
                image[c, pl.ds(first, WY)] = image[c, pl.ds(first, WY)] - near
                column[side, 8:40] = near
                for j, row in ((0, 7), (1, 40)):
                    corner = column[2 + 2 * side + j, pl.ds(part, 1)]
                    column[side, row : row + 1] = corner
                    at = pl.ds(first + (WY if j else -1), 1)
                    image[c, at] = image[c, at] - corner
                total = (far + inner) + (column[side, 7:39] + column[side, 9:41])
                for i in range(4):
                    r = slice(8 * i, 8 * i + 8)
                    ring = ring_x[side][r] * near[r] - (total[r] + _zsum(near[r], lane))
                    image[c, pl.ds(FIRST - PITCH + PITCH * (WX + 1) * side + 8 * i, 8)] = ring * in_x[side]
            return carry

        lax.fori_loop(0, HALF, edges, 0)
    occ = [occupations[k] for k in range(COMPS // 2)]

    def pair(k, sums):
        for d in range(2):
            x = (WX - 2) * k + d
            sums = _plane_charge(x, occ, psi, pot, (a, b), charge, sums, lane)
        return sums

    sums = lax.fori_loop(0, 2, pair, totals[...])
    mean = jnp.broadcast_to(jnp.sum(sums, keepdims=True) / (WX * WY * NZ), (8, 128))

    def group(g, carry):
        cells = charge[pl.ds(pl.multiple_of(128 * g, 128), 128), :] - mean[0:1]
        high, low = _split(cells)
        modes = lax.dot_general(
            beside[...],
            jnp.concatenate([high, low, high], axis=1),
            (((1,), (1,)), ((), ())),
            preferred_element_type=f32,
        )
        for k in range(16):
            message[pl.ds(8 * FWD * k + g, 8, FWD), :] = modes[8 * k : 8 * k + 8]
        return carry

    lax.fori_loop(0, WX // 4, group, 0, unroll=3)
    for k in range(16):
        message[pl.ds(8 * FWD * k + FWD - 1, 8, FWD), :] = mean


_HALF_IMAGE = jax.ShapeDtypeStruct((HALF, PADDED, NZ), f32)
_CHARGE = jax.ShapeDtypeStruct((WX * WY, NZ), f32)


def _middle(occupations, psi, pot, image_a, image_b, *faces):
    return pl.pallas_call(
        _middle_kernel,
        name="middle",
        in_specs=[_SM] + [_VM] * 8,
        out_specs=[_VM] * 4,
        out_shape=[_HALF_IMAGE, _HALF_IMAGE, _CHARGE, jax.ShapeDtypeStruct((8, NZ), f32)],
        scratch_shapes=[pltpu.VMEM((2, 64, NZ), f32)],
        input_output_aliases={3: 0, 4: 1},
        compiler_params=pltpu.CompilerParams(vmem_limit_bytes=16 * 1024 * 1024),
        cost_estimate=pl.CostEstimate(flops=100000000, bytes_accessed=8000000, transcendentals=0),
    )(occupations, psi, pot, image_a, image_b, *faces)


def _edge_messages(occupations, psi, pot, image_a, image_b, charge, totals, x_low, x_high):
    return pl.pallas_call(
        _edge_kernel,
        name="edge",
        in_specs=[_SM] + [_VM] * 9,
        out_specs=[_VM] * 4,
        out_shape=[_HALF_IMAGE, _HALF_IMAGE, _CHARGE, jax.ShapeDtypeStruct((DEVICES * FWD, 128), f32)],
        scratch_shapes=[pltpu.VMEM((6, 64, NZ), f32)],
        input_output_aliases={4: 0, 5: 1, 6: 2},
        compiler_params=pltpu.CompilerParams(vmem_limit_bytes=16 * 1024 * 1024),
        cost_estimate=pl.CostEstimate(flops=100000000, bytes_accessed=8000000, transcendentals=0),
    )(occupations, jnp.asarray(_tables()["beside"]), psi, pot, image_a, image_b, charge, totals, x_low, x_high)


def _swap_groups(blocks, group):
    out = []
    for i in range(4):
        value = None
        for j in range(4):
            shift = (32 * (j - i)) % 128
            moved = pltpu.roll(blocks[j], shift, 1) if shift else blocks[j]
            value = moved if value is None else jnp.where(group == j, moved, value)
        out.append(value)
    return out


def _plane_kernel(modes, recv, forward_x, stacked, back_x, ring_y, col, row, send, packed, block):
    dot = functools.partial(jnp.dot, preferred_element_type=f32)

    def parts(value, axis):
        high, low = _split(value)
        return jnp.concatenate([high, low, high], axis=axis)

    left = lambda table, value: dot(table[...], parts(value, 0))
    right = lambda value: dot(parts(value, 1), stacked[...])
    nt = lambda table, value: lax.dot_general(
        table[...], parts(value, 1), (((1,), (1,)), ((), ())), preferred_element_type=f32
    )
    kz = (lax.axis_index("orb") * POIS + lax.axis_index("pois")) * SLABS + lax.axis_index("slab")
    lam_z, sum_z = modes[0, kz], modes[1, kz]
    means = recv[pl.ds(FWD - 1, DEVICES, FWD), :]
    blocks = POIS * SLABS
    block_mean = sum(means[blocks * o : blocks * (o + 1)] for o in range(ORBS))
    mean = jnp.sum(block_mean, axis=0, keepdims=True) / blocks
    block_means = [block_mean[k : k + 1] for k in range(blocks)]
    for p in range(POIS):
        for s in range(SLABS):
            total = None
            for o in range(ORBS):
                part = recv[pl.ds(((o * POIS + p) * SLABS + s) * FWD, 12), :]
                total = part if total is None else total + part
            packed[p, pl.ds(12 * s, 12), :] = total + sum_z * (block_means[p * SLABS + s][0:1] - mean)
    group = lax.broadcasted_iota(jnp.int32, (WX, 128), 1) // 32
    plane = jnp.concatenate(_swap_groups([packed[p] for p in range(POIS)], group), axis=0)
    spectrum = right(left(forward_x, plane))
    divisor = col[:, 0:1] + row[0:1, :] + lam_z
    factor = 32.0 * math.pi / ((NX + 1) * (NY + 1) * (NZ + 1))
    scaled = spectrum * factor / divisor
    across = left(back_x, scaled)
    field = right(across[:NX])
    ring = right(across[NX + 256 :])
    cells = _swap_groups([field[WX * i : WX * (i + 1)] for i in range(4)], group)
    lane8 = lax.broadcasted_iota(jnp.int32, (8, 128), 1)
    group8 = lane8 // 32
    faces = [nt(ring_y, across[NX + 128 * h : NX + 128 * (h + 1)]) for h in range(2)]
    y_rows = []
    for s in range(SLABS):
        low, high = faces[s // 2][0:8], faces[s // 2][8:16]
        if s % 2 == 0:
            high = pltpu.roll(high, 64, 1)
        else:
            low = pltpu.roll(low, 64, 1)
        y_rows.append(jnp.where(lane8 < 64, low, high))
    for p in range(POIS):
        shift = lambda v, k: pltpu.roll(v, k % 128, 1) if k % 128 else v
        x_rows = jnp.where(
            group8 == 0,
            shift(ring[0:8], -32 * p),
            jnp.where(group8 == 1, shift(ring[8:16], 32 - 32 * p), 0.0),
        )
        for s in range(SLABS):
            base = (p * SLABS + s) * BACK
            block[pl.ds(base, 12), :] = cells[p][12 * s : 12 * s + 12]
            block[pl.ds(base + 12, 1), :] = x_rows[s : s + 1]
            block[pl.ds(base + 13, 1), :] = y_rows[s][p : p + 1]
    count = POIS * SLABS * BACK
    for o in range(ORBS):
        send[pl.ds(o * count, count), :] = block[...]


def _plane(recv):
    t = _tables()
    return pl.pallas_call(
        _plane_kernel,
        name="plane",
        in_specs=[_SM] + [_VM] * 7,
        out_specs=_VM,
        out_shape=jax.ShapeDtypeStruct((DEVICES * BACK, 128), f32),
        scratch_shapes=[
            pltpu.VMEM((POIS, WX, 128), f32),
            pltpu.VMEM((POIS * SLABS * BACK, 128), f32),
        ],
        compiler_params=pltpu.CompilerParams(vmem_limit_bytes=8 * 1024 * 1024),
        cost_estimate=pl.CostEstimate(flops=200000000, bytes_accessed=3000000, transcendentals=0),
    )(
        jnp.asarray(t["modes"]),
        recv,
        *(jnp.asarray(t[k]) for k in ("forward_x", "stacked", "back_x", "ring_y", "col", "row")),
    )


OUT_GROUP = 8


def _step_kernel(
    stacked, recv, tiled_hbm, image_a, image_b, psi, ext, old, x_low, x_high, y_low, y_high,
    new, hartree, image, pot, change, ring_y, tiled, slices, out, sem, out_sems,
):
    faces = (x_low, x_high, y_low, y_high)
    in_x, in_y = _inside()
    sub, lane = _iotas()
    tiled_copy = pltpu.make_async_copy(tiled_hbm.at[lax.axis_index("orb")], tiled, sem)
    tiled_copy.start()
    tiled_copy.wait()

    def back(r, table):
        high, low = _split(recv[pl.ds(r, 128, BACK), :])
        stack = jnp.concatenate([high, low, high], axis=0)
        return lax.dot_general(stack, table[...], (((0,), (0,)), ((), ())), preferred_element_type=f32)

    def planes(g, carry):
        field = back(g, stacked)
        first = pl.multiple_of(4 * WY * g, 8)
        block = pl.ds(first, 4 * WY)
        moved = pl.ds(pl.multiple_of(first + WY, 8), 4 * WY)
        pot[moved] = 6.0 + (2.0 * ext[block] + (old[block] + field))
        change[moved] = field - old[block]
        mine = back(g, tiled)
        for k in range(16):
            kept_lanes = jnp.where(lane // 16 == sub, mine[8 * k : 8 * k + 8], 0.0)
            slices[k % 4, pl.ds(4 * g + k // 4, 1), :] = jnp.sum(kept_lanes, axis=0, keepdims=True)
        return carry

    lax.fori_loop(0, WX // 4, planes, 0, unroll=2)
    x_field, y_field = back(12, stacked), back(13, stacked)
    for side in range(2):
        edge = pl.ds((WX + 1) * WY * side, WY)
        change[edge] = (x_field[32 * side : 32 * side + 32] - _pair(faces[side], COMPS + 1)) * in_x[side]
        ring_y[side] = (y_field[64 * side : 64 * side + WX] - _pair(faces[2 + side], COMPS + 1)) * in_y[side]
    for q in range(4):
        turned = jnp.transpose(slices[q])
        for y in range(8):
            hartree[8 * q + y] = turned[16 * y : 16 * y + 16, 0:WX]

    for half, start in enumerate((image_a, image_b)):

        def one(c, carry, half=half, start=start):
            part = HALF * half + c

            def planes_of(j, carry):
                for k in range(6):
                    x = 6 * j + k
                    value = psi[part, pl.ds(pl.multiple_of(WY * x, WY), WY)].astype(f32)
                    at = pl.ds(_base(x + 1), WY)
                    image[part, at] = start[c, at] + change[pl.ds(pl.multiple_of(WY * (x + 1), WY), WY)] * value
                return carry

            lax.fori_loop(0, WX // 6, planes_of, 0)
            for side in range(2):
                at = pl.ds(FIRST - PITCH + PITCH * (WX + 1) * side, WY)
                value = faces[side][part, 1 - side].astype(f32)
                image[part, at] = start[c, at] + change[pl.ds((WX + 1) * WY * side, WY)] * value
                at = pl.ds(FIRST + (WY if side else -1), WX, PITCH)
                image[part, at] = start[c, at] + ring_y[side] * faces[2 + side][part, 1 - side].astype(f32)
            return carry

        lax.fori_loop(0, HALF, one, 0)

    def out_copy(j, c):
        planes = pl.ds(OUT_GROUP * j, OUT_GROUP)
        return pltpu.make_async_copy(out.at[c, planes], new.at[c, planes], out_sems.at[j, c])

    def group(j, carry):
        def pair(k, carry):
            for d in range(2):
                x = OUT_GROUP * j + 2 * k + d
                for h in range(2):
                    rows = pl.ds(pl.multiple_of(WY * x + 16 * h, 16), 16)
                    cells = [psi[c, rows].astype(f32) for c in range(COMPS)]
                    for i in (2 * h, 2 * h + 1):
                        r = slice(8 * (i % 2), 8 * (i % 2) + 8)
                        weight = pot[pl.ds(pl.multiple_of(WY * (x + 1) + 8 * i, 8), 8)]
                        for orbital in range(COMPS // 2):
                            parts = (2 * orbital, 2 * orbital + 1)
                            picked = [lambda row, c=c: image[c, pl.ds(row, 8)] for c in parts]
                            own = [cells[c][r] for c in parts]
                            real, imag = _stepped(own, picked, weight, orbital, _base(x + 1) + 8 * i, lane)
                            out[2 * orbital, x, 8 * i : 8 * i + 8] = real
                            out[2 * orbital + 1, x, 8 * i : 8 * i + 8] = imag
            return carry

        lax.fori_loop(0, OUT_GROUP // 2, pair, 0)
        for c in range(COMPS):
            out_copy(j, c).start()
        return carry

    lax.fori_loop(0, WX // OUT_GROUP, group, 0)
    for j in range(WX // OUT_GROUP):
        for c in range(COMPS):
            out_copy(j, c).wait()


def _step(recv, *arrays):
    t = _tables()
    return pl.pallas_call(
        _step_kernel,
        name="step",
        in_specs=[_VM, _VM, _HBM] + [_VM] * len(arrays),
        out_specs=[_HBM, _VM],
        out_shape=[
            jax.ShapeDtypeStruct((COMPS, WX, WY, NZ), f32),
            jax.ShapeDtypeStruct((WY, NZ // ORBS, WX), f32),
        ],
        scratch_shapes=[
            pltpu.VMEM((COMPS, PADDED, NZ), f32),
            pltpu.VMEM((PLANES * WY, NZ), f32),
            pltpu.VMEM((PLANES * WY, NZ), f32),
            pltpu.VMEM((2, WX, NZ), f32),
            pltpu.VMEM((3 * NZ, 128), bf16),
            pltpu.VMEM((4, 128, 128), f32),
            pltpu.VMEM((COMPS, WX, WY, NZ), f32),
            pltpu.SemaphoreType.DMA,
            pltpu.SemaphoreType.DMA((WX // OUT_GROUP, COMPS)),
        ],
        compiler_params=pltpu.CompilerParams(vmem_limit_bytes=24 * 1024 * 1024),
        cost_estimate=pl.CostEstimate(flops=100000000, bytes_accessed=20000000, transcendentals=0),
    )(jnp.asarray(t["stacked"]), recv, jnp.asarray(t["tiled"]), *arrays)


def _shifted(value, axis, count, step):
    return lax.ppermute(value, axis, [(i, (i + step) % count) for i in range(count)])


def _swap(messages, rows):
    moved = lax.all_to_all(messages.reshape(DEVICES, 1, rows * 128), TRANSPOSE_AXES, 0, 0)
    return moved.reshape(DEVICES * rows, 128)


def body(orbitals, occupations, ext_pot, hartree_old):
    psi = orbitals.reshape(COMPS, WX * WY, NZ)
    ext, old = ext_pot.reshape(WX * WY, NZ), hartree_old.reshape(WX * WY, NZ)
    x_left, x_right, y_left, y_right, pot = _faces(psi, ext, old)
    y_low = _shifted(y_right, "pois", POIS, 1)
    y_high = _shifted(y_left, "pois", POIS, -1)
    image_a, done = _inner(0, psi, pot)
    x_left, x_right = _corners(x_left, x_right, y_low, y_high, done)
    x_low = _shifted(x_right, "slab", SLABS, 1)
    x_high = _shifted(x_left, "slab", SLABS, -1)
    image_b, _ = _inner(HALF, psi, pot)
    image_a, image_b, charge, totals = _middle(occupations, psi, pot, image_a, image_b, y_low, y_high, y_left, y_right)
    image_a, image_b, _, message = _edge_messages(
        occupations, psi, pot, image_a, image_b, charge, totals, x_low, x_high
    )
    faces = (x_low, x_high, y_low, y_high)
    back = _swap(_plane(_swap(message, FWD)), BACK)
    new, hartree = _step(back, image_a, image_b, psi, ext, old, *faces)
    return new.reshape(orbitals.shape), jnp.transpose(hartree, (2, 0, 1))


def solution(mesh):
    placed = (P("orb", None, "slab", "pois", None), P("orb"), P("slab", "pois", None), P("slab", "pois", None))
    return jax.shard_map(
        body,
        mesh=mesh,
        in_specs=placed,
        out_specs=(P("orb", None, "slab", "pois", None), P("slab", "pois", "orb")),
        check_vma=False,
    )
```

```python
import functools
import math

import jax
import jax.numpy as jnp
import ml_dtypes
import numpy as np
from jax import lax
from jax.experimental import pallas as pl
from jax.experimental.pallas import tpu as pltpu
from jax.sharding import PartitionSpec as P

NX, NY, NZ = 192, 128, 128
SLABS, ORBS, POIS = 4, 8, 4
WX, WY = NX // SLABS, NY // POIS
COMPS = 8
FWD = 13
BACK = 14
DEVICES = SLABS * ORBS * POIS
TRANSPOSE_AXES = ("orb", "pois", "slab")
DT = 0.3
VMEM_LIMIT = 67043328

PITCH = 40
PLANES = WX + 2
PADDED = 8 + (PLANES + 2) * PITCH
GROUP = 24
HALF = COMPS // 2
FIRST = 8 + 2 * PITCH
f32, bf16 = jnp.float32, jnp.bfloat16


def _sines(n):
    k = np.arange(1, n + 1)
    return np.sin(np.pi * ((k[:, None] * k[None, :]) % (2 * (n + 1))) / (n + 1))


def _lam(n):
    return 2.0 - 2.0 * np.cos(np.pi * np.arange(1, n + 1) / (n + 1))


@functools.cache
def _tables():
    sx, sy = _sines(NX), _sines(NY)
    order = np.array([s * WX + 4 * xb + xi for xi in range(4) for s in range(SLABS) for xb in range(WX // 4)])
    padded = np.zeros((SLABS * 64, NX))
    for s in range(SLABS):
        padded[s * 64 : s * 64 + WX] = sx[s * WX : (s + 1) * WX]
    ring_x = np.zeros((16, NX))
    ring_y = np.zeros((16, NY))
    for s in range(SLABS):
        if s > 0:
            ring_x[s] = sx[s * WX - 1]
        if s < SLABS - 1:
            ring_x[8 + s] = sx[(s + 1) * WX]
    for p in range(POIS):
        if p > 0:
            ring_y[p] = sy[p * WY - 1]
        if p < POIS - 1:
            ring_y[8 + p] = sy[(p + 1) * WY]
    back_x = np.concatenate([sx[order], padded, ring_x])
    modes = np.stack([_lam(NZ), sy.sum(1)])
    cast = lambda a: np.asarray(a, np.float32)

    def split(a):
        high = cast(a).astype(ml_dtypes.bfloat16)
        return high, (cast(a) - high.astype(np.float32)).astype(ml_dtypes.bfloat16)

    def wide(a):
        high, low = split(a)
        return np.concatenate([high, high, low], 1)

    high, low = split(sy)
    tiles = [np.arange(128) % (NZ // ORBS) + o * (NZ // ORBS) for o in range(ORBS)]
    stacked = np.concatenate([high, high, low], 0)
    shift = np.eye(NZ, k=1) + np.eye(NZ, k=-1)
    return dict(
        near=shift.astype(ml_dtypes.bfloat16),
        beside=wide(sy),
        stacked=stacked,
        tiled=np.stack([stacked[:, t] for t in tiles]),
        forward_x=wide(sx[:, order]),
        back_x=wide(back_x),
        ring_y=wide(ring_y),
        col=cast(np.stack([_lam(NX), sx.sum(1)] + [np.zeros(NX)] * 6, 1)),
        row=cast(np.stack([_lam(NY), sy.sum(1)] + [np.zeros(NY)] * 6, 0)),
        modes=cast(modes),
    )


_VM = pl.BlockSpec(memory_space=pltpu.VMEM)
_SM = pl.BlockSpec(memory_space=pltpu.SMEM)
_ANY = pl.BlockSpec(memory_space=pl.ANY)
_HBM = pl.BlockSpec(memory_space=pltpu.HBM)
CORNERS = COMPS + 2
_X_FACE, _Y_FACE = (COMPS + 3, 2, WY, NZ), (COMPS + 2, 2, WX, NZ)
_FACES = [_X_FACE, _X_FACE, _Y_FACE, _Y_FACE]


def _iotas():
    return (
        lax.broadcasted_iota(jnp.int32, (8, 128), 0),
        lax.broadcasted_iota(jnp.int32, (8, 128), 1),
    )


def _zsum(v, lane):
    return jnp.where(lane == 0, 0.0, pltpu.roll(v, 1, 1)) + jnp.where(lane == 127, 0.0, pltpu.roll(v, 127, 1))


def _base(plane):
    return pl.multiple_of(8 + PITCH + PITCH * plane, 8)


def _split(value):
    high = value.astype(bf16)
    return high, (value - high.astype(f32)).astype(bf16)


def _faces_kernel(psi_hbm, ext, old, x_left, x_right, y_left, y_right, pot, psi, pots, rows, sems):
    copies = [pltpu.make_async_copy(psi_hbm.at[c], psi.at[c], sems.at[2 + c]) for c in range(COMPS)]
    copies = [pltpu.make_async_copy(ref, pots.at[k], sems.at[k]) for k, ref in enumerate((ext, old))] + copies
    for copy in copies:
        copy.start()
    for c in range(COMPS):
        copies[2 + c].wait()

        def fill(x, carry, c=c):
            start = pl.multiple_of(WY * x, WY)
            rows[0, pl.ds(pl.multiple_of(8 * x, 8), 8), :] = psi[c, pl.ds(start, 16), :].astype(f32)[0:8]
            rows[1, pl.ds(pl.multiple_of(8 * x, 8), 8), :] = psi[c, pl.ds(start + 16, 16), :].astype(f32)[8:16]
            return carry

        lax.fori_loop(0, WX, fill, 0, unroll=WX)
        for d in range(2):
            x_left[c, d] = psi[c, WY * d : WY * (d + 1)]
            x_right[c, d] = psi[c, WY * (WX - 2 + d) : WY * (WX - 1 + d)]
        for half, ref, first in ((0, y_left, 0), (1, y_right, 6)):
            for d in range(2):
                ref[c, d] = rows[half, pl.ds(first + d, WX, 8), :].astype(bf16)
    for k in range(2):
        copies[k].wait()
        for ref, value in (
            (x_left, pots[k, 0:WY]),
            (x_right, pots[k, WY * (WX - 1) : WY * WX]),
            (y_left, pots[k, pl.ds(0, WX, WY), :]),
            (y_right, pots[k, pl.ds(WY - 1, WX, WY), :]),
        ):
            ref[COMPS + k, 0], ref[COMPS + k, 1] = _split(value)
    pot[...] = 6.0 + 2.0 * (pots[0] + pots[1])


def _faces(psi, ext, old):
    return pl.pallas_call(
        _faces_kernel,
        name="faces",
        in_specs=[_HBM] * 3,
        out_specs=[_VM] * 5,
        out_shape=[jax.ShapeDtypeStruct(s, bf16) for s in _FACES] + [jax.ShapeDtypeStruct((WX * WY, NZ), f32)],
        scratch_shapes=[
            pltpu.VMEM((COMPS, WX * WY, NZ), bf16),
            pltpu.VMEM((2, WX * WY, NZ), f32),
            pltpu.VMEM((2, 8 * WX, 128), f32),
            pltpu.SemaphoreType.DMA((2 + COMPS,)),
        ],
        compiler_params=pltpu.CompilerParams(vmem_limit_bytes=VMEM_LIMIT),
        cost_estimate=pl.CostEstimate(flops=1000000, bytes_accessed=6000000, transcendentals=0),
    )(psi, ext, old)


def _corners_kernel(x_left, x_right, y_low, y_high, after, left, right, block, entry, sems):
    del x_left, x_right, after
    copies = []
    for k, (out, first, row) in enumerate(((left, 0, 0), (right, WX - 16, 15))):
        for side, ref in enumerate((y_low, y_high)):
            for c in range(COMPS):
                cells = ref[c, 1 - side, first : first + 16].astype(f32)
                block[c : c + 1] = cells[row : row + 1]
            entry[k, side] = block[...].astype(bf16)
        copies.append(pltpu.make_async_copy(entry.at[k], out.at[CORNERS], sems.at[k]))
        copies[k].start()
    for copy in copies:
        copy.wait()


def _corners(x_left, x_right, y_low, y_high, after):
    shape = jax.ShapeDtypeStruct(_X_FACE, bf16)
    return pl.pallas_call(
        _corners_kernel,
        name="corners",
        in_specs=[_ANY, _ANY, _VM, _VM, _ANY],
        out_specs=[_ANY, _ANY],
        out_shape=[shape, shape],
        scratch_shapes=[
            pltpu.VMEM((WY, NZ), f32),
            pltpu.VMEM((2, 2, WY, NZ), bf16),
            pltpu.SemaphoreType.DMA((2,)),
        ],
        input_output_aliases={0: 0, 1: 1},
        compiler_params=pltpu.CompilerParams(vmem_limit_bytes=2 * 1024 * 1024),
        cost_estimate=pl.CostEstimate(flops=10000, bytes_accessed=200000, transcendentals=0),
    )(x_left, x_right, y_low, y_high, after)


def _inner_kernel(first_part, near, psi, pot, image, token, psi_f):
    token[...] = jnp.zeros((8, NZ), f32)
    for c in range(HALF):

        def widen(x, carry, c=c):
            rows = pl.ds(pl.multiple_of(WY * x, WY), WY)
            psi_f[c, pl.ds(_base(x + 1), WY)] = psi[first_part + c, rows].astype(f32)
            return carry

        lax.fori_loop(0, WX, widen, 0, unroll=16)
        for side in range(2):
            psi_f[c, pl.ds(FIRST + (WY if side else -1), WX, PITCH)] = jnp.zeros((WX, NZ), f32)
            psi_f[c, pl.ds(FIRST - PITCH + (WX + 1) * PITCH * side, WY)] = jnp.zeros((WY, NZ), f32)

    def group(k, carry):
        c, j = k // (WX // GROUP), k % (WX // GROUP)
        start = pl.multiple_of(GROUP * WY * j, WY)
        sums = jnp.dot(
            psi[first_part + c, pl.ds(start, GROUP * WY)], near[...], preferred_element_type=f32
        )
        for g in range(GROUP):
            base = _base(GROUP * j + g + 1)
            for i in range(4):
                at = base + 8 * i
                load = lambda row: psi_f[c, pl.ds(row, 8)]
                beside = (load(at - 1) + load(at + 1)) + (load(at - PITCH) + load(at + PITCH))
                first = WY * g + 8 * i
                weight = pot[pl.ds(pl.multiple_of(start + first, 8), 8)]
                value = weight * load(pl.multiple_of(at, 8)) - (beside + sums[first : first + 8])
                image[c, pl.ds(pl.multiple_of(at, 8), 8)] = value
        return carry

    lax.fori_loop(0, HALF * (WX // GROUP), group, 0)


def _inner(first_part, psi, pot):
    return pl.pallas_call(
        functools.partial(_inner_kernel, first_part),
        name="inner",
        in_specs=[_VM] * 3,
        out_specs=[_VM, _VM],
        out_shape=[jax.ShapeDtypeStruct((HALF, PADDED, NZ), f32), jax.ShapeDtypeStruct((8, NZ), f32)],
        scratch_shapes=[pltpu.VMEM((HALF, PADDED, NZ), f32)],
        compiler_params=pltpu.CompilerParams(vmem_limit_bytes=24 * 1024 * 1024),
        cost_estimate=pl.CostEstimate(flops=400000000, bytes_accessed=12000000, transcendentals=0),
    )(jnp.asarray(_tables()["near"]), psi, pot)


def _inside():
    slab, pois = lax.axis_index("slab"), lax.axis_index("pois")
    number = lambda cond: jnp.where(cond, 1.0, 0.0).astype(f32)
    return (
        (number(slab > 0), number(slab < SLABS - 1)),
        (number(pois > 0), number(pois < POIS - 1)),
    )


def _pair(ref, k):
    return ref[k, 0].astype(f32) + ref[k, 1].astype(f32)


def _stepped(cells, images, pot, orbital, at, lane):
    parts = []
    for k in range(2):
        load = lambda row, hint=True: images[k](pl.multiple_of(row, 8) if hint else row)
        u = load(at)
        total = (load(at - PITCH) + load(at + PITCH)) + (load(at - 1, False) + load(at + 1, False)) + _zsum(u, lane)
        parts.append((cells[k], u, pot * u - total))
    (a, ua, wa), (b, ub, wb) = parts
    scale = 0.125 * DT * DT
    return (a - scale * wa) + (0.5 * DT) * ub, (b - scale * wb) - (0.5 * DT) * ua


def _plane_charge(x, occ, psi, pot, halves, charge, totals, lane):
    for h in range(2):
        cells = [psi[c, pl.ds(pl.multiple_of(WY * x + 16 * h, 16), 16)].astype(f32) for c in range(COMPS)]
        for i in (2 * h, 2 * h + 1):
            r = slice(8 * (i % 2), 8 * (i % 2) + 8)
            row = pl.ds(pl.multiple_of(WY * x + 8 * i, 8), 8)
            weight = pot[row]
            sums = None
            for orbital in range(COMPS // 2):
                parts = (2 * orbital, 2 * orbital + 1)
                picked = [lambda at, c=c: halves[c // HALF][c % HALF, pl.ds(at, 8)] for c in parts]
                own = [cells[c][r] for c in parts]
                real, imag = _stepped(own, picked, weight, orbital, _base(x + 1) + 8 * i, lane)
                term = occ[orbital] * (real * real + imag * imag)
                sums = term if sums is None else sums + term
            charge[row, :] = sums
            totals = totals + sums
    return totals


def _middle_kernel(occupations, psi, pot, image_a, image_b, y_low, y_high, own_low, own_high, a, b, charge, totals, column):
    del image_a, image_b
    _, lane = _iotas()
    _, in_y = _inside()
    y_faces, own = (y_low, y_high), (own_low, own_high)
    ring_y = [6.0 + 2.0 * (_pair(f, COMPS) + _pair(f, COMPS + 1)) for f in y_faces]
    column[...] = jnp.zeros_like(column)
    for half, image in enumerate((a, b)):

        def edges(c, carry, half=half, image=image):
            part = HALF * half + c
            for side in range(2):
                near = y_faces[side][part, 1 - side].astype(f32) * in_y[side]
                far = y_faces[side][part, side].astype(f32)
                inner = own[side][part, side].astype(f32)
                at = pl.ds(FIRST + (WY - 1) * side, WX, PITCH)
                image[c, at] = image[c, at] - near
                column[side, 8:56] = near
                total = (far + inner) + (column[side, 7:55] + column[side, 9:57])
                value = [
                    ring_y[side][r] * near[r] - (total[r] + _zsum(near[r], lane))
                    for r in (slice(8 * i, 8 * i + 8) for i in range(WX // 8))
                ]
                image[c, pl.ds(FIRST + (WY if side else -1), WX, PITCH)] = jnp.concatenate(value, axis=0) * in_y[side]
            return carry

        lax.fori_loop(0, HALF, edges, 0)
    occ = [occupations[k] for k in range(COMPS // 2)]

    def pair(k, sums):
        for d in range(2):
            sums = _plane_charge(2 * k + d, occ, psi, pot, (a, b), charge, sums, lane)
        return sums

    totals[...] = lax.fori_loop(1, WX // 2 - 1, pair, jnp.zeros((8, 128), f32))


def _edge_kernel(
    occupations, beside, psi, pot, image_a, image_b, charge_in, totals, x_low, x_high, a, b, charge, message, column
):
    del image_a, image_b, charge_in
    _, lane = _iotas()
    in_x, in_y = _inside()
    x_faces = (x_low, x_high)
    ring_x = [6.0 + 2.0 * (_pair(f, COMPS) + _pair(f, COMPS + 1)) for f in x_faces]
    for i in range(2):
        for j in range(2):
            column[2 + 2 * i + j, 0:8] = x_faces[i][CORNERS, j].astype(f32)[0:8] * (in_x[i] * in_y[j])
    for half, image in enumerate((a, b)):

        def edges(c, carry, half=half, image=image):
            part = HALF * half + c
            for side in range(2):
                near = x_faces[side][part, 1 - side].astype(f32) * in_x[side]
                far = x_faces[side][part, side].astype(f32)
                inner = psi[part, pl.ds(WY * (WX - 1) * side, WY)].astype(f32)
                first = FIRST + PITCH * (WX - 1) * side
                image[c, pl.ds(first, WY)] = image[c, pl.ds(first, WY)] - near
                column[side, 8:40] = near
                for j, row in ((0, 7), (1, 40)):
                    corner = column[2 + 2 * side + j, pl.ds(part, 1)]
                    column[side, row : row + 1] = corner
                    at = pl.ds(first + (WY if j else -1), 1)
                    image[c, at] = image[c, at] - corner
                total = (far + inner) + (column[side, 7:39] + column[side, 9:41])
                for i in range(4):
                    r = slice(8 * i, 8 * i + 8)
                    ring = ring_x[side][r] * near[r] - (total[r] + _zsum(near[r], lane))
                    image[c, pl.ds(FIRST - PITCH + PITCH * (WX + 1) * side + 8 * i, 8)] = ring * in_x[side]
            return carry

        lax.fori_loop(0, HALF, edges, 0)
    occ = [occupations[k] for k in range(COMPS // 2)]

    def pair(k, sums):
        for d in range(2):
            x = (WX - 2) * k + d
            sums = _plane_charge(x, occ, psi, pot, (a, b), charge, sums, lane)
        return sums

    sums = lax.fori_loop(0, 2, pair, totals[...])
    mean = jnp.broadcast_to(jnp.sum(sums, keepdims=True) / (WX * WY * NZ), (8, 128))

    def group(g, carry):
        cells = charge[pl.ds(pl.multiple_of(256 * g, 256), 256), :] - mean[0:1]
        high, low = _split(cells)
        modes = lax.dot_general(
            beside[...],
            jnp.concatenate([high, low, high], axis=1),
            (((1,), (1,)), ((), ())),
            preferred_element_type=f32,
        )
        for k in range(16):
            for h in range(2):
                piece = modes[8 * k : 8 * k + 8, 128 * h : 128 * h + 128]
                message[pl.ds(8 * FWD * k + 2 * g + h, 8, FWD), :] = piece
        return carry

    lax.fori_loop(0, WX // 8, group, 0, unroll=2)
    for k in range(16):
        message[pl.ds(8 * FWD * k + FWD - 1, 8, FWD), :] = mean


_HALF_IMAGE = jax.ShapeDtypeStruct((HALF, PADDED, NZ), f32)
_CHARGE = jax.ShapeDtypeStruct((WX * WY, NZ), f32)


def _middle(occupations, psi, pot, image_a, image_b, *faces):
    return pl.pallas_call(
        _middle_kernel,
        name="middle",
        in_specs=[_SM] + [_VM] * 8,
        out_specs=[_VM] * 4,
        out_shape=[_HALF_IMAGE, _HALF_IMAGE, _CHARGE, jax.ShapeDtypeStruct((8, NZ), f32)],
        scratch_shapes=[pltpu.VMEM((2, 64, NZ), f32)],
        input_output_aliases={3: 0, 4: 1},
        compiler_params=pltpu.CompilerParams(vmem_limit_bytes=16 * 1024 * 1024),
        cost_estimate=pl.CostEstimate(flops=100000000, bytes_accessed=8000000, transcendentals=0),
    )(occupations, psi, pot, image_a, image_b, *faces)


def _edge_messages(occupations, psi, pot, image_a, image_b, charge, totals, x_low, x_high):
    return pl.pallas_call(
        _edge_kernel,
        name="edge",
        in_specs=[_SM] + [_VM] * 9,
        out_specs=[_VM] * 4,
        out_shape=[_HALF_IMAGE, _HALF_IMAGE, _CHARGE, jax.ShapeDtypeStruct((DEVICES * FWD, 128), f32)],
        scratch_shapes=[pltpu.VMEM((6, 64, NZ), f32)],
        input_output_aliases={4: 0, 5: 1, 6: 2},
        compiler_params=pltpu.CompilerParams(vmem_limit_bytes=16 * 1024 * 1024),
        cost_estimate=pl.CostEstimate(flops=100000000, bytes_accessed=8000000, transcendentals=0),
    )(occupations, jnp.asarray(_tables()["beside"]), psi, pot, image_a, image_b, charge, totals, x_low, x_high)


def _swap_groups(blocks, group):
    out = []
    for i in range(4):
        value = None
        for j in range(4):
            shift = (32 * (j - i)) % 128
            moved = pltpu.roll(blocks[j], shift, 1) if shift else blocks[j]
            value = moved if value is None else jnp.where(group == j, moved, value)
        out.append(value)
    return out


def _plane_kernel(modes, recv, forward_x, stacked, back_x, ring_y, col, row, send, packed, block):
    dot = functools.partial(jnp.dot, preferred_element_type=f32)

    def parts(value, axis):
        high, low = _split(value)
        return jnp.concatenate([high, low, high], axis=axis)

    left = lambda table, value: dot(table[...], parts(value, 0))
    right = lambda value: dot(parts(value, 1), stacked[...])
    nt = lambda table, value: lax.dot_general(
        table[...], parts(value, 1), (((1,), (1,)), ((), ())), preferred_element_type=f32
    )
    kz = (lax.axis_index("orb") * POIS + lax.axis_index("pois")) * SLABS + lax.axis_index("slab")
    lam_z, sum_z = modes[0, kz], modes[1, kz]
    means = recv[pl.ds(FWD - 1, DEVICES, FWD), :]
    blocks = POIS * SLABS
    block_mean = sum(means[blocks * o : blocks * (o + 1)] for o in range(ORBS))
    mean = jnp.sum(block_mean, axis=0, keepdims=True) / blocks
    block_means = [block_mean[k : k + 1] for k in range(blocks)]
    for p in range(POIS):
        for s in range(SLABS):
            first = [((o * POIS + p) * SLABS + s) * FWD for o in range(ORBS)]
            shift = sum_z * (block_means[p * SLABS + s][0:1] - mean)
            packed[p, pl.ds(12 * s, 8), :] = sum(recv[pl.ds(r, 8), :] for r in first) + shift
            last = sum(recv[pl.ds(r + FWD - 8, 8), :] for r in first) + shift
            packed[p, pl.ds(12 * s + 8, 4), :] = last[3:7]
    group = lax.broadcasted_iota(jnp.int32, (WX, 128), 1) // 32
    plane = jnp.concatenate(_swap_groups([packed[p, 0:WX] for p in range(POIS)], group), axis=0)
    spectrum = right(left(forward_x, plane))
    divisor = col[:, 0:1] + row[0:1, :] + lam_z
    factor = 32.0 * math.pi / ((NX + 1) * (NY + 1) * (NZ + 1))
    scaled = spectrum * factor / divisor
    across = left(back_x, scaled)
    field = right(across[:NX])
    ring = right(across[NX + 256 :])
    cells = _swap_groups([field[WX * i : WX * (i + 1)] for i in range(4)], group)
    lane8 = lax.broadcasted_iota(jnp.int32, (8, 128), 1)
    group8 = lane8 // 32
    faces = [nt(ring_y, across[NX + 128 * h : NX + 128 * (h + 1)]) for h in range(2)]
    y_rows = []
    for s in range(SLABS):
        low, high = faces[s // 2][0:8], faces[s // 2][8:16]
        if s % 2 == 0:
            high = pltpu.roll(high, 64, 1)
        else:
            low = pltpu.roll(low, 64, 1)
        y_rows.append(jnp.where(lane8 < 64, low, high))
    for p in range(POIS):
        shift = lambda v, k: pltpu.roll(v, k % 128, 1) if k % 128 else v
        x_rows = jnp.where(
            group8 == 0,
            shift(ring[0:8], -32 * p),
            jnp.where(group8 == 1, shift(ring[8:16], 32 - 32 * p), 0.0),
        )
        for s in range(SLABS):
            base = (p * SLABS + s) * BACK
            block[pl.ds(base, 12), :] = cells[p][12 * s : 12 * s + 12]
            block[pl.ds(base + 12, 1), :] = x_rows[s : s + 1]
            block[pl.ds(base + 13, 1), :] = y_rows[s][p : p + 1]
    count = POIS * SLABS * BACK
    for o in range(ORBS):
        send[pl.ds(o * count, count), :] = block[0:count]


def _plane(recv):
    t = _tables()
    return pl.pallas_call(
        _plane_kernel,
        name="plane",
        in_specs=[_SM] + [_VM] * 7,
        out_specs=_VM,
        out_shape=jax.ShapeDtypeStruct((DEVICES * BACK, 128), f32),
        scratch_shapes=[
            pltpu.VMEM((POIS, WX + 8, 128), f32),
            pltpu.VMEM((POIS * SLABS * BACK + 16, 128), f32),
        ],
        compiler_params=pltpu.CompilerParams(vmem_limit_bytes=8 * 1024 * 1024),
        cost_estimate=pl.CostEstimate(flops=200000000, bytes_accessed=3000000, transcendentals=0),
    )(
        jnp.asarray(t["modes"]),
        recv,
        *(jnp.asarray(t[k]) for k in ("forward_x", "stacked", "back_x", "ring_y", "col", "row")),
    )


OUT_GROUP = 4


def _step_kernel(
    stacked, recv, tiled, image_a, image_b, psi, ext, old, x_low, x_high, y_low, y_high,
    new, hartree, image, pot, change, ring_y, tables, slices, out, out_sems,
):
    faces = (x_low, x_high, y_low, y_high)
    in_x, in_y = _inside()
    sub, lane = _iotas()
    tables[:, 0:128] = stacked[...]
    tables[:, 128:256] = tiled[lax.axis_index("orb")]

    def back(r, table):
        high, low = _split(recv[pl.ds(r, 128, BACK), :])
        stack = jnp.concatenate([high, low, high], axis=0)
        return lax.dot_general(stack, table[...], (((0,), (0,)), ((), ())), preferred_element_type=f32)

    def planes(g, carry):
        both = back(g, tables)
        field, mine = both[:, 0:128], both[:, 128:256]
        first = pl.multiple_of(4 * WY * g, 8)
        block = pl.ds(first, 4 * WY)
        moved = pl.ds(pl.multiple_of(first + WY, 8), 4 * WY)
        pot[moved] = 6.0 + (2.0 * ext[block] + (old[block] + field))
        change[moved] = field - old[block]
        for k in range(16):
            kept_lanes = jnp.where(lane // 16 == sub, mine[8 * k : 8 * k + 8], 0.0)
            slices[k % 4, pl.ds(4 * g + k // 4, 1), :] = jnp.sum(kept_lanes, axis=0, keepdims=True)
        return carry

    lax.fori_loop(0, WX // 4, planes, 0, unroll=2)
    x_field, y_field = back(12, stacked), back(13, stacked)
    for side in range(2):
        edge = pl.ds((WX + 1) * WY * side, WY)
        change[edge] = (x_field[32 * side : 32 * side + 32] - _pair(faces[side], COMPS + 1)) * in_x[side]
        ring_y[side] = (y_field[64 * side : 64 * side + WX] - _pair(faces[2 + side], COMPS + 1)) * in_y[side]
    for q in range(4):
        turned = jnp.transpose(slices[q])
        for y in range(8):
            hartree[8 * q + y] = turned[16 * y : 16 * y + 16, 0:WX]

    for half, start in enumerate((image_a, image_b)):

        def one(c, carry, half=half, start=start):
            part = HALF * half + c

            def planes_of(j, carry):
                for k in range(6):
                    x = 6 * j + k
                    value = psi[part, pl.ds(pl.multiple_of(WY * x, WY), WY)].astype(f32)
                    at = pl.ds(_base(x + 1), WY)
                    image[part, at] = start[c, at] + change[pl.ds(pl.multiple_of(WY * (x + 1), WY), WY)] * value
                return carry

            lax.fori_loop(0, WX // 6, planes_of, 0)
            for side in range(2):
                at = pl.ds(FIRST - PITCH + PITCH * (WX + 1) * side, WY)
                value = faces[side][part, 1 - side].astype(f32)
                image[part, at] = start[c, at] + change[pl.ds((WX + 1) * WY * side, WY)] * value
                at = pl.ds(FIRST + (WY if side else -1), WX, PITCH)
                image[part, at] = start[c, at] + ring_y[side] * faces[2 + side][part, 1 - side].astype(f32)
            return carry

        lax.fori_loop(0, HALF, one, 0)

    def out_copy(j, c):
        planes = pl.ds(OUT_GROUP * j, OUT_GROUP)
        return pltpu.make_async_copy(out.at[c, planes], new.at[c, planes], out_sems.at[j, c])

    def group(j, carry):
        def pair(k, carry):
            for d in range(2):
                x = OUT_GROUP * j + 2 * k + d
                for h in range(2):
                    rows = pl.ds(pl.multiple_of(WY * x + 16 * h, 16), 16)
                    cells = [psi[c, rows].astype(f32) for c in range(COMPS)]
                    for i in (2 * h, 2 * h + 1):
                        r = slice(8 * (i % 2), 8 * (i % 2) + 8)
                        weight = pot[pl.ds(pl.multiple_of(WY * (x + 1) + 8 * i, 8), 8)]
                        for orbital in range(COMPS // 2):
                            parts = (2 * orbital, 2 * orbital + 1)
                            picked = [lambda row, c=c: image[c, pl.ds(row, 8)] for c in parts]
                            own = [cells[c][r] for c in parts]
                            real, imag = _stepped(own, picked, weight, orbital, _base(x + 1) + 8 * i, lane)
                            out[2 * orbital, x, 8 * i : 8 * i + 8] = real
                            out[2 * orbital + 1, x, 8 * i : 8 * i + 8] = imag
            return carry

        lax.fori_loop(0, OUT_GROUP // 2, pair, 0)
        for c in range(COMPS):
            out_copy(j, c).start()
        return carry

    lax.fori_loop(0, WX // OUT_GROUP, group, 0)
    for j in range(WX // OUT_GROUP):
        for c in range(COMPS):
            out_copy(j, c).wait()


def _step(recv, *arrays):
    t = _tables()
    return pl.pallas_call(
        _step_kernel,
        name="step",
        in_specs=[_VM] * (3 + len(arrays)),
        out_specs=[_HBM, _VM],
        out_shape=[
            jax.ShapeDtypeStruct((COMPS, WX, WY, NZ), f32),
            jax.ShapeDtypeStruct((WY, NZ // ORBS, WX), f32),
        ],
        scratch_shapes=[
            pltpu.VMEM((COMPS, PADDED, NZ), f32),
            pltpu.VMEM((PLANES * WY, NZ), f32),
            pltpu.VMEM((PLANES * WY, NZ), f32),
            pltpu.VMEM((2, WX, NZ), f32),
            pltpu.VMEM((3 * NZ, 256), bf16),
            pltpu.VMEM((4, 128, 128), f32),
            pltpu.VMEM((COMPS, WX, WY, NZ), f32),
            pltpu.SemaphoreType.DMA((WX // OUT_GROUP, COMPS)),
        ],
        compiler_params=pltpu.CompilerParams(vmem_limit_bytes=24 * 1024 * 1024),
        cost_estimate=pl.CostEstimate(flops=100000000, bytes_accessed=20000000, transcendentals=0),
    )(jnp.asarray(t["stacked"]), recv, jnp.asarray(t["tiled"]), *arrays)


def _shifted(value, axis, count, step):
    return lax.ppermute(value, axis, [(i, (i + step) % count) for i in range(count)])


def _swap(messages, rows):
    moved = lax.all_to_all(messages.reshape(DEVICES, 1, rows * 128), TRANSPOSE_AXES, 0, 0)
    return moved.reshape(DEVICES * rows, 128)


def body(orbitals, occupations, ext_pot, hartree_old):
    psi = orbitals.reshape(COMPS, WX * WY, NZ)
    ext, old = ext_pot.reshape(WX * WY, NZ), hartree_old.reshape(WX * WY, NZ)
    x_left, x_right, y_left, y_right, pot = _faces(psi, ext, old)
    y_low = _shifted(y_right, "pois", POIS, 1)
    y_high = _shifted(y_left, "pois", POIS, -1)
    image_a, done = _inner(0, psi, pot)
    x_left, x_right = _corners(x_left, x_right, y_low, y_high, done)
    x_low = _shifted(x_right, "slab", SLABS, 1)
    x_high = _shifted(x_left, "slab", SLABS, -1)
    image_b, _ = _inner(HALF, psi, pot)
    image_a, image_b, charge, totals = _middle(occupations, psi, pot, image_a, image_b, y_low, y_high, y_left, y_right)
    image_a, image_b, _, message = _edge_messages(
        occupations, psi, pot, image_a, image_b, charge, totals, x_low, x_high
    )
    faces = (x_low, x_high, y_low, y_high)
    back = _swap(_plane(_swap(message, FWD)), BACK)
    new, hartree = _step(back, image_a, image_b, psi, ext, old, *faces)
    return new.reshape(orbitals.shape), jnp.transpose(hartree, (2, 0, 1))


def solution(mesh):
    placed = (P("orb", None, "slab", "pois", None), P("orb"), P("slab", "pois", None), P("slab", "pois", None))
    return jax.shard_map(
        body,
        mesh=mesh,
        in_specs=placed,
        out_specs=(P("orb", None, "slab", "pois", None), P("slab", "pois", "orb")),
        check_vma=False,
    )
```

```python
import functools
import math

import jax
import jax.numpy as jnp
import ml_dtypes
import numpy as np
from jax import lax
from jax.experimental import pallas as pl
from jax.experimental.pallas import tpu as pltpu
from jax.sharding import PartitionSpec as P

NX, NY, NZ = 192, 128, 128
SLABS, ORBS, POIS = 4, 8, 4
WX, WY = NX // SLABS, NY // POIS
COMPS = 8
FWD = 13
BACK = 14
DEVICES = SLABS * ORBS * POIS
TRANSPOSE_AXES = ("orb", "pois", "slab")
DT = 0.3
VMEM_LIMIT = 67043328

PITCH = 40
PLANES = WX + 2
PADDED = 8 + (PLANES + 2) * PITCH
GROUP = 24
SHARE = (5, 3)
FIRST = 8 + 2 * PITCH
f32, bf16 = jnp.float32, jnp.bfloat16


def _sines(n):
    k = np.arange(1, n + 1)
    return np.sin(np.pi * ((k[:, None] * k[None, :]) % (2 * (n + 1))) / (n + 1))


def _lam(n):
    return 2.0 - 2.0 * np.cos(np.pi * np.arange(1, n + 1) / (n + 1))


@functools.cache
def _tables():
    sx, sy = _sines(NX), _sines(NY)
    order = np.array([s * WX + 4 * xb + xi for xi in range(4) for s in range(SLABS) for xb in range(WX // 4)])
    padded = np.zeros((SLABS * 64, NX))
    for s in range(SLABS):
        padded[s * 64 : s * 64 + WX] = sx[s * WX : (s + 1) * WX]
    ring_x = np.zeros((16, NX))
    ring_y = np.zeros((16, NY))
    for s in range(SLABS):
        if s > 0:
            ring_x[s] = sx[s * WX - 1]
        if s < SLABS - 1:
            ring_x[8 + s] = sx[(s + 1) * WX]
    for p in range(POIS):
        if p > 0:
            ring_y[p] = sy[p * WY - 1]
        if p < POIS - 1:
            ring_y[8 + p] = sy[(p + 1) * WY]
    back_x = np.concatenate([sx[order], padded, ring_x])
    modes = np.stack([_lam(NZ), sy.sum(1)])
    cast = lambda a: np.asarray(a, np.float32)

    def split(a):
        high = cast(a).astype(ml_dtypes.bfloat16)
        return high, (cast(a) - high.astype(np.float32)).astype(ml_dtypes.bfloat16)

    def wide(a):
        high, low = split(a)
        return np.concatenate([high, high, low], 1)

    high, low = split(sy)
    tiles = [np.arange(128) % (NZ // ORBS) + o * (NZ // ORBS) for o in range(ORBS)]
    stacked = np.concatenate([high, high, low], 0)
    shift = np.eye(NZ, k=1) + np.eye(NZ, k=-1)
    return dict(
        near=shift.astype(ml_dtypes.bfloat16),
        beside=wide(sy),
        stacked=stacked,
        tiled=np.stack([stacked[:, t] for t in tiles]),
        forward_x=wide(sx[:, order]),
        back_x=wide(back_x),
        ring_y=wide(ring_y),
        col=cast(np.stack([_lam(NX), sx.sum(1)] + [np.zeros(NX)] * 6, 1)),
        row=cast(np.stack([_lam(NY), sy.sum(1)] + [np.zeros(NY)] * 6, 0)),
        modes=cast(modes),
    )


_VM = pl.BlockSpec(memory_space=pltpu.VMEM)
_SM = pl.BlockSpec(memory_space=pltpu.SMEM)
_ANY = pl.BlockSpec(memory_space=pl.ANY)
_HBM = pl.BlockSpec(memory_space=pltpu.HBM)
CORNERS = COMPS + 1
_X_FACE, _Y_FACE = (COMPS + 2, 2, WY, NZ), (COMPS + 1, 2, WX, NZ)
_FACES = [_X_FACE, _X_FACE, _Y_FACE, _Y_FACE]


def _iotas():
    return (
        lax.broadcasted_iota(jnp.int32, (8, 128), 0),
        lax.broadcasted_iota(jnp.int32, (8, 128), 1),
    )


def _zsum(v, lane):
    return jnp.where(lane == 0, 0.0, pltpu.roll(v, 1, 1)) + jnp.where(lane == 127, 0.0, pltpu.roll(v, 127, 1))


def _base(plane):
    return pl.multiple_of(8 + PITCH + PITCH * plane, 8)


def _split(value):
    high = value.astype(bf16)
    return high, (value - high.astype(f32)).astype(bf16)


def _faces_kernel(
    psi_hbm, ext, old, x_left, x_right, y_left, y_right, pot, psi, pots, rows, potential, x_edge, y_edge, sems, out_sems, pot_sem
):
    copies = [pltpu.make_async_copy(ref, pots.at[k], sems.at[k]) for k, ref in enumerate((ext, old))]
    copies += [pltpu.make_async_copy(psi_hbm.at[c], psi.at[c], sems.at[2 + c]) for c in range(COMPS)]
    for copy in copies:
        copy.start()
    sent = []

    def send(c, x_sources):
        sources = (*x_sources, y_edge.at[0, c], y_edge.at[1, c])
        for k, (source, ref) in enumerate(zip(sources, (x_left, x_right, y_left, y_right))):
            sent.append(pltpu.make_async_copy(source, ref.at[c], out_sems.at[c, k]))
            sent[-1].start()

    copies[0].wait()
    copies[1].wait()
    pots[0] = pots[0] + pots[1]
    potential[...] = 6.0 + 2.0 * pots[0]
    sent.append(pltpu.make_async_copy(potential, pot, pot_sem))
    sent[-1].start()
    for k in range(2):
        x_edge[0, k] = pots[k, 0:WY].astype(bf16)
        x_edge[1, k] = pots[k, WY * (WX - 1) : WY * WX].astype(bf16)
        y_edge[0, COMPS, k] = pots[k, pl.ds(0, WX, WY), :].astype(bf16)
        y_edge[1, COMPS, k] = pots[k, pl.ds(WY - 1, WX, WY), :].astype(bf16)
    send(COMPS, (x_edge.at[0], x_edge.at[1]))
    for c in range(COMPS):
        copies[2 + c].wait()

        def fill(x, carry, c=c):
            rows[0, pl.ds(pl.multiple_of(8 * x, 8), 8), :] = psi[c, x, 0:16, :].astype(f32)[0:8]
            rows[1, pl.ds(pl.multiple_of(8 * x, 8), 8), :] = psi[c, x, 16:32, :].astype(f32)[8:16]
            return carry

        lax.fori_loop(0, WX, fill, 0, unroll=WX)
        for half, first in ((0, 0), (1, 6)):
            for d in range(2):
                y_edge[half, c, d] = rows[half, pl.ds(first + d, WX, 8), :].astype(bf16)
        send(c, (psi.at[c, pl.ds(0, 2)], psi.at[c, pl.ds(WX - 2, 2)]))
    for copy in sent:
        copy.wait()


def _faces(psi, ext, old):
    return pl.pallas_call(
        _faces_kernel,
        name="faces",
        in_specs=[_HBM] * 3,
        out_specs=[_HBM] * 5,
        out_shape=[jax.ShapeDtypeStruct(s, bf16) for s in _FACES] + [jax.ShapeDtypeStruct((WX * WY, NZ), f32)],
        scratch_shapes=[
            pltpu.VMEM((COMPS, WX, WY, NZ), bf16),
            pltpu.VMEM((2, WX * WY, NZ), f32),
            pltpu.VMEM((2, 8 * WX, 128), f32),
            pltpu.VMEM((WX * WY, NZ), f32),
            pltpu.VMEM((2, 2, WY, NZ), bf16),
            pltpu.VMEM((2, COMPS + 1, 2, WX, NZ), bf16),
            pltpu.SemaphoreType.DMA((2 + COMPS,)),
            pltpu.SemaphoreType.DMA((COMPS + 1, 4)),
            pltpu.SemaphoreType.DMA,
        ],
        compiler_params=pltpu.CompilerParams(vmem_limit_bytes=VMEM_LIMIT),
        cost_estimate=pl.CostEstimate(flops=1000000, bytes_accessed=6000000, transcendentals=0),
    )(psi, ext, old)


def _corners_kernel(x_left, x_right, y_low, y_high, after, left, right, block, entry, sems):
    del x_left, x_right, after
    copies = []
    for k, (out, first, row) in enumerate(((left, 0, 0), (right, WX - 16, 15))):
        for side, ref in enumerate((y_low, y_high)):
            for c in range(COMPS):
                cells = ref[c, 1 - side, first : first + 16].astype(f32)
                block[c : c + 1] = cells[row : row + 1]
            entry[k, side] = block[...].astype(bf16)
        copies.append(pltpu.make_async_copy(entry.at[k], out.at[CORNERS], sems.at[k]))
        copies[k].start()
    for copy in copies:
        copy.wait()


def _corners(x_left, x_right, y_low, y_high, after):
    shape = jax.ShapeDtypeStruct(_X_FACE, bf16)
    return pl.pallas_call(
        _corners_kernel,
        name="corners",
        in_specs=[_ANY, _ANY, _VM, _VM, _ANY],
        out_specs=[_ANY, _ANY],
        out_shape=[shape, shape],
        scratch_shapes=[
            pltpu.VMEM((WY, NZ), f32),
            pltpu.VMEM((2, 2, WY, NZ), bf16),
            pltpu.SemaphoreType.DMA((2,)),
        ],
        input_output_aliases={0: 0, 1: 1},
        compiler_params=pltpu.CompilerParams(vmem_limit_bytes=2 * 1024 * 1024),
        cost_estimate=pl.CostEstimate(flops=10000, bytes_accessed=200000, transcendentals=0),
    )(x_left, x_right, y_low, y_high, after)


def _inner_kernel(first_part, near, psi, pot, image, token, psi_f):
    token[...] = jnp.zeros((8, NZ), f32)
    count = image.shape[0]
    for c in range(count):

        def widen(x, carry, c=c):
            rows = pl.ds(pl.multiple_of(WY * x, WY), WY)
            psi_f[c, pl.ds(_base(x + 1), WY)] = psi[first_part + c, rows].astype(f32)
            return carry

        lax.fori_loop(0, WX, widen, 0, unroll=16)
        for side in range(2):
            psi_f[c, pl.ds(FIRST + (WY if side else -1), WX, PITCH)] = jnp.zeros((WX, NZ), f32)
            psi_f[c, pl.ds(FIRST - PITCH + (WX + 1) * PITCH * side, WY)] = jnp.zeros((WY, NZ), f32)

    def group(k, carry):
        c, j = k // (WX // GROUP), k % (WX // GROUP)
        start = pl.multiple_of(GROUP * WY * j, WY)
        sums = jnp.dot(
            psi[first_part + c, pl.ds(start, GROUP * WY)], near[...], preferred_element_type=f32
        )
        for g in range(GROUP):
            base = _base(GROUP * j + g + 1)
            for i in range(4):
                at = base + 8 * i
                load = lambda row: psi_f[c, pl.ds(row, 8)]
                beside = (load(at - 1) + load(at + 1)) + (load(at - PITCH) + load(at + PITCH))
                first = WY * g + 8 * i
                weight = pot[pl.ds(pl.multiple_of(start + first, 8), 8)]
                value = weight * load(pl.multiple_of(at, 8)) - (beside + sums[first : first + 8])
                image[c, pl.ds(pl.multiple_of(at, 8), 8)] = value
        return carry

    lax.fori_loop(0, count * (WX // GROUP), group, 0)


_IMAGES = [jax.ShapeDtypeStruct((n, PADDED, NZ), f32) for n in SHARE]


def _inner(which, psi, pot):
    return pl.pallas_call(
        functools.partial(_inner_kernel, SHARE[0] * which),
        name="inner",
        in_specs=[_VM] * 3,
        out_specs=[_VM, _VM],
        out_shape=[_IMAGES[which], jax.ShapeDtypeStruct((8, NZ), f32)],
        scratch_shapes=[pltpu.VMEM(_IMAGES[which].shape, f32)],
        compiler_params=pltpu.CompilerParams(vmem_limit_bytes=24 * 1024 * 1024),
        cost_estimate=pl.CostEstimate(flops=400000000, bytes_accessed=12000000, transcendentals=0),
    )(jnp.asarray(_tables()["near"]), psi, pot)


def _inside():
    slab, pois = lax.axis_index("slab"), lax.axis_index("pois")
    number = lambda cond: jnp.where(cond, 1.0, 0.0).astype(f32)
    return (
        (number(slab > 0), number(slab < SLABS - 1)),
        (number(pois > 0), number(pois < POIS - 1)),
    )


def _place(part):
    return (0, part) if part < SHARE[0] else (1, part - SHARE[0])


def _stepped(cells, images, pot, orbital, at, lane):
    parts = []
    for k in range(2):
        load = lambda row, hint=True: images[k](pl.multiple_of(row, 8) if hint else row)
        u = load(at)
        total = (load(at - PITCH) + load(at + PITCH)) + (load(at - 1, False) + load(at + 1, False)) + _zsum(u, lane)
        parts.append((cells[k], u, pot * u - total))
    (a, ua, wa), (b, ub, wb) = parts
    scale = 0.125 * DT * DT
    return (a - scale * wa) + (0.5 * DT) * ub, (b - scale * wb) - (0.5 * DT) * ua


def _plane_charge(x, occ, psi, pot, halves, charge, totals, lane):
    for h in range(2):
        cells = [psi[c, pl.ds(pl.multiple_of(WY * x + 16 * h, 16), 16)].astype(f32) for c in range(COMPS)]
        for i in (2 * h, 2 * h + 1):
            r = slice(8 * (i % 2), 8 * (i % 2) + 8)
            row = pl.ds(pl.multiple_of(WY * x + 8 * i, 8), 8)
            weight = pot[row]
            sums = None
            for orbital in range(COMPS // 2):
                parts = (2 * orbital, 2 * orbital + 1)
                picked = [lambda at, c=c: halves[_place(c)[0]][_place(c)[1], pl.ds(at, 8)] for c in parts]
                own = [cells[c][r] for c in parts]
                real, imag = _stepped(own, picked, weight, orbital, _base(x + 1) + 8 * i, lane)
                term = occ[orbital] * (real * real + imag * imag)
                sums = term if sums is None else sums + term
            charge[row, :] = sums
            totals = totals + sums
    return totals


def _middle_kernel(occupations, psi, pot, image_a, image_b, y_low, y_high, own_low, own_high, a, b, charge, totals, column):
    del image_a, image_b
    _, lane = _iotas()
    _, in_y = _inside()
    y_faces, own = (y_low, y_high), (own_low, own_high)
    ring_y = [6.0 + 2.0 * f[COMPS, 0].astype(f32) for f in y_faces]
    column[...] = jnp.zeros_like(column)
    for half, image in enumerate((a, b)):

        def edges(c, carry, half=half, image=image):
            part = SHARE[0] * half + c
            for side in range(2):
                near = y_faces[side][part, 1 - side].astype(f32) * in_y[side]
                far = y_faces[side][part, side].astype(f32)
                inner = own[side][part, side].astype(f32)
                at = pl.ds(FIRST + (WY - 1) * side, WX, PITCH)
                image[c, at] = image[c, at] - near
                column[side, 8:56] = near
                total = (far + inner) + (column[side, 7:55] + column[side, 9:57])
                value = [
                    ring_y[side][r] * near[r] - (total[r] + _zsum(near[r], lane))
                    for r in (slice(8 * i, 8 * i + 8) for i in range(WX // 8))
                ]
                image[c, pl.ds(FIRST + (WY if side else -1), WX, PITCH)] = jnp.concatenate(value, axis=0) * in_y[side]
            return carry

        lax.fori_loop(0, SHARE[half], edges, 0)
    occ = [occupations[k] for k in range(COMPS // 2)]

    def pair(k, sums):
        for d in range(2):
            sums = _plane_charge(2 * k + d, occ, psi, pot, (a, b), charge, sums, lane)
        return sums

    totals[...] = lax.fori_loop(1, WX // 2 - 1, pair, jnp.zeros((8, 128), f32))


def _edge_kernel(
    occupations, beside, psi, pot, image_a, image_b, charge_in, totals, x_low, x_high, a, b, charge, message, column
):
    del image_a, image_b, charge_in
    _, lane = _iotas()
    in_x, in_y = _inside()
    x_faces = (x_low, x_high)
    ring_x = [6.0 + 2.0 * f[COMPS, 0].astype(f32) for f in x_faces]
    for i in range(2):
        for j in range(2):
            column[2 + 2 * i + j, 0:8] = x_faces[i][CORNERS, j].astype(f32)[0:8] * (in_x[i] * in_y[j])
    for half, image in enumerate((a, b)):

        def edges(c, carry, half=half, image=image):
            part = SHARE[0] * half + c
            for side in range(2):
                near = x_faces[side][part, 1 - side].astype(f32) * in_x[side]
                far = x_faces[side][part, side].astype(f32)
                inner = psi[part, pl.ds(WY * (WX - 1) * side, WY)].astype(f32)
                first = FIRST + PITCH * (WX - 1) * side
                image[c, pl.ds(first, WY)] = image[c, pl.ds(first, WY)] - near
                column[side, 8:40] = near
                for j, row in ((0, 7), (1, 40)):
                    corner = column[2 + 2 * side + j, pl.ds(part, 1)]
                    column[side, row : row + 1] = corner
                    at = pl.ds(first + (WY if j else -1), 1)
                    image[c, at] = image[c, at] - corner
                total = (far + inner) + (column[side, 7:39] + column[side, 9:41])
                for i in range(4):
                    r = slice(8 * i, 8 * i + 8)
                    ring = ring_x[side][r] * near[r] - (total[r] + _zsum(near[r], lane))
                    image[c, pl.ds(FIRST - PITCH + PITCH * (WX + 1) * side + 8 * i, 8)] = ring * in_x[side]
            return carry

        lax.fori_loop(0, SHARE[half], edges, 0)
    occ = [occupations[k] for k in range(COMPS // 2)]

    def pair(k, sums):
        for d in range(2):
            x = (WX - 2) * k + d
            sums = _plane_charge(x, occ, psi, pot, (a, b), charge, sums, lane)
        return sums

    sums = lax.fori_loop(0, 2, pair, totals[...])
    mean = jnp.broadcast_to(jnp.sum(sums, keepdims=True) / (WX * WY * NZ), (8, 128))

    def group(g, carry):
        cells = charge[pl.ds(pl.multiple_of(256 * g, 256), 256), :] - mean[0:1]
        high, low = _split(cells)
        modes = lax.dot_general(
            beside[...],
            jnp.concatenate([high, low, high], axis=1),
            (((1,), (1,)), ((), ())),
            preferred_element_type=f32,
        )
        for k in range(16):
            for h in range(2):
                piece = modes[8 * k : 8 * k + 8, 128 * h : 128 * h + 128]
                message[pl.ds(8 * FWD * k + 2 * g + h, 8, FWD), :] = piece
        return carry

    lax.fori_loop(0, WX // 8, group, 0, unroll=2)
    for k in range(16):
        message[pl.ds(8 * FWD * k + FWD - 1, 8, FWD), :] = mean


_CHARGE = jax.ShapeDtypeStruct((WX * WY, NZ), f32)


def _middle(occupations, psi, pot, image_a, image_b, *faces):
    return pl.pallas_call(
        _middle_kernel,
        name="middle",
        in_specs=[_SM] + [_VM] * 8,
        out_specs=[_VM] * 4,
        out_shape=[*_IMAGES, _CHARGE, jax.ShapeDtypeStruct((8, NZ), f32)],
        scratch_shapes=[pltpu.VMEM((2, 64, NZ), f32)],
        input_output_aliases={3: 0, 4: 1},
        compiler_params=pltpu.CompilerParams(vmem_limit_bytes=16 * 1024 * 1024),
        cost_estimate=pl.CostEstimate(flops=100000000, bytes_accessed=8000000, transcendentals=0),
    )(occupations, psi, pot, image_a, image_b, *faces)


def _edge_messages(occupations, psi, pot, image_a, image_b, charge, totals, x_low, x_high):
    return pl.pallas_call(
        _edge_kernel,
        name="edge",
        in_specs=[_SM] + [_VM] * 9,
        out_specs=[_VM] * 4,
        out_shape=[*_IMAGES, _CHARGE, jax.ShapeDtypeStruct((DEVICES * FWD, 128), f32)],
        scratch_shapes=[pltpu.VMEM((6, 64, NZ), f32)],
        input_output_aliases={4: 0, 5: 1, 6: 2},
        compiler_params=pltpu.CompilerParams(vmem_limit_bytes=16 * 1024 * 1024),
        cost_estimate=pl.CostEstimate(flops=100000000, bytes_accessed=8000000, transcendentals=0),
    )(occupations, jnp.asarray(_tables()["beside"]), psi, pot, image_a, image_b, charge, totals, x_low, x_high)


def _swap_groups(blocks, group):
    out = []
    for i in range(4):
        value = None
        for j in range(4):
            shift = (32 * (j - i)) % 128
            moved = pltpu.roll(blocks[j], shift, 1) if shift else blocks[j]
            value = moved if value is None else jnp.where(group == j, moved, value)
        out.append(value)
    return out


def _plane_kernel(modes, recv, forward_x, stacked, back_x, ring_y, col, row, send, packed, block):
    dot = functools.partial(jnp.dot, preferred_element_type=f32)

    def parts(value, axis):
        high, low = _split(value)
        return jnp.concatenate([high, low, high], axis=axis)

    left = lambda table, value: dot(table[...], parts(value, 0))
    right = lambda value: dot(parts(value, 1), stacked[...])
    nt = lambda table, value: lax.dot_general(
        table[...], parts(value, 1), (((1,), (1,)), ((), ())), preferred_element_type=f32
    )
    kz = (lax.axis_index("orb") * POIS + lax.axis_index("pois")) * SLABS + lax.axis_index("slab")
    lam_z, sum_z = modes[0, kz], modes[1, kz]
    means = recv[pl.ds(FWD - 1, DEVICES, FWD), :]
    blocks = POIS * SLABS
    block_mean = sum(means[blocks * o : blocks * (o + 1)] for o in range(ORBS))
    mean = jnp.sum(block_mean, axis=0, keepdims=True) / blocks
    block_means = [block_mean[k : k + 1] for k in range(blocks)]
    for p in range(POIS):
        for s in range(SLABS):
            first = [((o * POIS + p) * SLABS + s) * FWD for o in range(ORBS)]
            shift = sum_z * (block_means[p * SLABS + s][0:1] - mean)
            packed[p, pl.ds(12 * s, 8), :] = sum(recv[pl.ds(r, 8), :] for r in first) + shift
            last = sum(recv[pl.ds(r + FWD - 8, 8), :] for r in first) + shift
            packed[p, pl.ds(12 * s + 8, 4), :] = last[3:7]
    group = lax.broadcasted_iota(jnp.int32, (WX, 128), 1) // 32
    plane = jnp.concatenate(_swap_groups([packed[p, 0:WX] for p in range(POIS)], group), axis=0)
    spectrum = right(left(forward_x, plane))
    divisor = col[:, 0:1] + row[0:1, :] + lam_z
    factor = 32.0 * math.pi / ((NX + 1) * (NY + 1) * (NZ + 1))
    scaled = spectrum * factor / divisor
    across = left(back_x, scaled)
    field = right(across[:NX])
    ring = right(across[NX + 256 :])
    cells = _swap_groups([field[WX * i : WX * (i + 1)] for i in range(4)], group)
    lane8 = lax.broadcasted_iota(jnp.int32, (8, 128), 1)
    group8 = lane8 // 32
    faces = [nt(ring_y, across[NX + 128 * h : NX + 128 * (h + 1)]) for h in range(2)]
    y_rows = []
    for s in range(SLABS):
        low, high = faces[s // 2][0:8], faces[s // 2][8:16]
        if s % 2 == 0:
            high = pltpu.roll(high, 64, 1)
        else:
            low = pltpu.roll(low, 64, 1)
        y_rows.append(jnp.where(lane8 < 64, low, high))
    for p in range(POIS):
        shift = lambda v, k: pltpu.roll(v, k % 128, 1) if k % 128 else v
        x_rows = jnp.where(
            group8 == 0,
            shift(ring[0:8], -32 * p),
            jnp.where(group8 == 1, shift(ring[8:16], 32 - 32 * p), 0.0),
        )
        for s in range(SLABS):
            base = (p * SLABS + s) * BACK
            block[pl.ds(base, 12), :] = cells[p][12 * s : 12 * s + 12]
            block[pl.ds(base + 12, 1), :] = x_rows[s : s + 1]
            block[pl.ds(base + 13, 1), :] = y_rows[s][p : p + 1]
    count = POIS * SLABS * BACK
    for o in range(ORBS):
        send[pl.ds(o * count, count), :] = block[0:count]


def _plane(recv):
    t = _tables()
    return pl.pallas_call(
        _plane_kernel,
        name="plane",
        in_specs=[_SM] + [_VM] * 7,
        out_specs=_VM,
        out_shape=jax.ShapeDtypeStruct((DEVICES * BACK, 128), f32),
        scratch_shapes=[
            pltpu.VMEM((POIS, WX + 8, 128), f32),
            pltpu.VMEM((POIS * SLABS * BACK + 16, 128), f32),
        ],
        compiler_params=pltpu.CompilerParams(vmem_limit_bytes=8 * 1024 * 1024),
        cost_estimate=pl.CostEstimate(flops=200000000, bytes_accessed=3000000, transcendentals=0),
    )(
        jnp.asarray(t["modes"]),
        recv,
        *(jnp.asarray(t[k]) for k in ("forward_x", "stacked", "back_x", "ring_y", "col", "row")),
    )


OUT_GROUP = 4


def _step_kernel(
    stacked, recv, tiled, image_a, image_b, psi, ext, old, x_low, x_high, y_low, y_high,
    new, hartree, image, pot, change, ring_y, tables, slices, out, out_sems,
):
    faces = (x_low, x_high, y_low, y_high)
    in_x, in_y = _inside()
    sub, lane = _iotas()
    tables[:, 0:128] = stacked[...]
    tables[:, 128:256] = tiled[lax.axis_index("orb")]

    def back(r, table):
        high, low = _split(recv[pl.ds(r, 128, BACK), :])
        stack = jnp.concatenate([high, low, high], axis=0)
        return lax.dot_general(stack, table[...], (((0,), (0,)), ((), ())), preferred_element_type=f32)

    def planes(g, carry):
        both = back(g, tables)
        field, mine = both[:, 0:128], both[:, 128:256]
        first = pl.multiple_of(4 * WY * g, 8)
        block = pl.ds(first, 4 * WY)
        moved = pl.ds(pl.multiple_of(first + WY, 8), 4 * WY)
        pot[moved] = 6.0 + (2.0 * ext[block] + (old[block] + field))
        change[moved] = field - old[block]
        for k in range(16):
            kept_lanes = jnp.where(lane // 16 == sub, mine[8 * k : 8 * k + 8], 0.0)
            slices[k % 4, pl.ds(4 * g + k // 4, 1), :] = jnp.sum(kept_lanes, axis=0, keepdims=True)
        return carry

    lax.fori_loop(0, WX // 4, planes, 0, unroll=2)
    x_field, y_field = back(12, stacked), back(13, stacked)
    for side in range(2):
        edge = pl.ds((WX + 1) * WY * side, WY)
        change[edge] = (x_field[32 * side : 32 * side + 32] - faces[side][COMPS, 1].astype(f32)) * in_x[side]
        ring_y[side] = (y_field[64 * side : 64 * side + WX] - faces[2 + side][COMPS, 1].astype(f32)) * in_y[side]
    for q in range(4):
        turned = jnp.transpose(slices[q])
        for y in range(8):
            hartree[8 * q + y] = turned[16 * y : 16 * y + 16, 0:WX]

    for half, start in enumerate((image_a, image_b)):

        def one(c, carry, half=half, start=start):
            part = SHARE[0] * half + c

            def planes_of(j, carry):
                for k in range(6):
                    x = 6 * j + k
                    value = psi[part, pl.ds(pl.multiple_of(WY * x, WY), WY)].astype(f32)
                    at = pl.ds(_base(x + 1), WY)
                    image[part, at] = start[c, at] + change[pl.ds(pl.multiple_of(WY * (x + 1), WY), WY)] * value
                return carry

            lax.fori_loop(0, WX // 6, planes_of, 0)
            for side in range(2):
                at = pl.ds(FIRST - PITCH + PITCH * (WX + 1) * side, WY)
                value = faces[side][part, 1 - side].astype(f32)
                image[part, at] = start[c, at] + change[pl.ds((WX + 1) * WY * side, WY)] * value
                at = pl.ds(FIRST + (WY if side else -1), WX, PITCH)
                image[part, at] = start[c, at] + ring_y[side] * faces[2 + side][part, 1 - side].astype(f32)
            return carry

        lax.fori_loop(0, SHARE[half], one, 0)

    def out_copy(j, c):
        planes = pl.ds(OUT_GROUP * j, OUT_GROUP)
        return pltpu.make_async_copy(out.at[c, planes], new.at[c, planes], out_sems.at[j, c])

    def group(j, carry):
        def pair(k, carry):
            for d in range(2):
                x = OUT_GROUP * j + 2 * k + d
                for h in range(2):
                    rows = pl.ds(pl.multiple_of(WY * x + 16 * h, 16), 16)
                    cells = [psi[c, rows].astype(f32) for c in range(COMPS)]
                    for i in (2 * h, 2 * h + 1):
                        r = slice(8 * (i % 2), 8 * (i % 2) + 8)
                        weight = pot[pl.ds(pl.multiple_of(WY * (x + 1) + 8 * i, 8), 8)]
                        for orbital in range(COMPS // 2):
                            parts = (2 * orbital, 2 * orbital + 1)
                            picked = [lambda row, c=c: image[c, pl.ds(row, 8)] for c in parts]
                            own = [cells[c][r] for c in parts]
                            real, imag = _stepped(own, picked, weight, orbital, _base(x + 1) + 8 * i, lane)
                            out[2 * orbital, x, 8 * i : 8 * i + 8] = real
                            out[2 * orbital + 1, x, 8 * i : 8 * i + 8] = imag
            return carry

        lax.fori_loop(0, OUT_GROUP // 2, pair, 0)
        for c in range(COMPS):
            out_copy(j, c).start()
        return carry

    lax.fori_loop(0, WX // OUT_GROUP, group, 0)
    for j in range(WX // OUT_GROUP):
        for c in range(COMPS):
            out_copy(j, c).wait()


def _step(recv, *arrays):
    t = _tables()
    return pl.pallas_call(
        _step_kernel,
        name="step",
        in_specs=[_VM] * (3 + len(arrays)),
        out_specs=[_HBM, _VM],
        out_shape=[
            jax.ShapeDtypeStruct((COMPS, WX, WY, NZ), f32),
            jax.ShapeDtypeStruct((WY, NZ // ORBS, WX), f32),
        ],
        scratch_shapes=[
            pltpu.VMEM((COMPS, PADDED, NZ), f32),
            pltpu.VMEM((PLANES * WY, NZ), f32),
            pltpu.VMEM((PLANES * WY, NZ), f32),
            pltpu.VMEM((2, WX, NZ), f32),
            pltpu.VMEM((3 * NZ, 256), bf16),
            pltpu.VMEM((4, 128, 128), f32),
            pltpu.VMEM((COMPS, WX, WY, NZ), f32),
            pltpu.SemaphoreType.DMA((WX // OUT_GROUP, COMPS)),
        ],
        compiler_params=pltpu.CompilerParams(vmem_limit_bytes=24 * 1024 * 1024),
        cost_estimate=pl.CostEstimate(flops=100000000, bytes_accessed=20000000, transcendentals=0),
    )(jnp.asarray(t["stacked"]), recv, jnp.asarray(t["tiled"]), *arrays)


def _shifted(value, axis, count, step):
    return lax.ppermute(value, axis, [(i, (i + step) % count) for i in range(count)])


def _swap(messages, rows):
    moved = lax.all_to_all(messages.reshape(DEVICES, 1, rows * 128), TRANSPOSE_AXES, 0, 0)
    return moved.reshape(DEVICES * rows, 128)


def body(orbitals, occupations, ext_pot, hartree_old):
    psi = orbitals.reshape(COMPS, WX * WY, NZ)
    ext, old = ext_pot.reshape(WX * WY, NZ), hartree_old.reshape(WX * WY, NZ)
    x_left, x_right, y_left, y_right, pot = _faces(orbitals.reshape(COMPS, WX, WY, NZ), ext, old)
    y_low = _shifted(y_right, "pois", POIS, 1)
    y_high = _shifted(y_left, "pois", POIS, -1)
    image_a, done = _inner(0, psi, pot)
    x_left, x_right = _corners(x_left, x_right, y_low, y_high, done)
    x_low = _shifted(x_right, "slab", SLABS, 1)
    x_high = _shifted(x_left, "slab", SLABS, -1)
    image_b, _ = _inner(1, psi, pot)
    image_a, image_b, charge, totals = _middle(occupations, psi, pot, image_a, image_b, y_low, y_high, y_left, y_right)
    image_a, image_b, _, message = _edge_messages(
        occupations, psi, pot, image_a, image_b, charge, totals, x_low, x_high
    )
    faces = (x_low, x_high, y_low, y_high)
    back = _swap(_plane(_swap(message, FWD)), BACK)
    new, hartree = _step(back, image_a, image_b, psi, ext, old, *faces)
    return new.reshape(orbitals.shape), jnp.transpose(hartree, (2, 0, 1))


def solution(mesh):
    placed = (P("orb", None, "slab", "pois", None), P("orb"), P("slab", "pois", None), P("slab", "pois", None))
    return jax.shard_map(
        body,
        mesh=mesh,
        in_specs=placed,
        out_specs=(P("orb", None, "slab", "pois", None), P("slab", "pois", "orb")),
        check_vma=False,
    )
```

```python
import functools
import math

import jax
import jax.numpy as jnp
import ml_dtypes
import numpy as np
from jax import lax
from jax.experimental import pallas as pl
from jax.experimental.pallas import tpu as pltpu
from jax.sharding import PartitionSpec as P

NX, NY, NZ = 192, 128, 128
SLABS, ORBS, POIS = 4, 8, 4
WX, WY = NX // SLABS, NY // POIS
COMPS = 8
FWD = 13
BACK = 14
DEVICES = SLABS * ORBS * POIS
TRANSPOSE_AXES = ("orb", "pois", "slab")
DT = 0.3
VMEM_LIMIT = 67043328

PITCH = 40
PLANES = WX + 2
PADDED = 8 + (PLANES + 2) * PITCH
GROUP = 24
SHARE = (7, 1)
FIRST = 8 + 2 * PITCH
f32, bf16 = jnp.float32, jnp.bfloat16


def _sines(n):
    k = np.arange(1, n + 1)
    return np.sin(np.pi * ((k[:, None] * k[None, :]) % (2 * (n + 1))) / (n + 1))


def _lam(n):
    return 2.0 - 2.0 * np.cos(np.pi * np.arange(1, n + 1) / (n + 1))


@functools.cache
def _tables():
    sx, sy = _sines(NX), _sines(NY)
    order = np.array([s * WX + 4 * xb + xi for xi in range(4) for s in range(SLABS) for xb in range(WX // 4)])
    padded = np.zeros((SLABS * 64, NX))
    for s in range(SLABS):
        padded[s * 64 : s * 64 + WX] = sx[s * WX : (s + 1) * WX]
    ring_x = np.zeros((16, NX))
    ring_y = np.zeros((16, NY))
    for s in range(SLABS):
        if s > 0:
            ring_x[s] = sx[s * WX - 1]
        if s < SLABS - 1:
            ring_x[8 + s] = sx[(s + 1) * WX]
    for p in range(POIS):
        if p > 0:
            ring_y[p] = sy[p * WY - 1]
        if p < POIS - 1:
            ring_y[8 + p] = sy[(p + 1) * WY]
    back_x = np.concatenate([sx[order], padded, ring_x])
    modes = np.stack([_lam(NZ), sy.sum(1)])
    cast = lambda a: np.asarray(a, np.float32)

    def split(a):
        high = cast(a).astype(ml_dtypes.bfloat16)
        return high, (cast(a) - high.astype(np.float32)).astype(ml_dtypes.bfloat16)

    def wide(a):
        high, low = split(a)
        return np.concatenate([high, high, low], 1)

    high, low = split(sy)
    tiles = [np.arange(128) % (NZ // ORBS) + o * (NZ // ORBS) for o in range(ORBS)]
    stacked = np.concatenate([high, high, low], 0)
    return dict(
        beside=wide(sy),
        stacked=stacked,
        tiled=np.stack([stacked[:, t] for t in tiles]),
        forward_x=wide(sx[:, order]),
        back_x=wide(back_x),
        ring_y=wide(ring_y),
        col=cast(np.stack([_lam(NX), sx.sum(1)] + [np.zeros(NX)] * 6, 1)),
        row=cast(np.stack([_lam(NY), sy.sum(1)] + [np.zeros(NY)] * 6, 0)),
        modes=cast(modes),
    )


_VM = pl.BlockSpec(memory_space=pltpu.VMEM)
_SM = pl.BlockSpec(memory_space=pltpu.SMEM)
_ANY = pl.BlockSpec(memory_space=pl.ANY)
_HBM = pl.BlockSpec(memory_space=pltpu.HBM)
CORNERS = COMPS + 1
_X_FACE, _Y_FACE = (COMPS + 2, 2, WY, NZ), (COMPS + 1, 2, WX, NZ)
_FACES = [_X_FACE, _X_FACE, _Y_FACE, _Y_FACE]


def _iotas():
    return (
        lax.broadcasted_iota(jnp.int32, (8, 128), 0),
        lax.broadcasted_iota(jnp.int32, (8, 128), 1),
    )


def _zsum(v, lane):
    return jnp.where(lane == 0, 0.0, pltpu.roll(v, 1, 1)) + jnp.where(lane == 127, 0.0, pltpu.roll(v, 127, 1))


def _base(plane):
    return pl.multiple_of(8 + PITCH + PITCH * plane, 8)


def _split(value):
    high = value.astype(bf16)
    return high, (value - high.astype(f32)).astype(bf16)


def _faces_kernel(
    psi_hbm, ext, old, x_left, x_right, y_left, y_right, pot, psi, pots, rows, potential, x_edge, y_edge, sems, out_sems, pot_sem
):
    copies = [pltpu.make_async_copy(ref, pots.at[k], sems.at[k]) for k, ref in enumerate((ext, old))]
    copies += [pltpu.make_async_copy(psi_hbm.at[c], psi.at[c], sems.at[2 + c]) for c in range(COMPS)]
    for copy in copies:
        copy.start()
    sent = []

    def send(c, x_sources):
        sources = (*x_sources, y_edge.at[0, c], y_edge.at[1, c])
        for k, (source, ref) in enumerate(zip(sources, (x_left, x_right, y_left, y_right))):
            sent.append(pltpu.make_async_copy(source, ref.at[c], out_sems.at[c, k]))
            sent[-1].start()

    copies[0].wait()
    copies[1].wait()
    pots[0] = pots[0] + pots[1]
    potential[...] = 6.0 + 2.0 * pots[0]
    sent.append(pltpu.make_async_copy(potential, pot, pot_sem))
    sent[-1].start()
    for k in range(2):
        x_edge[0, k] = pots[k, 0:WY].astype(bf16)
        x_edge[1, k] = pots[k, WY * (WX - 1) : WY * WX].astype(bf16)
        y_edge[0, COMPS, k] = pots[k, pl.ds(0, WX, WY), :].astype(bf16)
        y_edge[1, COMPS, k] = pots[k, pl.ds(WY - 1, WX, WY), :].astype(bf16)
    send(COMPS, (x_edge.at[0], x_edge.at[1]))
    for c in range(COMPS):
        copies[2 + c].wait()

        def fill(x, carry, c=c):
            rows[0, pl.ds(pl.multiple_of(8 * x, 8), 8), :] = psi[c, x, 0:16, :].astype(f32)[0:8]
            rows[1, pl.ds(pl.multiple_of(8 * x, 8), 8), :] = psi[c, x, 16:32, :].astype(f32)[8:16]
            return carry

        lax.fori_loop(0, WX, fill, 0, unroll=WX)
        for half, first in ((0, 0), (1, 6)):
            for d in range(2):
                y_edge[half, c, d] = rows[half, pl.ds(first + d, WX, 8), :].astype(bf16)
        send(c, (psi.at[c, pl.ds(0, 2)], psi.at[c, pl.ds(WX - 2, 2)]))
    for copy in sent:
        copy.wait()


def _faces(psi, ext, old):
    return pl.pallas_call(
        _faces_kernel,
        name="faces",
        in_specs=[_HBM] * 3,
        out_specs=[_HBM] * 5,
        out_shape=[jax.ShapeDtypeStruct(s, bf16) for s in _FACES] + [jax.ShapeDtypeStruct((WX * WY, NZ), f32)],
        scratch_shapes=[
            pltpu.VMEM((COMPS, WX, WY, NZ), bf16),
            pltpu.VMEM((2, WX * WY, NZ), f32),
            pltpu.VMEM((2, 8 * WX, 128), f32),
            pltpu.VMEM((WX * WY, NZ), f32),
            pltpu.VMEM((2, 2, WY, NZ), bf16),
            pltpu.VMEM((2, COMPS + 1, 2, WX, NZ), bf16),
            pltpu.SemaphoreType.DMA((2 + COMPS,)),
            pltpu.SemaphoreType.DMA((COMPS + 1, 4)),
            pltpu.SemaphoreType.DMA,
        ],
        compiler_params=pltpu.CompilerParams(vmem_limit_bytes=VMEM_LIMIT - 5 * 1024 * 1024),
        cost_estimate=pl.CostEstimate(flops=1000000, bytes_accessed=6000000, transcendentals=0),
    )(psi, ext, old)


def _corners_kernel(x_left, x_right, y_low, y_high, after, left, right, block, entry, sems):
    del x_left, x_right, after
    copies = []
    for k, (out, first, row) in enumerate(((left, 0, 0), (right, WX - 16, 15))):
        for side, ref in enumerate((y_low, y_high)):
            for c in range(COMPS):
                cells = ref[c, 1 - side, first : first + 16].astype(f32)
                block[c : c + 1] = cells[row : row + 1]
            entry[k, side] = block[...].astype(bf16)
        copies.append(pltpu.make_async_copy(entry.at[k], out.at[CORNERS], sems.at[k]))
        copies[k].start()
    for copy in copies:
        copy.wait()


def _corners(x_left, x_right, y_low, y_high, after):
    shape = jax.ShapeDtypeStruct(_X_FACE, bf16)
    return pl.pallas_call(
        _corners_kernel,
        name="corners",
        in_specs=[_ANY, _ANY, _VM, _VM, _ANY],
        out_specs=[_ANY, _ANY],
        out_shape=[shape, shape],
        scratch_shapes=[
            pltpu.VMEM((WY, NZ), f32),
            pltpu.VMEM((2, 2, WY, NZ), bf16),
            pltpu.SemaphoreType.DMA((2,)),
        ],
        input_output_aliases={0: 0, 1: 1},
        compiler_params=pltpu.CompilerParams(vmem_limit_bytes=2 * 1024 * 1024),
        cost_estimate=pl.CostEstimate(flops=10000, bytes_accessed=200000, transcendentals=0),
    )(x_left, x_right, y_low, y_high, after)


def _inner_kernel(first_part, psi, pot, image, token, psi_f):
    ends = [lax.broadcasted_iota(jnp.int32, (NZ, NZ), k) for k in range(2)]
    near = jnp.where(jnp.abs(ends[0] - ends[1]) == 1, 1.0, 0.0).astype(bf16)
    token[...] = jnp.zeros((8, NZ), f32)
    count = image.shape[0]
    for c in range(count):

        def widen(x, carry, c=c):
            rows = pl.ds(pl.multiple_of(WY * x, WY), WY)
            psi_f[c, pl.ds(_base(x + 1), WY)] = psi[first_part + c, rows].astype(f32)
            return carry

        lax.fori_loop(0, WX, widen, 0, unroll=16)
        for side in range(2):
            psi_f[c, pl.ds(FIRST + (WY if side else -1), WX, PITCH)] = jnp.zeros((WX, NZ), f32)
            psi_f[c, pl.ds(FIRST - PITCH + (WX + 1) * PITCH * side, WY)] = jnp.zeros((WY, NZ), f32)

    def group(k, carry):
        c, j = k // (WX // GROUP), k % (WX // GROUP)
        start = pl.multiple_of(GROUP * WY * j, WY)
        sums = jnp.dot(
            psi[first_part + c, pl.ds(start, GROUP * WY)], near, preferred_element_type=f32
        )
        for g in range(GROUP):
            base = _base(GROUP * j + g + 1)
            for i in range(4):
                at = base + 8 * i
                load = lambda row: psi_f[c, pl.ds(row, 8)]
                beside = (load(at - 1) + load(at + 1)) + (load(at - PITCH) + load(at + PITCH))
                first = WY * g + 8 * i
                weight = pot[pl.ds(pl.multiple_of(start + first, 8), 8)]
                value = weight * load(pl.multiple_of(at, 8)) - (beside + sums[first : first + 8])
                image[c, pl.ds(pl.multiple_of(at, 8), 8)] = value
        return carry

    lax.fori_loop(0, count * (WX // GROUP), group, 0)


_IMAGES = [jax.ShapeDtypeStruct((n, PADDED, NZ), f32) for n in SHARE]


def _inner(which, psi, pot):
    return pl.pallas_call(
        functools.partial(_inner_kernel, SHARE[0] * which),
        name="inner",
        in_specs=[_VM] * 2,
        out_specs=[_VM, _VM],
        out_shape=[_IMAGES[which], jax.ShapeDtypeStruct((8, NZ), f32)],
        scratch_shapes=[pltpu.VMEM(_IMAGES[which].shape, f32)],
        compiler_params=pltpu.CompilerParams(vmem_limit_bytes=24 * 1024 * 1024),
        cost_estimate=pl.CostEstimate(flops=400000000, bytes_accessed=12000000, transcendentals=0),
    )(psi, pot)


def _inside():
    slab, pois = lax.axis_index("slab"), lax.axis_index("pois")
    number = lambda cond: jnp.where(cond, 1.0, 0.0).astype(f32)
    return (
        (number(slab > 0), number(slab < SLABS - 1)),
        (number(pois > 0), number(pois < POIS - 1)),
    )


def _place(part):
    return (0, part) if part < SHARE[0] else (1, part - SHARE[0])


def _stepped(cells, images, pot, orbital, at, lane):
    parts = []
    for k in range(2):
        load = lambda row, hint=True: images[k](pl.multiple_of(row, 8) if hint else row)
        u = load(at)
        total = (load(at - PITCH) + load(at + PITCH)) + (load(at - 1, False) + load(at + 1, False)) + _zsum(u, lane)
        parts.append((cells[k], u, pot * u - total))
    (a, ua, wa), (b, ub, wb) = parts
    scale = 0.125 * DT * DT
    return (a - scale * wa) + (0.5 * DT) * ub, (b - scale * wb) - (0.5 * DT) * ua


def _plane_charge(x, occ, psi, pot, halves, charge, totals, lane):
    for h in range(2):
        cells = [psi[c, pl.ds(pl.multiple_of(WY * x + 16 * h, 16), 16)].astype(f32) for c in range(COMPS)]
        for i in (2 * h, 2 * h + 1):
            r = slice(8 * (i % 2), 8 * (i % 2) + 8)
            row = pl.ds(pl.multiple_of(WY * x + 8 * i, 8), 8)
            weight = pot[row]
            sums = None
            for orbital in range(COMPS // 2):
                parts = (2 * orbital, 2 * orbital + 1)
                picked = [lambda at, c=c: halves[_place(c)[0]][_place(c)[1], pl.ds(at, 8)] for c in parts]
                own = [cells[c][r] for c in parts]
                real, imag = _stepped(own, picked, weight, orbital, _base(x + 1) + 8 * i, lane)
                term = occ[orbital] * (real * real + imag * imag)
                sums = term if sums is None else sums + term
            charge[row, :] = sums
            totals = totals + sums
    return totals


def _middle_kernel(occupations, psi, pot, image_a, image_b, y_low, y_high, own_low, own_high, a, b, charge, totals, column):
    del image_a, image_b
    _, lane = _iotas()
    _, in_y = _inside()
    y_faces, own = (y_low, y_high), (own_low, own_high)
    ring_y = [6.0 + 2.0 * f[COMPS, 0].astype(f32) for f in y_faces]
    column[...] = jnp.zeros_like(column)
    for half, image in enumerate((a, b)):

        def edges(c, carry, half=half, image=image):
            part = SHARE[0] * half + c
            for side in range(2):
                near = y_faces[side][part, 1 - side].astype(f32) * in_y[side]
                far = y_faces[side][part, side].astype(f32)
                inner = own[side][part, side].astype(f32)
                at = pl.ds(FIRST + (WY - 1) * side, WX, PITCH)
                image[c, at] = image[c, at] - near
                column[side, 8:56] = near
                total = (far + inner) + (column[side, 7:55] + column[side, 9:57])
                value = [
                    ring_y[side][r] * near[r] - (total[r] + _zsum(near[r], lane))
                    for r in (slice(8 * i, 8 * i + 8) for i in range(WX // 8))
                ]
                image[c, pl.ds(FIRST + (WY if side else -1), WX, PITCH)] = jnp.concatenate(value, axis=0) * in_y[side]
            return carry

        lax.fori_loop(0, SHARE[half], edges, 0)
    occ = [occupations[k] for k in range(COMPS // 2)]

    def pair(k, sums):
        for d in range(2):
            sums = _plane_charge(2 * k + d, occ, psi, pot, (a, b), charge, sums, lane)
        return sums

    totals[...] = lax.fori_loop(1, WX // 2 - 1, pair, jnp.zeros((8, 128), f32))


def _edge_kernel(
    occupations, beside, psi, pot, image_a, image_b, charge_in, totals, x_low, x_high, a, b, charge, message, column
):
    del image_a, image_b, charge_in
    _, lane = _iotas()
    in_x, in_y = _inside()
    x_faces = (x_low, x_high)
    ring_x = [6.0 + 2.0 * f[COMPS, 0].astype(f32) for f in x_faces]
    for i in range(2):
        for j in range(2):
            column[2 + 2 * i + j, 0:8] = x_faces[i][CORNERS, j].astype(f32)[0:8] * (in_x[i] * in_y[j])
    for half, image in enumerate((a, b)):

        def edges(c, carry, half=half, image=image):
            part = SHARE[0] * half + c
            for side in range(2):
                near = x_faces[side][part, 1 - side].astype(f32) * in_x[side]
                far = x_faces[side][part, side].astype(f32)
                inner = psi[part, pl.ds(WY * (WX - 1) * side, WY)].astype(f32)
                first = FIRST + PITCH * (WX - 1) * side
                image[c, pl.ds(first, WY)] = image[c, pl.ds(first, WY)] - near
                column[side, 8:40] = near
                for j, row in ((0, 7), (1, 40)):
                    corner = column[2 + 2 * side + j, pl.ds(part, 1)]
                    column[side, row : row + 1] = corner
                    at = pl.ds(first + (WY if j else -1), 1)
                    image[c, at] = image[c, at] - corner
                total = (far + inner) + (column[side, 7:39] + column[side, 9:41])
                for i in range(4):
                    r = slice(8 * i, 8 * i + 8)
                    ring = ring_x[side][r] * near[r] - (total[r] + _zsum(near[r], lane))
                    image[c, pl.ds(FIRST - PITCH + PITCH * (WX + 1) * side + 8 * i, 8)] = ring * in_x[side]
            return carry

        lax.fori_loop(0, SHARE[half], edges, 0)
    occ = [occupations[k] for k in range(COMPS // 2)]

    def pair(k, sums):
        for d in range(2):
            x = (WX - 2) * k + d
            sums = _plane_charge(x, occ, psi, pot, (a, b), charge, sums, lane)
        return sums

    sums = lax.fori_loop(0, 2, pair, totals[...])
    mean = jnp.broadcast_to(jnp.sum(sums, keepdims=True) / (WX * WY * NZ), (8, 128))

    def group(g, carry):
        cells = charge[pl.ds(pl.multiple_of(256 * g, 256), 256), :] - mean[0:1]
        high, low = _split(cells)
        modes = lax.dot_general(
            beside[...],
            jnp.concatenate([high, low, high], axis=1),
            (((1,), (1,)), ((), ())),
            preferred_element_type=f32,
        )
        for k in range(16):
            for h in range(2):
                piece = modes[8 * k : 8 * k + 8, 128 * h : 128 * h + 128]
                message[pl.ds(8 * FWD * k + 2 * g + h, 8, FWD), :] = piece
        return carry

    lax.fori_loop(0, WX // 8, group, 0, unroll=2)
    for k in range(16):
        message[pl.ds(8 * FWD * k + FWD - 1, 8, FWD), :] = mean


_CHARGE = jax.ShapeDtypeStruct((WX * WY, NZ), f32)


def _middle(occupations, psi, pot, image_a, image_b, *faces):
    return pl.pallas_call(
        _middle_kernel,
        name="middle",
        in_specs=[_SM] + [_VM] * 8,
        out_specs=[_VM] * 4,
        out_shape=[*_IMAGES, _CHARGE, jax.ShapeDtypeStruct((8, NZ), f32)],
        scratch_shapes=[pltpu.VMEM((2, 64, NZ), f32)],
        input_output_aliases={3: 0, 4: 1},
        compiler_params=pltpu.CompilerParams(vmem_limit_bytes=16 * 1024 * 1024),
        cost_estimate=pl.CostEstimate(flops=100000000, bytes_accessed=8000000, transcendentals=0),
    )(occupations, psi, pot, image_a, image_b, *faces)


def _edge_messages(occupations, psi, pot, image_a, image_b, charge, totals, x_low, x_high):
    return pl.pallas_call(
        _edge_kernel,
        name="edge",
        in_specs=[_SM] + [_VM] * 9,
        out_specs=[_VM] * 4,
        out_shape=[*_IMAGES, _CHARGE, jax.ShapeDtypeStruct((DEVICES * FWD, 128), f32)],
        scratch_shapes=[pltpu.VMEM((6, 64, NZ), f32)],
        input_output_aliases={4: 0, 5: 1, 6: 2},
        compiler_params=pltpu.CompilerParams(vmem_limit_bytes=16 * 1024 * 1024),
        cost_estimate=pl.CostEstimate(flops=100000000, bytes_accessed=8000000, transcendentals=0),
    )(occupations, jnp.asarray(_tables()["beside"]), psi, pot, image_a, image_b, charge, totals, x_low, x_high)


def _swap_groups(blocks, group):
    out = []
    for i in range(4):
        value = None
        for j in range(4):
            shift = (32 * (j - i)) % 128
            moved = pltpu.roll(blocks[j], shift, 1) if shift else blocks[j]
            value = moved if value is None else jnp.where(group == j, moved, value)
        out.append(value)
    return out


def _plane_kernel(modes, recv, forward_x, stacked, back_x, ring_y, col, row, send, packed, block):
    dot = functools.partial(jnp.dot, preferred_element_type=f32)

    def parts(value, axis):
        high, low = _split(value)
        return jnp.concatenate([high, low, high], axis=axis)

    left = lambda table, value: dot(table[...], parts(value, 0))
    right = lambda value: dot(parts(value, 1), stacked[...])
    nt = lambda table, value: lax.dot_general(
        table[...], parts(value, 1), (((1,), (1,)), ((), ())), preferred_element_type=f32
    )
    kz = (lax.axis_index("orb") * POIS + lax.axis_index("pois")) * SLABS + lax.axis_index("slab")
    lam_z, sum_z = modes[0, kz], modes[1, kz]
    means = recv[pl.ds(FWD - 1, DEVICES, FWD), :]
    blocks = POIS * SLABS
    block_mean = sum(means[blocks * o : blocks * (o + 1)] for o in range(ORBS))
    mean = jnp.sum(block_mean, axis=0, keepdims=True) / blocks
    block_means = [block_mean[k : k + 1] for k in range(blocks)]
    for p in range(POIS):
        for s in range(SLABS):
            first = [((o * POIS + p) * SLABS + s) * FWD for o in range(ORBS)]
            shift = sum_z * (block_means[p * SLABS + s][0:1] - mean)
            packed[p, pl.ds(12 * s, 8), :] = sum(recv[pl.ds(r, 8), :] for r in first) + shift
            last = sum(recv[pl.ds(r + FWD - 8, 8), :] for r in first) + shift
            packed[p, pl.ds(12 * s + 8, 4), :] = last[3:7]
    group = lax.broadcasted_iota(jnp.int32, (WX, 128), 1) // 32
    plane = jnp.concatenate(_swap_groups([packed[p, 0:WX] for p in range(POIS)], group), axis=0)
    spectrum = right(left(forward_x, plane))
    divisor = col[:, 0:1] + row[0:1, :] + lam_z
    factor = 32.0 * math.pi / ((NX + 1) * (NY + 1) * (NZ + 1))
    scaled = spectrum * factor / divisor
    across = left(back_x, scaled)
    field = right(across[:NX])
    ring = right(across[NX + 256 :])
    cells = _swap_groups([field[WX * i : WX * (i + 1)] for i in range(4)], group)
    lane8 = lax.broadcasted_iota(jnp.int32, (8, 128), 1)
    group8 = lane8 // 32
    faces = [nt(ring_y, across[NX + 128 * h : NX + 128 * (h + 1)]) for h in range(2)]
    y_rows = []
    for s in range(SLABS):
        low, high = faces[s // 2][0:8], faces[s // 2][8:16]
        if s % 2 == 0:
            high = pltpu.roll(high, 64, 1)
        else:
            low = pltpu.roll(low, 64, 1)
        y_rows.append(jnp.where(lane8 < 64, low, high))
    for p in range(POIS):
        shift = lambda v, k: pltpu.roll(v, k % 128, 1) if k % 128 else v
        x_rows = jnp.where(
            group8 == 0,
            shift(ring[0:8], -32 * p),
            jnp.where(group8 == 1, shift(ring[8:16], 32 - 32 * p), 0.0),
        )
        for s in range(SLABS):
            base = (p * SLABS + s) * BACK
            block[pl.ds(base, 12), :] = cells[p][12 * s : 12 * s + 12]
            block[pl.ds(base + 12, 1), :] = x_rows[s : s + 1]
            block[pl.ds(base + 13, 1), :] = y_rows[s][p : p + 1]
    count = POIS * SLABS * BACK
    for o in range(ORBS):
        send[pl.ds(o * count, count), :] = block[0:count]


def _plane(recv):
    t = _tables()
    return pl.pallas_call(
        _plane_kernel,
        name="plane",
        in_specs=[_SM] + [_VM] * 7,
        out_specs=_VM,
        out_shape=jax.ShapeDtypeStruct((DEVICES * BACK, 128), f32),
        scratch_shapes=[
            pltpu.VMEM((POIS, WX + 8, 128), f32),
            pltpu.VMEM((POIS * SLABS * BACK + 16, 128), f32),
        ],
        compiler_params=pltpu.CompilerParams(vmem_limit_bytes=8 * 1024 * 1024),
        cost_estimate=pl.CostEstimate(flops=200000000, bytes_accessed=3000000, transcendentals=0),
    )(
        jnp.asarray(t["modes"]),
        recv,
        *(jnp.asarray(t[k]) for k in ("forward_x", "stacked", "back_x", "ring_y", "col", "row")),
    )


OUT_GROUP = 4


def _step_kernel(
    stacked, recv, tiled, image_a, image_b, psi, ext, old, x_low, x_high, y_low, y_high,
    new, hartree, image, pot, change, ring_y, tables, slices, out, out_sems,
):
    faces = (x_low, x_high, y_low, y_high)
    in_x, in_y = _inside()
    sub, lane = _iotas()
    tables[:, 0:128] = stacked[...]
    tables[:, 128:256] = tiled[lax.axis_index("orb")]

    def back(r, table):
        high, low = _split(recv[pl.ds(r, 128, BACK), :])
        stack = jnp.concatenate([high, low, high], axis=0)
        return lax.dot_general(stack, table[...], (((0,), (0,)), ((), ())), preferred_element_type=f32)

    def planes(g, carry):
        both = back(g, tables)
        field, mine = both[:, 0:128], both[:, 128:256]
        first = pl.multiple_of(4 * WY * g, 8)
        block = pl.ds(first, 4 * WY)
        moved = pl.ds(pl.multiple_of(first + WY, 8), 4 * WY)
        pot[moved] = 6.0 + (2.0 * ext[block] + (old[block] + field))
        change[moved] = field - old[block]
        for k in range(16):
            kept_lanes = jnp.where(lane // 16 == sub, mine[8 * k : 8 * k + 8], 0.0)
            slices[k % 4, pl.ds(4 * g + k // 4, 1), :] = jnp.sum(kept_lanes, axis=0, keepdims=True)
        return carry

    lax.fori_loop(0, WX // 4, planes, 0, unroll=2)
    x_field, y_field = back(12, stacked), back(13, stacked)
    for side in range(2):
        edge = pl.ds((WX + 1) * WY * side, WY)
        change[edge] = (x_field[32 * side : 32 * side + 32] - faces[side][COMPS, 1].astype(f32)) * in_x[side]
        ring_y[side] = (y_field[64 * side : 64 * side + WX] - faces[2 + side][COMPS, 1].astype(f32)) * in_y[side]
    for q in range(4):
        turned = jnp.transpose(slices[q])
        for y in range(8):
            hartree[8 * q + y] = turned[16 * y : 16 * y + 16, 0:WX]

    for half, start in enumerate((image_a, image_b)):

        def one(c, carry, half=half, start=start):
            part = SHARE[0] * half + c

            def planes_of(j, carry):
                for k in range(6):
                    x = 6 * j + k
                    value = psi[part, pl.ds(pl.multiple_of(WY * x, WY), WY)].astype(f32)
                    at = pl.ds(_base(x + 1), WY)
                    image[part, at] = start[c, at] + change[pl.ds(pl.multiple_of(WY * (x + 1), WY), WY)] * value
                return carry

            lax.fori_loop(0, WX // 6, planes_of, 0)
            for side in range(2):
                at = pl.ds(FIRST - PITCH + PITCH * (WX + 1) * side, WY)
                value = faces[side][part, 1 - side].astype(f32)
                image[part, at] = start[c, at] + change[pl.ds((WX + 1) * WY * side, WY)] * value
                at = pl.ds(FIRST + (WY if side else -1), WX, PITCH)
                image[part, at] = start[c, at] + ring_y[side] * faces[2 + side][part, 1 - side].astype(f32)
            return carry

        lax.fori_loop(0, SHARE[half], one, 0)

    def out_copy(j, c):
        planes = pl.ds(OUT_GROUP * j, OUT_GROUP)
        return pltpu.make_async_copy(out.at[c, planes], new.at[c, planes], out_sems.at[j, c])

    def group(j, carry):
        def pair(k, carry):
            for d in range(2):
                x = OUT_GROUP * j + 2 * k + d
                for h in range(2):
                    rows = pl.ds(pl.multiple_of(WY * x + 16 * h, 16), 16)
                    cells = [psi[c, rows].astype(f32) for c in range(COMPS)]
                    for i in (2 * h, 2 * h + 1):
                        r = slice(8 * (i % 2), 8 * (i % 2) + 8)
                        weight = pot[pl.ds(pl.multiple_of(WY * (x + 1) + 8 * i, 8), 8)]
                        for orbital in range(COMPS // 2):
                            parts = (2 * orbital, 2 * orbital + 1)
                            picked = [lambda row, c=c: image[c, pl.ds(row, 8)] for c in parts]
                            own = [cells[c][r] for c in parts]
                            real, imag = _stepped(own, picked, weight, orbital, _base(x + 1) + 8 * i, lane)
                            out[2 * orbital, x, 8 * i : 8 * i + 8] = real
                            out[2 * orbital + 1, x, 8 * i : 8 * i + 8] = imag
            return carry

        lax.fori_loop(0, OUT_GROUP // 2, pair, 0)
        for c in range(COMPS):
            out_copy(j, c).start()
        return carry

    lax.fori_loop(0, WX // OUT_GROUP, group, 0)
    for j in range(WX // OUT_GROUP):
        for c in range(COMPS):
            out_copy(j, c).wait()


def _step(recv, *arrays):
    t = _tables()
    return pl.pallas_call(
        _step_kernel,
        name="step",
        in_specs=[_VM] * (3 + len(arrays)),
        out_specs=[_HBM, _VM],
        out_shape=[
            jax.ShapeDtypeStruct((COMPS, WX, WY, NZ), f32),
            jax.ShapeDtypeStruct((WY, NZ // ORBS, WX), f32),
        ],
        scratch_shapes=[
            pltpu.VMEM((COMPS, PADDED, NZ), f32),
            pltpu.VMEM((PLANES * WY, NZ), f32),
            pltpu.VMEM((PLANES * WY, NZ), f32),
            pltpu.VMEM((2, WX, NZ), f32),
            pltpu.VMEM((3 * NZ, 256), bf16),
            pltpu.VMEM((4, 128, 128), f32),
            pltpu.VMEM((COMPS, WX, WY, NZ), f32),
            pltpu.SemaphoreType.DMA((WX // OUT_GROUP, COMPS)),
        ],
        compiler_params=pltpu.CompilerParams(vmem_limit_bytes=24 * 1024 * 1024),
        cost_estimate=pl.CostEstimate(flops=100000000, bytes_accessed=20000000, transcendentals=0),
    )(jnp.asarray(t["stacked"]), recv, jnp.asarray(t["tiled"]), *arrays)


def _shifted(value, axis, count, step):
    return lax.ppermute(value, axis, [(i, (i + step) % count) for i in range(count)])


def _swap(messages, rows):
    moved = lax.all_to_all(messages.reshape(DEVICES, 1, rows * 128), TRANSPOSE_AXES, 0, 0)
    return moved.reshape(DEVICES * rows, 128)


def body(orbitals, occupations, ext_pot, hartree_old):
    psi = orbitals.reshape(COMPS, WX * WY, NZ)
    ext, old = ext_pot.reshape(WX * WY, NZ), hartree_old.reshape(WX * WY, NZ)
    x_left, x_right, y_left, y_right, pot = _faces(orbitals.reshape(COMPS, WX, WY, NZ), ext, old)
    y_low = _shifted(y_right, "pois", POIS, 1)
    y_high = _shifted(y_left, "pois", POIS, -1)
    image_a, done = _inner(0, psi, pot)
    x_left, x_right = _corners(x_left, x_right, y_low, y_high, done)
    x_low = _shifted(x_right, "slab", SLABS, 1)
    x_high = _shifted(x_left, "slab", SLABS, -1)
    image_b, _ = _inner(1, psi, pot)
    image_a, image_b, charge, totals = _middle(occupations, psi, pot, image_a, image_b, y_low, y_high, y_left, y_right)
    image_a, image_b, _, message = _edge_messages(
        occupations, psi, pot, image_a, image_b, charge, totals, x_low, x_high
    )
    faces = (x_low, x_high, y_low, y_high)
    back = _swap(_plane(_swap(message, FWD)), BACK)
    new, hartree = _step(back, image_a, image_b, psi, ext, old, *faces)
    return new.reshape(orbitals.shape), jnp.transpose(hartree, (2, 0, 1))


def solution(mesh):
    placed = (P("orb", None, "slab", "pois", None), P("orb"), P("slab", "pois", None), P("slab", "pois", None))
    return jax.shard_map(
        body,
        mesh=mesh,
        in_specs=placed,
        out_specs=(P("orb", None, "slab", "pois", None), P("slab", "pois", "orb")),
        check_vma=False,
    )
```

```python
import functools
import math

import jax
import jax.numpy as jnp
import ml_dtypes
import numpy as np
from jax import lax
from jax.experimental import pallas as pl
from jax.experimental.pallas import tpu as pltpu
from jax.sharding import PartitionSpec as P

NX, NY, NZ = 192, 128, 128
SLABS, ORBS, POIS = 4, 8, 4
WX, WY = NX // SLABS, NY // POIS
COMPS = 8
FWD = 13
BACK = 14
DEVICES = SLABS * ORBS * POIS
TRANSPOSE_AXES = ("orb", "pois", "slab")
DT = 0.3
VMEM_LIMIT = 67043328

PITCH = 40
PLANES = WX + 2
PADDED = 8 + (PLANES + 2) * PITCH
GROUP = 24
SHARE = (7, 1)
FIRST = 8 + 2 * PITCH
f32, bf16 = jnp.float32, jnp.bfloat16


def _sines(n):
    k = np.arange(1, n + 1)
    return np.sin(np.pi * ((k[:, None] * k[None, :]) % (2 * (n + 1))) / (n + 1))


def _lam(n):
    return 2.0 - 2.0 * np.cos(np.pi * np.arange(1, n + 1) / (n + 1))


@functools.cache
def _tables():
    sx, sy = _sines(NX), _sines(NY)
    order = np.array([s * WX + 4 * xb + xi for xi in range(4) for s in range(SLABS) for xb in range(WX // 4)])
    padded = np.zeros((SLABS * 64, NX))
    for s in range(SLABS):
        padded[s * 64 : s * 64 + WX] = sx[s * WX : (s + 1) * WX]
    ring_x = np.zeros((16, NX))
    ring_y = np.zeros((16, NY))
    for s in range(SLABS):
        if s > 0:
            ring_x[s] = sx[s * WX - 1]
        if s < SLABS - 1:
            ring_x[8 + s] = sx[(s + 1) * WX]
    for p in range(POIS):
        if p > 0:
            ring_y[p] = sy[p * WY - 1]
        if p < POIS - 1:
            ring_y[8 + p] = sy[(p + 1) * WY]
    back_x = np.concatenate([sx[order], padded, ring_x])
    modes = np.stack([_lam(NZ), sy.sum(1)])
    cast = lambda a: np.asarray(a, np.float32)

    def split(a):
        high = cast(a).astype(ml_dtypes.bfloat16)
        return high, (cast(a) - high.astype(np.float32)).astype(ml_dtypes.bfloat16)

    def wide(a):
        high, low = split(a)
        return np.concatenate([high, high, low], 1)

    high, low = split(sy)
    tiles = [np.arange(128) % (NZ // ORBS) + o * (NZ // ORBS) for o in range(ORBS)]
    stacked = np.concatenate([high, high, low], 0)
    return dict(
        beside=wide(sy),
        stacked=stacked,
        tiled=np.stack([stacked[:, t] for t in tiles]),
        forward_x=wide(sx[:, order]),
        back_x=wide(back_x),
        ring_y=wide(ring_y),
        col=cast(np.stack([_lam(NX), sx.sum(1)] + [np.zeros(NX)] * 6, 1)),
        row=cast(np.stack([_lam(NY), sy.sum(1)] + [np.zeros(NY)] * 6, 0)),
        modes=cast(modes),
    )


_VM = pl.BlockSpec(memory_space=pltpu.VMEM)
_SM = pl.BlockSpec(memory_space=pltpu.SMEM)
_ANY = pl.BlockSpec(memory_space=pl.ANY)
_HBM = pl.BlockSpec(memory_space=pltpu.HBM)
CORNERS = COMPS + 1
_X_FACE, _Y_FACE = (COMPS + 2, 2, WY, NZ), (COMPS + 1, 2, WX, NZ)
_FACES = [_X_FACE, _X_FACE, _Y_FACE, _Y_FACE]


def _iotas():
    return (
        lax.broadcasted_iota(jnp.int32, (8, 128), 0),
        lax.broadcasted_iota(jnp.int32, (8, 128), 1),
    )


def _zsum(v, lane):
    return jnp.where(lane == 0, 0.0, pltpu.roll(v, 1, 1)) + jnp.where(lane == 127, 0.0, pltpu.roll(v, 127, 1))


def _base(plane):
    return pl.multiple_of(8 + PITCH + PITCH * plane, 8)


def _split(value):
    high = value.astype(bf16)
    return high, (value - high.astype(f32)).astype(bf16)


def _faces_kernel(
    psi_hbm, ext, old, x_left, x_right, y_left, y_right, pot, psi, pots, rows, potential, x_edge, y_edge, sems, out_sems, pot_sem
):
    copies = [pltpu.make_async_copy(ref, pots.at[k], sems.at[k]) for k, ref in enumerate((ext, old))]
    copies += [pltpu.make_async_copy(psi_hbm.at[c], psi.at[c], sems.at[2 + c]) for c in range(COMPS)]
    for copy in copies:
        copy.start()
    sent = []

    def send(c, x_sources):
        sources = (*x_sources, y_edge.at[0, c], y_edge.at[1, c])
        for k, (source, ref) in enumerate(zip(sources, (x_left, x_right, y_left, y_right))):
            sent.append(pltpu.make_async_copy(source, ref.at[c], out_sems.at[c, k]))
            sent[-1].start()

    copies[0].wait()
    copies[1].wait()
    pots[0] = pots[0] + pots[1]
    potential[...] = 6.0 + 2.0 * pots[0]
    sent.append(pltpu.make_async_copy(potential, pot, pot_sem))
    sent[-1].start()
    for k in range(2):
        x_edge[0, k] = pots[k, 0:WY].astype(bf16)
        x_edge[1, k] = pots[k, WY * (WX - 1) : WY * WX].astype(bf16)
        y_edge[0, COMPS, k] = pots[k, pl.ds(0, WX, WY), :].astype(bf16)
        y_edge[1, COMPS, k] = pots[k, pl.ds(WY - 1, WX, WY), :].astype(bf16)
    send(COMPS, (x_edge.at[0], x_edge.at[1]))
    for c in range(COMPS):
        copies[2 + c].wait()

        def fill(x, carry, c=c):
            rows[0, pl.ds(pl.multiple_of(8 * x, 8), 8), :] = psi[c, x, 0:16, :].astype(f32)[0:8]
            rows[1, pl.ds(pl.multiple_of(8 * x, 8), 8), :] = psi[c, x, 16:32, :].astype(f32)[8:16]
            return carry

        lax.fori_loop(0, WX, fill, 0, unroll=WX)
        for half, first in ((0, 0), (1, 6)):
            for d in range(2):
                y_edge[half, c, d] = rows[half, pl.ds(first + d, WX, 8), :].astype(bf16)
        send(c, (psi.at[c, pl.ds(0, 2)], psi.at[c, pl.ds(WX - 2, 2)]))
    for copy in sent:
        copy.wait()


def _faces(psi, ext, old):
    return pl.pallas_call(
        _faces_kernel,
        name="faces",
        in_specs=[_HBM] * 3,
        out_specs=[_HBM] * 5,
        out_shape=[jax.ShapeDtypeStruct(s, bf16) for s in _FACES] + [jax.ShapeDtypeStruct((WX * WY, NZ), f32)],
        scratch_shapes=[
            pltpu.VMEM((COMPS, WX, WY, NZ), bf16),
            pltpu.VMEM((2, WX * WY, NZ), f32),
            pltpu.VMEM((2, 8 * WX, 128), f32),
            pltpu.VMEM((WX * WY, NZ), f32),
            pltpu.VMEM((2, 2, WY, NZ), bf16),
            pltpu.VMEM((2, COMPS + 1, 2, WX, NZ), bf16),
            pltpu.SemaphoreType.DMA((2 + COMPS,)),
            pltpu.SemaphoreType.DMA((COMPS + 1, 4)),
            pltpu.SemaphoreType.DMA,
        ],
        compiler_params=pltpu.CompilerParams(vmem_limit_bytes=VMEM_LIMIT - 5 * 1024 * 1024),
        cost_estimate=pl.CostEstimate(flops=1000000, bytes_accessed=6000000, transcendentals=0),
    )(psi, ext, old)


def _corners_kernel(x_left, x_right, y_low, y_high, after, left, right, block, entry, sems):
    del x_left, x_right, after
    copies = []
    for k, (out, first, row) in enumerate(((left, 0, 0), (right, WX - 16, 15))):
        for side, ref in enumerate((y_low, y_high)):
            for c in range(COMPS):
                cells = ref[c, 1 - side, first : first + 16].astype(f32)
                block[c : c + 1] = cells[row : row + 1]
            entry[k, side] = block[...].astype(bf16)
        copies.append(pltpu.make_async_copy(entry.at[k], out.at[CORNERS], sems.at[k]))
        copies[k].start()
    for copy in copies:
        copy.wait()


def _corners(x_left, x_right, y_low, y_high, after):
    shape = jax.ShapeDtypeStruct(_X_FACE, bf16)
    return pl.pallas_call(
        _corners_kernel,
        name="corners",
        in_specs=[_ANY, _ANY, _VM, _VM, _ANY],
        out_specs=[_ANY, _ANY],
        out_shape=[shape, shape],
        scratch_shapes=[
            pltpu.VMEM((WY, NZ), f32),
            pltpu.VMEM((2, 2, WY, NZ), bf16),
            pltpu.SemaphoreType.DMA((2,)),
        ],
        input_output_aliases={0: 0, 1: 1},
        compiler_params=pltpu.CompilerParams(vmem_limit_bytes=2 * 1024 * 1024),
        cost_estimate=pl.CostEstimate(flops=10000, bytes_accessed=200000, transcendentals=0),
    )(x_left, x_right, y_low, y_high, after)


def _inner_kernel(first_part, psi, pot, image, token, psi_f):
    ends = [lax.broadcasted_iota(jnp.int32, (NZ, NZ), k) for k in range(2)]
    near = jnp.where(jnp.abs(ends[0] - ends[1]) == 1, 1.0, 0.0).astype(bf16)
    token[...] = jnp.zeros((8, NZ), f32)
    count = image.shape[0]
    for c in range(count):

        def widen(x, carry, c=c):
            rows = pl.ds(pl.multiple_of(WY * x, WY), WY)
            psi_f[c, pl.ds(_base(x + 1), WY)] = psi[first_part + c, rows].astype(f32)
            return carry

        lax.fori_loop(0, WX, widen, 0, unroll=16)
        for side in range(2):
            psi_f[c, pl.ds(FIRST + (WY if side else -1), WX, PITCH)] = jnp.zeros((WX, NZ), f32)
            psi_f[c, pl.ds(FIRST - PITCH + (WX + 1) * PITCH * side, WY)] = jnp.zeros((WY, NZ), f32)

    def group(k, carry):
        c, j = k // (WX // GROUP), k % (WX // GROUP)
        start = pl.multiple_of(GROUP * WY * j, WY)
        sums = jnp.dot(
            psi[first_part + c, pl.ds(start, GROUP * WY)], near, preferred_element_type=f32
        )
        for g in range(GROUP):
            base = _base(GROUP * j + g + 1)
            for i in range(4):
                at = base + 8 * i
                load = lambda row: psi_f[c, pl.ds(row, 8)]
                beside = (load(at - 1) + load(at + 1)) + (load(at - PITCH) + load(at + PITCH))
                first = WY * g + 8 * i
                weight = pot[pl.ds(pl.multiple_of(start + first, 8), 8)]
                value = weight * load(pl.multiple_of(at, 8)) - (beside + sums[first : first + 8])
                image[c, pl.ds(pl.multiple_of(at, 8), 8)] = value
        return carry

    lax.fori_loop(0, count * (WX // GROUP), group, 0)


_IMAGES = [jax.ShapeDtypeStruct((n, PADDED, NZ), f32) for n in SHARE]


def _inner(which, psi, pot):
    return pl.pallas_call(
        functools.partial(_inner_kernel, SHARE[0] * which),
        name="inner",
        in_specs=[_VM] * 2,
        out_specs=[_VM, _VM],
        out_shape=[_IMAGES[which], jax.ShapeDtypeStruct((8, NZ), f32)],
        scratch_shapes=[pltpu.VMEM(_IMAGES[which].shape, f32)],
        compiler_params=pltpu.CompilerParams(vmem_limit_bytes=24 * 1024 * 1024),
        cost_estimate=pl.CostEstimate(flops=400000000, bytes_accessed=12000000, transcendentals=0),
    )(psi, pot)


def _inside():
    slab, pois = lax.axis_index("slab"), lax.axis_index("pois")
    number = lambda cond: jnp.where(cond, 1.0, 0.0).astype(f32)
    return (
        (number(slab > 0), number(slab < SLABS - 1)),
        (number(pois > 0), number(pois < POIS - 1)),
    )


def _place(part):
    return (0, part) if part < SHARE[0] else (1, part - SHARE[0])


def _stepped(cells, images, pot, orbital, at, lane):
    parts = []
    for k in range(2):
        load = lambda row, hint=True: images[k](pl.multiple_of(row, 8) if hint else row)
        u = load(at)
        total = (load(at - PITCH) + load(at + PITCH)) + (load(at - 1, False) + load(at + 1, False)) + _zsum(u, lane)
        parts.append((cells[k], u, pot * u - total))
    (a, ua, wa), (b, ub, wb) = parts
    scale = 0.125 * DT * DT
    return (a - scale * wa) + (0.5 * DT) * ub, (b - scale * wb) - (0.5 * DT) * ua


def _plane_charge(x, occ, psi, pot, halves, charge, totals, lane):
    for h in range(2):
        cells = [psi[c, pl.ds(pl.multiple_of(WY * x + 16 * h, 16), 16)].astype(f32) for c in range(COMPS)]
        for i in (2 * h, 2 * h + 1):
            r = slice(8 * (i % 2), 8 * (i % 2) + 8)
            row = pl.ds(pl.multiple_of(WY * x + 8 * i, 8), 8)
            weight = pot[row]
            sums = None
            for orbital in range(COMPS // 2):
                parts = (2 * orbital, 2 * orbital + 1)
                picked = [lambda at, c=c: halves[_place(c)[0]][_place(c)[1], pl.ds(at, 8)] for c in parts]
                own = [cells[c][r] for c in parts]
                real, imag = _stepped(own, picked, weight, orbital, _base(x + 1) + 8 * i, lane)
                term = occ[orbital] * (real * real + imag * imag)
                sums = term if sums is None else sums + term
            charge[row, :] = sums
            totals = totals + sums
    return totals


def _middle_kernel(occupations, psi, pot, image_a, image_b, y_low, y_high, own_low, own_high, a, b, charge, totals, column):
    del image_a, image_b
    _, lane = _iotas()
    _, in_y = _inside()
    y_faces, own = (y_low, y_high), (own_low, own_high)
    ring_y = [6.0 + 2.0 * f[COMPS, 0].astype(f32) for f in y_faces]
    column[...] = jnp.zeros_like(column)
    for half, image in enumerate((a, b)):

        def edges(c, carry, half=half, image=image):
            part = SHARE[0] * half + c
            for side in range(2):
                near = y_faces[side][part, 1 - side].astype(f32) * in_y[side]
                far = y_faces[side][part, side].astype(f32)
                inner = own[side][part, side].astype(f32)
                at = pl.ds(FIRST + (WY - 1) * side, WX, PITCH)
                image[c, at] = image[c, at] - near
                column[side, 8:56] = near
                total = (far + inner) + (column[side, 7:55] + column[side, 9:57])
                value = [
                    ring_y[side][r] * near[r] - (total[r] + _zsum(near[r], lane))
                    for r in (slice(8 * i, 8 * i + 8) for i in range(WX // 8))
                ]
                image[c, pl.ds(FIRST + (WY if side else -1), WX, PITCH)] = jnp.concatenate(value, axis=0) * in_y[side]
            return carry

        lax.fori_loop(0, SHARE[half], edges, 0)
    occ = [occupations[k] for k in range(COMPS // 2)]

    def pair(k, sums):
        for d in range(2):
            sums = _plane_charge(2 * k + d, occ, psi, pot, (a, b), charge, sums, lane)
        return sums

    totals[...] = lax.fori_loop(1, WX // 2 - 1, pair, jnp.zeros((8, 128), f32))


def _edge_kernel(
    occupations, beside, psi, pot, image_a, image_b, charge_in, totals, x_low, x_high, a, b, charge, message, column
):
    del image_a, image_b, charge_in
    _, lane = _iotas()
    in_x, in_y = _inside()
    x_faces = (x_low, x_high)
    ring_x = [6.0 + 2.0 * f[COMPS, 0].astype(f32) for f in x_faces]
    for i in range(2):
        for j in range(2):
            column[2 + 2 * i + j, 0:8] = x_faces[i][CORNERS, j].astype(f32)[0:8] * (in_x[i] * in_y[j])
    for half, image in enumerate((a, b)):

        def edges(c, carry, half=half, image=image):
            part = SHARE[0] * half + c
            for side in range(2):
                near = x_faces[side][part, 1 - side].astype(f32) * in_x[side]
                far = x_faces[side][part, side].astype(f32)
                inner = psi[part, pl.ds(WY * (WX - 1) * side, WY)].astype(f32)
                first = FIRST + PITCH * (WX - 1) * side
                image[c, pl.ds(first, WY)] = image[c, pl.ds(first, WY)] - near
                column[side, 8:40] = near
                for j, row in ((0, 7), (1, 40)):
                    corner = column[2 + 2 * side + j, pl.ds(part, 1)]
                    column[side, row : row + 1] = corner
                    at = pl.ds(first + (WY if j else -1), 1)
                    image[c, at] = image[c, at] - corner
                total = (far + inner) + (column[side, 7:39] + column[side, 9:41])
                for i in range(4):
                    r = slice(8 * i, 8 * i + 8)
                    ring = ring_x[side][r] * near[r] - (total[r] + _zsum(near[r], lane))
                    image[c, pl.ds(FIRST - PITCH + PITCH * (WX + 1) * side + 8 * i, 8)] = ring * in_x[side]
            return carry

        lax.fori_loop(0, SHARE[half], edges, 0)
    occ = [occupations[k] for k in range(COMPS // 2)]

    def pair(k, sums):
        for d in range(2):
            x = (WX - 2) * k + d
            sums = _plane_charge(x, occ, psi, pot, (a, b), charge, sums, lane)
        return sums

    sums = lax.fori_loop(0, 2, pair, totals[...])
    mean = jnp.broadcast_to(jnp.sum(sums, keepdims=True) / (WX * WY * NZ), (8, 128))

    def group(g, carry):
        cells = charge[pl.ds(pl.multiple_of(256 * g, 256), 256), :] - mean[0:1]
        high, low = _split(cells)
        modes = lax.dot_general(
            beside[...],
            jnp.concatenate([high, low, high], axis=1),
            (((1,), (1,)), ((), ())),
            preferred_element_type=f32,
        )
        for k in range(16):
            for h in range(2):
                piece = modes[8 * k : 8 * k + 8, 128 * h : 128 * h + 128]
                message[pl.ds(8 * FWD * k + 2 * g + h, 8, FWD), :] = piece
        return carry

    lax.fori_loop(0, WX // 8, group, 0, unroll=2)
    for k in range(16):
        message[pl.ds(8 * FWD * k + FWD - 1, 8, FWD), :] = mean


_CHARGE = jax.ShapeDtypeStruct((WX * WY, NZ), f32)


def _middle(occupations, psi, pot, image_a, image_b, *faces):
    return pl.pallas_call(
        _middle_kernel,
        name="middle",
        in_specs=[_SM] + [_VM] * 8,
        out_specs=[_VM] * 4,
        out_shape=[*_IMAGES, _CHARGE, jax.ShapeDtypeStruct((8, NZ), f32)],
        scratch_shapes=[pltpu.VMEM((2, 64, NZ), f32)],
        input_output_aliases={3: 0, 4: 1},
        compiler_params=pltpu.CompilerParams(vmem_limit_bytes=16 * 1024 * 1024),
        cost_estimate=pl.CostEstimate(flops=100000000, bytes_accessed=8000000, transcendentals=0),
    )(occupations, psi, pot, image_a, image_b, *faces)


def _edge_messages(occupations, psi, pot, image_a, image_b, charge, totals, x_low, x_high):
    return pl.pallas_call(
        _edge_kernel,
        name="edge",
        in_specs=[_SM] + [_VM] * 9,
        out_specs=[_VM] * 4,
        out_shape=[*_IMAGES, _CHARGE, jax.ShapeDtypeStruct((DEVICES * FWD, 128), f32)],
        scratch_shapes=[pltpu.VMEM((6, 64, NZ), f32)],
        input_output_aliases={4: 0, 5: 1, 6: 2},
        compiler_params=pltpu.CompilerParams(vmem_limit_bytes=16 * 1024 * 1024),
        cost_estimate=pl.CostEstimate(flops=100000000, bytes_accessed=8000000, transcendentals=0),
    )(occupations, jnp.asarray(_tables()["beside"]), psi, pot, image_a, image_b, charge, totals, x_low, x_high)


def _swap_groups(blocks, group):
    out = []
    for i in range(4):
        value = None
        for j in range(4):
            shift = (32 * (j - i)) % 128
            moved = pltpu.roll(blocks[j], shift, 1) if shift else blocks[j]
            value = moved if value is None else jnp.where(group == j, moved, value)
        out.append(value)
    return out


def _plane_kernel(modes, recv, forward_x, stacked, back_x, ring_y, col, row, send, packed, block):
    dot = functools.partial(jnp.dot, preferred_element_type=f32)

    def parts(value, axis):
        high, low = _split(value)
        return jnp.concatenate([high, low, high], axis=axis)

    left = lambda table, value: dot(table[...], parts(value, 0))
    right = lambda value: dot(parts(value, 1), stacked[...])
    nt = lambda table, value: lax.dot_general(
        table[...], parts(value, 1), (((1,), (1,)), ((), ())), preferred_element_type=f32
    )
    kz = (lax.axis_index("orb") * POIS + lax.axis_index("pois")) * SLABS + lax.axis_index("slab")
    lam_z, sum_z = modes[0, kz], modes[1, kz]
    means = recv[pl.ds(FWD - 1, DEVICES, FWD), :]
    blocks = POIS * SLABS
    block_mean = sum(means[blocks * o : blocks * (o + 1)] for o in range(ORBS))
    mean = jnp.sum(block_mean, axis=0, keepdims=True) / blocks
    block_means = [block_mean[k : k + 1] for k in range(blocks)]
    for p in range(POIS):
        for s in range(SLABS):
            first = [((o * POIS + p) * SLABS + s) * FWD for o in range(ORBS)]
            shift = sum_z * (block_means[p * SLABS + s][0:1] - mean)
            packed[p, pl.ds(12 * s, 8), :] = sum(recv[pl.ds(r, 8), :] for r in first) + shift
            last = sum(recv[pl.ds(r + FWD - 8, 8), :] for r in first) + shift
            packed[p, pl.ds(12 * s + 8, 4), :] = last[3:7]
    group = lax.broadcasted_iota(jnp.int32, (WX, 128), 1) // 32
    plane = jnp.concatenate(_swap_groups([packed[p, 0:WX] for p in range(POIS)], group), axis=0)
    spectrum = right(left(forward_x, plane))
    divisor = col[:, 0:1] + row[0:1, :] + lam_z
    factor = 32.0 * math.pi / ((NX + 1) * (NY + 1) * (NZ + 1))
    scaled = spectrum * factor / divisor
    across = left(back_x, scaled)
    field = right(across[:NX])
    ring = right(across[NX + 256 :])
    cells = _swap_groups([field[WX * i : WX * (i + 1)] for i in range(4)], group)
    lane8 = lax.broadcasted_iota(jnp.int32, (8, 128), 1)
    group8 = lane8 // 32
    faces = [nt(ring_y, across[NX + 128 * h : NX + 128 * (h + 1)]) for h in range(2)]
    y_rows = []
    for s in range(SLABS):
        low, high = faces[s // 2][0:8], faces[s // 2][8:16]
        if s % 2 == 0:
            high = pltpu.roll(high, 64, 1)
        else:
            low = pltpu.roll(low, 64, 1)
        y_rows.append(jnp.where(lane8 < 64, low, high))
    for p in range(POIS):
        shift = lambda v, k: pltpu.roll(v, k % 128, 1) if k % 128 else v
        x_rows = jnp.where(
            group8 == 0,
            shift(ring[0:8], -32 * p),
            jnp.where(group8 == 1, shift(ring[8:16], 32 - 32 * p), 0.0),
        )
        for s in range(SLABS):
            base = (p * SLABS + s) * BACK
            block[pl.ds(base, 12), :] = cells[p][12 * s : 12 * s + 12]
            block[pl.ds(base + 12, 1), :] = x_rows[s : s + 1]
            block[pl.ds(base + 13, 1), :] = y_rows[s][p : p + 1]
    count = POIS * SLABS * BACK
    for o in range(ORBS):
        send[pl.ds(o * count, count), :] = block[0:count]


def _plane(recv):
    t = _tables()
    return pl.pallas_call(
        _plane_kernel,
        name="plane",
        in_specs=[_SM] + [_VM] * 7,
        out_specs=_VM,
        out_shape=jax.ShapeDtypeStruct((DEVICES * BACK, 128), f32),
        scratch_shapes=[
            pltpu.VMEM((POIS, WX + 8, 128), f32),
            pltpu.VMEM((POIS * SLABS * BACK + 16, 128), f32),
        ],
        compiler_params=pltpu.CompilerParams(vmem_limit_bytes=8 * 1024 * 1024),
        cost_estimate=pl.CostEstimate(flops=200000000, bytes_accessed=3000000, transcendentals=0),
    )(
        jnp.asarray(t["modes"]),
        recv,
        *(jnp.asarray(t[k]) for k in ("forward_x", "stacked", "back_x", "ring_y", "col", "row")),
    )


OUT_GROUP = 4


def _step_kernel(
    stacked, recv, tiled, image_a, image_b, psi, ext, old, x_low, x_high, y_low, y_high,
    new, hartree, image, pot, change, ring_y, tables, slices, out, out_sems,
):
    faces = (x_low, x_high, y_low, y_high)
    in_x, in_y = _inside()
    sub, lane = _iotas()
    tables[:, 0:128] = stacked[...]
    tables[:, 128:256] = tiled[lax.axis_index("orb")]

    def back(r, table):
        high, low = _split(recv[pl.ds(r, 128, BACK), :])
        stack = jnp.concatenate([high, low, high], axis=0)
        return lax.dot_general(stack, table[...], (((0,), (0,)), ((), ())), preferred_element_type=f32)

    def planes(g, carry):
        both = back(g, tables)
        field, mine = both[:, 0:128], both[:, 128:256]
        first = pl.multiple_of(4 * WY * g, 8)
        block = pl.ds(first, 4 * WY)
        moved = pl.ds(pl.multiple_of(first + WY, 8), 4 * WY)
        pot[moved] = 6.0 + (2.0 * ext[block] + (old[block] + field))
        change[moved] = field - old[block]
        for k in range(16):
            kept_lanes = jnp.where(lane // 16 == sub, mine[8 * k : 8 * k + 8], 0.0)
            slices[k % 4, pl.ds(4 * g + k // 4, 1), :] = jnp.sum(kept_lanes, axis=0, keepdims=True)
        return carry

    lax.fori_loop(0, WX // 4, planes, 0, unroll=2)
    x_field, y_field = back(12, stacked), back(13, stacked)
    for side in range(2):
        edge = pl.ds((WX + 1) * WY * side, WY)
        change[edge] = (x_field[32 * side : 32 * side + 32] - faces[side][COMPS, 1].astype(f32)) * in_x[side]
        ring_y[side] = (y_field[64 * side : 64 * side + WX] - faces[2 + side][COMPS, 1].astype(f32)) * in_y[side]
    for q in range(4):
        turned = jnp.transpose(slices[q])
        for y in range(8):
            hartree[8 * q + y] = turned[16 * y : 16 * y + 16, 0:WX]

    for half, start in enumerate((image_a, image_b)):

        def one(c, carry, half=half, start=start):
            part = SHARE[0] * half + c

            def planes_of(j, carry):
                for k in range(6):
                    x = 6 * j + k
                    value = psi[part, pl.ds(pl.multiple_of(WY * x, WY), WY)].astype(f32)
                    at = pl.ds(_base(x + 1), WY)
                    image[part, at] = start[c, at] + change[pl.ds(pl.multiple_of(WY * (x + 1), WY), WY)] * value
                return carry

            lax.fori_loop(0, WX // 6, planes_of, 0)
            for side in range(2):
                at = pl.ds(FIRST - PITCH + PITCH * (WX + 1) * side, WY)
                value = faces[side][part, 1 - side].astype(f32)
                image[part, at] = start[c, at] + change[pl.ds((WX + 1) * WY * side, WY)] * value
                at = pl.ds(FIRST + (WY if side else -1), WX, PITCH)
                image[part, at] = start[c, at] + ring_y[side] * faces[2 + side][part, 1 - side].astype(f32)
            return carry

        lax.fori_loop(0, SHARE[half], one, 0)

    def out_copy(j, c):
        planes = pl.ds(OUT_GROUP * j, OUT_GROUP)
        return pltpu.make_async_copy(out.at[c, planes], new.at[c, planes], out_sems.at[j, c])

    def group(j, carry):
        def pair(k, carry):
            for d in range(2):
                x = OUT_GROUP * j + 2 * k + d
                for h in range(2):
                    rows = pl.ds(pl.multiple_of(WY * x + 16 * h, 16), 16)
                    cells = [psi[c, rows].astype(f32) for c in range(COMPS)]
                    for i in (2 * h, 2 * h + 1):
                        r = slice(8 * (i % 2), 8 * (i % 2) + 8)
                        weight = pot[pl.ds(pl.multiple_of(WY * (x + 1) + 8 * i, 8), 8)]
                        for orbital in range(COMPS // 2):
                            parts = (2 * orbital, 2 * orbital + 1)
                            picked = [lambda row, c=c: image[c, pl.ds(row, 8)] for c in parts]
                            own = [cells[c][r] for c in parts]
                            real, imag = _stepped(own, picked, weight, orbital, _base(x + 1) + 8 * i, lane)
                            out[2 * orbital, x, 8 * i : 8 * i + 8] = real
                            out[2 * orbital + 1, x, 8 * i : 8 * i + 8] = imag
            return carry

        lax.fori_loop(0, OUT_GROUP // 2, pair, 0)
        for c in range(COMPS):
            out_copy(j, c).start()
        return carry

    lax.fori_loop(0, WX // OUT_GROUP, group, 0)
    for j in range(WX // OUT_GROUP):
        for c in range(COMPS):
            out_copy(j, c).wait()


def _step(recv, *arrays):
    t = _tables()
    return pl.pallas_call(
        _step_kernel,
        name="step",
        in_specs=[_VM] * (3 + len(arrays)),
        out_specs=[_HBM, _VM],
        out_shape=[
            jax.ShapeDtypeStruct((COMPS, WX, WY, NZ), f32),
            jax.ShapeDtypeStruct((WY, NZ // ORBS, WX), f32),
        ],
        scratch_shapes=[
            pltpu.VMEM((COMPS, PADDED, NZ), f32),
            pltpu.VMEM((PLANES * WY, NZ), f32),
            pltpu.VMEM((PLANES * WY, NZ), f32),
            pltpu.VMEM((2, WX, NZ), f32),
            pltpu.VMEM((3 * NZ, 256), bf16),
            pltpu.VMEM((4, 128, 128), f32),
            pltpu.VMEM((COMPS, WX, WY, NZ), f32),
            pltpu.SemaphoreType.DMA((WX // OUT_GROUP, COMPS)),
        ],
        compiler_params=pltpu.CompilerParams(vmem_limit_bytes=24 * 1024 * 1024),
        cost_estimate=pl.CostEstimate(flops=100000000, bytes_accessed=20000000, transcendentals=0),
    )(jnp.asarray(t["stacked"]), recv, jnp.asarray(t["tiled"]), *arrays)


def _shifted(value, axis, count, step):
    return lax.ppermute(value, axis, [(i, (i + step) % count) for i in range(count)])


def _swap(messages, rows):
    moved = lax.all_to_all(messages.reshape(DEVICES, 1, rows * 128), TRANSPOSE_AXES, 0, 0)
    return moved.reshape(DEVICES * rows, 128)


def body(orbitals, occupations, ext_pot, hartree_old):
    psi = orbitals.reshape(COMPS, WX * WY, NZ)
    ext, old = ext_pot.reshape(WX * WY, NZ), hartree_old.reshape(WX * WY, NZ)
    x_left, x_right, y_left, y_right, pot = _faces(orbitals.reshape(COMPS, WX, WY, NZ), ext, old)
    y_low = _shifted(y_right, "pois", POIS, 1)
    y_high = _shifted(y_left, "pois", POIS, -1)
    image_a, _ = _inner(0, psi, pot)
    image_b, done = _inner(1, psi, pot)
    x_left, x_right = _corners(x_left, x_right, y_low, y_high, done)
    x_low = _shifted(x_right, "slab", SLABS, 1)
    x_high = _shifted(x_left, "slab", SLABS, -1)
    image_a, image_b, charge, totals = _middle(occupations, psi, pot, image_a, image_b, y_low, y_high, y_left, y_right)
    image_a, image_b, _, message = _edge_messages(
        occupations, psi, pot, image_a, image_b, charge, totals, x_low, x_high
    )
    faces = (x_low, x_high, y_low, y_high)
    back = _swap(_plane(_swap(message, FWD)), BACK)
    new, hartree = _step(back, image_a, image_b, psi, ext, old, *faces)
    return new.reshape(orbitals.shape), jnp.transpose(hartree, (2, 0, 1))


def solution(mesh):
    placed = (P("orb", None, "slab", "pois", None), P("orb"), P("slab", "pois", None), P("slab", "pois", None))
    return jax.shard_map(
        body,
        mesh=mesh,
        in_specs=placed,
        out_specs=(P("orb", None, "slab", "pois", None), P("slab", "pois", "orb")),
        check_vma=False,
    )
```
